128 devices in a mesh: depth: 2 (over core), lat: 64 (over z, y, x).
Axes of the slice: x: 4, y: 4, z: 4, core: 2. Of those that a mesh axis runs over, the one named last changes fastest.
Arguments:
- object_slices: float32 [2, 2, 16384, 2048], P('depth', None, 'lat'), may hold values from -1.1 to 1.1, as said below
- probe: float32 [2, 256, 256], replicated, may hold values from -6 to 6
- measured: float32 [256, 256, 256], P('lat'), may hold values from 0.2 to 3
- positions: int32 [256, 2], P('lat'), may hold values from 0 to 1792, as said below
- counts: int32 [64], P('lat'), may hold values from 1 to 4, 160 in all
Outputs:
- object_gradient: float32 [2, 2, 16384, 2048], P('depth', None, 'lat')
The draws below stay inside these ranges and needn't reach their ends.
Inputs may be any that keep to these rules, and one draw needn't show every extreme that they name: `object_slices`: each transmission value has modulus at most 1.1. `positions`: column 0 is a row offset within the slot's own tile, from 0 to 255; column 1 is a column offset from 0 to 1792; both ends are reached. `counts`: every tile uses at least one slot; some tile uses all 4.
All inputs are finite; a program needn't handle non-finite values. No bound on the sum of `counts` on one device may be relied on, other than what follows from the above.
Results may differ from the reference program's by a relative error of at most 0.0003.
Values sent between devices are 32-bit elements; how exact they have to be, the bound alone decides.
A program may use at most 128 MiB of HBM per device.

```python
import math
import jax
import jax.numpy as jnp
import numpy as np
from jax import lax

PROBE = 256
TILE_H = 256
OBJ_W = 2048
POS_CAP = 4
SLICES = 2
ROWS = 16384
POSITIONS = 256
LIVE = 160
N_LAT = 64


def draw_object_slices(key, part):
    first, second = jax.random.split(jax.random.fold_in(key, 11))
    shape = (SLICES, ROWS, OBJ_W)
    amplitude = jax.random.uniform(first, shape, jnp.float32, 0.6, 1.1)
    phase = jax.random.uniform(second, shape, jnp.float32, -1.0, 1.0)
    return jnp.stack([amplitude * jnp.cos(phase), amplitude * jnp.sin(phase)], axis=1).astype(jnp.float32)


def draw_positions(key, part):
    first, second = jax.random.split(jax.random.fold_in(key, 23))
    row_offsets = jax.random.randint(first, (POSITIONS,), 0, TILE_H, dtype=jnp.int32)
    column_offsets = jax.random.randint(second, (POSITIONS,), 0, OBJ_W - PROBE + 1, dtype=jnp.int32)
    row_offsets = row_offsets.at[1].set(TILE_H - 1).at[2].set(0)
    column_offsets = column_offsets.at[0].set(OBJ_W - PROBE).at[3].set(0)
    return jnp.stack([row_offsets, column_offsets], axis=1).astype(jnp.int32)


def level_of(key, extent, shards, least, largest):
    loudness = 1.0
    for axis_at, shards_of in shards:
        draws = jax.random.uniform(jax.random.fold_in(jax.random.fold_in(key, 6), axis_at), (shards_of,), jnp.float32, least / len(shards), largest / len(shards))
        loudness = loudness * jnp.repeat(jnp.exp(draws), extent[axis_at] // shards_of).reshape((-1,) + (1,) * (len(extent) - 1 - axis_at))
    return loudness


def length_profile(number_of, total, reach, skew):
    loads = [(1 << 20) // math.isqrt(rank ** skew) + 1 for rank in range(2, number_of + 1)]
    spare, holding = total - reach - (number_of - 1), [1] * (number_of - 1)
    while spare > 0:
        free = [i for i in range(number_of - 1) if holding[i] < reach]
        mass, left = sum([loads[i] for i in free]), spare
        for i in free:
            extra = min(reach - holding[i], max(1, left * loads[i] // mass), spare)
            holding[i] = holding[i] + extra
            spare = spare - extra
    return np.array([reach] + holding)


def uneven_parts(stream_key, number_of, total, reach, slope):
    if number_of == 2:
        one = jax.random.randint(stream_key, (), max(1, total - reach), min(reach, total - 1) + 1)
        return jnp.stack([one, total - one])
    lengths = jnp.asarray(length_profile(number_of, total, reach, slope), jnp.int32)
    couples = (number_of - 1) // 2
    source_of, sink = lengths[1:1 + 2 * couples:2], lengths[2:2 + 2 * couples:2]
    room = jnp.minimum(source_of - 1, reach - sink)
    passed = jax.random.randint(jax.random.fold_in(stream_key, 1), (couples,), 0, 1 << 20) % (room + 1)
    lengths = lengths.at[1:1 + 2 * couples:2].set(source_of - passed).at[2:2 + 2 * couples:2].set(sink + passed)
    return lengths[jax.random.permutation(jax.random.fold_in(stream_key, 2), number_of)]


def gaussian(key, dims, scale, most, kind=jnp.bfloat16):
    result = jax.random.normal(key, dims, jnp.float32) * scale
    return jnp.minimum(jnp.maximum(result, -most), most).astype(kind)


def setup_inputs(seed: int = 0) -> dict:
    streams_of = jax.random.split(jax.random.key(seed), 6)
    object_slices = draw_object_slices(jax.random.fold_in(streams_of[5], 71), 0)
    probe = gaussian(streams_of[1], (2, PROBE, PROBE), 1.0, 6.0, jnp.float32)
    measured = jnp.clip(0.2 + 2.8 * jax.random.uniform(streams_of[2], (POSITIONS, PROBE, PROBE), jnp.float32) ** level_of(streams_of[2], (POSITIONS, PROBE, PROBE), ((0, 64),), -0.2, 0.2), 0.2, 3.0)
    positions = draw_positions(jax.random.fold_in(streams_of[5], 71), 0)
    counts = uneven_parts(streams_of[4], N_LAT, LIVE, POS_CAP, 2).astype(jnp.int32)
    return dict(object_slices=object_slices, probe=probe, measured=measured, positions=positions, counts=counts)


fresnel_strength = 8.0

def dft_tables(length):
    index = jnp.arange(length, dtype=jnp.int32)
    product = index[:, None] * index[None, :] % length
    angle = 2.0 * math.pi / length * product.astype(jnp.float32)
    scale = 1.0 / math.sqrt(length)
    return (jnp.cos(angle) * scale, jnp.sin(angle) * scale)

def kernel_tables(length):
    index = jnp.arange(length, dtype=jnp.int32)
    centred = (index - length * (index >= length // 2).astype(jnp.int32)).astype(jnp.float32) / length
    phase = math.pi * fresnel_strength * (centred[:, None] ** 2 + centred[None, :] ** 2)
    return (jnp.cos(phase), jnp.sin(phase))

def left_product(matrix, values):
    return jnp.einsum('jk,...kl->...jl', matrix, values, precision=lax.Precision.HIGHEST)

def right_product(values, matrix):
    return jnp.einsum('...jk,kl->...jl', values, matrix, precision=lax.Precision.HIGHEST)

def transform(values, tables, sign):
    cosine, sine = tables
    sine = sine * sign
    left_real = left_product(cosine, values[0]) - left_product(sine, values[1])
    left_imaginary = left_product(cosine, values[1]) + left_product(sine, values[0])
    out_real = right_product(left_real, cosine) - right_product(left_imaginary, sine)
    out_imaginary = right_product(left_imaginary, cosine) + right_product(left_real, sine)
    return jnp.stack([out_real, out_imaginary])

def complex_product(first, second):
    return jnp.stack([first[0] * second[0] - first[1] * second[1], first[0] * second[1] + first[1] * second[0]])

def conj_product(first, second):
    return jnp.stack([first[0] * second[0] + first[1] * second[1], first[0] * second[1] - first[1] * second[0]])

def propagate(values, tables, kernel, sign):
    spectrum = transform(values, tables, -1.0)
    turned = complex_product(spectrum, jnp.stack([kernel[0], sign * kernel[1]]))
    return transform(turned, tables, 1.0)

def reference(object_slices, probe, measured, positions, counts):
    tables = dft_tables(PROBE)
    kernel = kernel_tables(PROBE)
    offsets = jnp.arange(PROBE, dtype=jnp.int32)

    def one_position(index):
        device = index // POS_CAP
        slot_number = index % POS_CAP
        first_row = device * TILE_H + positions[index, 0]
        row_index = ((first_row + offsets) % ROWS).astype(jnp.int32)
        column_index = (positions[index, 1] + offsets).astype(jnp.int32)
        window = object_slices[:, :, row_index[:, None], column_index[None, :]]
        live = (slot_number < counts[device]).astype(jnp.float32)
        wave = probe
        inputs = []
        for layer in range(SLICES):
            inputs.append(wave)
            wave = propagate(complex_product(wave, window[layer]), tables, kernel, 1.0)
        far = transform(wave, tables, -1.0)
        factor = live * (1.0 - measured[index] / jnp.sqrt(far[0] * far[0] + far[1] * far[1] + 1.0))
        back = transform(far * factor, tables, 1.0)
        pieces = [None] * SLICES
        for layer in reversed(range(SLICES)):
            adjoint = propagate(back, tables, kernel, -1.0)
            pieces[layer] = conj_product(inputs[layer], adjoint)
            back = conj_product(window[layer], adjoint)
        return (jnp.stack(pieces), row_index, column_index)
    gradients, row_lists, column_lists = lax.map(one_position, jnp.arange(POSITIONS, dtype=jnp.int32))

    def accumulate(total, item):
        piece, row_index, column_index = item
        return (total.at[:, :, row_index[:, None], column_index[None, :]].add(piece), None)
    total, unused = lax.scan(accumulate, jnp.zeros(object_slices.shape, jnp.float32), (gradients, row_lists, column_lists))
    return total
```

```python
import functools

import jax
import jax.numpy as jnp
import ml_dtypes
import numpy as np
from jax import lax
from jax.experimental import pallas as pl
from jax.experimental.pallas import tpu as pltpu
from jax.sharding import PartitionSpec as P

N = 256
HALF = 128
STRENGTH = 8.0
MAX_JOBS = 3
BUDGET = 48
ROWS = 8 * BUDGET
PAD = 256
SPAN = 20


def split_bf16(a):
    hi = a.astype(np.float32).astype(ml_dtypes.bfloat16)
    lo = (a - hi.astype(np.float64)).astype(np.float32).astype(ml_dtypes.bfloat16)
    return hi, lo


def left_table(a):
    hi, lo = split_bf16(a)
    return np.concatenate([hi, hi, lo], axis=1)


def right_table(a):
    hi, lo = split_bf16(a)
    return np.concatenate([hi, hi, lo], axis=0)


def tables():
    index = np.arange(N)
    angle = 2.0 * np.pi * ((index[:, None] * index[None, :]) % N) / N
    dft = np.exp(-1j * angle) / 16.0
    centred = (index - N * (index >= HALF)) / N
    turn = np.exp(1j * np.pi * STRENGTH * centred**2)
    prop = np.conj(dft) @ (turn[:, None] * dft)
    c0, c1 = prop[:HALF, :HALF], prop[:HALF, HALF:]
    plus, minus = (c0 + c1) / 2, (c0 - c1) / 2

    def real_left(m):
        return np.block([[m.real, -m.imag], [m.imag, m.real]])

    lp, lm = real_left(plus), real_left(minus)
    lefts = np.stack([left_table(lp), left_table(lm), left_table(lp.T), left_table(lm.T)])
    rights = np.stack([right_table(lp.T), right_table(lm.T), right_table(lp), right_table(lm)])
    cos, sin = np.cos(angle) / 16.0, np.sin(angle) / 16.0
    dft_left = np.concatenate([left_table(cos), left_table(sin)], axis=0)
    dft_right = np.stack([right_table(cos), right_table(sin)])
    return lefts, rights, dft_left, dft_right


def make_plan(rows_of, cols_of, live, plan, base):
    up = [lax.div(rows_of[i] + 7, 8) for i in range(4)]
    down = [40 - lax.div(rows_of[i], 8) for i in range(4)]
    best = jnp.int32(1 << 20)
    pick = jnp.int32(0)
    for mask in range(16):
        right = [(mask >> i) & 1 for i in range(4)]
        top = max([i + 1 for i in range(4) if right[i]], default=0)
        n_right = sum(right)
        lefts = [jnp.where(live > i, up[i], 0) for i in range(4) if not right[i]]
        cost_left = sum(lefts, jnp.int32(0))
        cost_right = sum([down[i] for i in range(4) if right[i]], jnp.int32(0))
        n_left = live - n_right
        widest = jnp.maximum(cost_left, cost_right)
        most = jnp.maximum(n_left, n_right)
        bad = (live < top) | (widest > BUDGET) | (most > MAX_JOBS)
        key = most * 64 + widest + jnp.where(bad, jnp.int32(1 << 16), 0)
        pick = jnp.where(key < best, mask, pick)
        best = jnp.minimum(key, best)
    for side in range(2):
        at = base + side * SPAN
        count = jnp.int32(0)
        total = jnp.int32(0)
        for j in range(MAX_JOBS):
            for f in range(5):
                plan[at + 2 + 5 * j + f] = jnp.int32(0)
        for i in range(4):
            mine = (live > i) & ((lax.shift_right_logical(pick, i) & 1) == side)
            block = jnp.minimum(lax.div(cols_of[i], N), 6)
            spot = at + 2 + 5 * count

            @pl.when(mine)
            def _(spot=spot, i=i, block=block, total=total):
                plan[spot] = rows_of[i]
                plan[spot + 1] = block
                plan[spot + 2] = cols_of[i] - block * N
                plan[spot + 3] = total
                plan[spot + 4] = jnp.int32(i)

            size = up[i] if side == 0 else down[i] - 8
            total = total + jnp.where(mine, size, 0)
            count = count + jnp.where(mine, 1, 0)
        plan[at] = count
        plan[at + 1] = total


OWN_LEFT, OWN_RIGHT, PREV_LEFT, PREV_RIGHT = 0, SPAN, 2 * SPAN, 3 * SPAN


def lanes():
    return lax.broadcasted_iota(jnp.int32, (8, N), 1)


def pack_kernel(pos, cnt, prev_pos, prev_cnt, tile, measured, plan, a_ref, b_ref):
    depth = lax.axis_index("depth")
    make_plan([pos[i, 0] for i in range(4)], [pos[i, 1] for i in range(4)], cnt[0], plan, 0)
    make_plan(
        [prev_pos[i, 0] for i in range(4)],
        [prev_pos[i, 1] for i in range(4)],
        prev_cnt[0],
        plan,
        2 * SPAN,
    )

    def copy_rows(out, at, j, first, count):
        block = plan[at + 2 + 5 * j + 1]
        shift = plan[at + 2 + 5 * j + 2]
        start = plan[at + 2 + 5 * j + 3]
        low = pl.multiple_of(block * N, N)
        high = pl.multiple_of(block * N + N, N)
        keep = lanes() >= shift

        def step(g, carry):
            src = pl.multiple_of((first + g) * 8, 8)
            dst = pl.multiple_of((start + g) * 8, 8)
            for c in range(2):
                out[c, pl.ds(dst, 8), :] = jnp.where(
                    keep, tile[c, pl.ds(src, 8), pl.ds(low, N)], tile[c, pl.ds(src, 8), pl.ds(high, N)]
                )
            return carry

        lax.fori_loop(0, count, step, 0)

    def right_job(j, carry):
        first = lax.div(plan[OWN_RIGHT + 2 + 5 * j], 8)
        copy_rows(a_ref, OWN_RIGHT, j, first, 32 - first)
        slot = plan[OWN_RIGHT + 2 + 5 * j + 4]
        dst = pl.multiple_of((plan[OWN_RIGHT + 1] + 8 * j) * 8, 8)
        for c in range(2):
            src = pl.multiple_of(depth * HALF + 64 * c, 64)
            a_ref[c, pl.ds(dst, 64), :] = measured[slot, pl.ds(src, 64), :]
        return carry

    lax.fori_loop(0, plan[OWN_RIGHT], right_job, 0)

    def left_job(j, carry):
        count = lax.div(plan[PREV_LEFT + 2 + 5 * j] + 7, 8)
        copy_rows(b_ref, PREV_LEFT, j, 0, count)
        return carry

    lax.fori_loop(0, plan[PREV_LEFT], left_job, 0)


def halves(x):
    hi = x.astype(jnp.bfloat16)
    lo = (x - hi.astype(jnp.float32)).astype(jnp.bfloat16)
    return hi, lo


def dot(a, b):
    return jnp.dot(a, b, preferred_element_type=jnp.float32)


def wide(x):
    hi, lo = halves(x)
    return jnp.concatenate([hi, lo, hi], axis=1)


def tall(x):
    hi, lo = halves(x)
    return jnp.concatenate([hi, lo, hi], axis=0)


def propagate(re, im, lefts, rights, at):
    plus = jnp.concatenate([re[:, :HALF] + re[:, HALF:], im[:, :HALF] + im[:, HALF:]], axis=1)
    minus = jnp.concatenate([re[:, :HALF] - re[:, HALF:], im[:, :HALF] - im[:, HALF:]], axis=1)
    plus = dot(wide(plus), rights[at])
    minus = dot(wide(minus), rights[at + 1])
    first, second = plus + minus, plus - minus
    re = jnp.concatenate([first[:, :HALF], second[:, :HALF]], axis=1)
    im = jnp.concatenate([first[:, HALF:], second[:, HALF:]], axis=1)
    plus = jnp.concatenate([re[:HALF] + re[HALF:], im[:HALF] + im[HALF:]], axis=0)
    minus = jnp.concatenate([re[:HALF] - re[HALF:], im[:HALF] - im[HALF:]], axis=0)
    plus = dot(lefts[at], tall(plus))
    minus = dot(lefts[at + 1], tall(minus))
    first, second = plus + minus, plus - minus
    return (
        jnp.concatenate([first[:HALF], second[:HALF]], axis=0),
        jnp.concatenate([first[HALF:], second[HALF:]], axis=0),
    )


def transform(re, im, dft_left, dft_right, sign):
    both = wide(jnp.concatenate([re, im], axis=0))
    c = dot(both, dft_right[0])
    s = dot(both, dft_right[1]) * sign
    re, im = c[:N] - s[N:], c[N:] + s[:N]
    both = tall(jnp.concatenate([re, im], axis=1))
    c = dot(dft_left[:N], both)
    s = dot(dft_left[N:], both) * sign
    return c[:, :N] - s[:, N:], c[:, N:] + s[:, :N]


def compute_kernel(
    plan, tile, other, x_other, x_same, measured, probe, lefts, rights, dft_left, dft_right,
    g_other, g_same, mine, theirs,
    strips, received, amplitude, grads, sems,
):
    depth = lax.axis_index("depth")
    at = jnp.where(depth == 0, OWN_LEFT, PREV_RIGHT)
    copies = [
        pltpu.make_async_copy(x_same, received.at[depth, :, pl.ds(PAD, ROWS), :], sems.at[0]),
        pltpu.make_async_copy(x_other, received.at[1 - depth, :, pl.ds(PAD, ROWS), :], sems.at[1]),
    ]
    for copy in copies:
        copy.start()
    for copy in copies:
        copy.wait()
    row = lax.broadcasted_iota(jnp.int32, (N, N), 0)
    lane = lax.broadcasted_iota(jnp.int32, (N, N), 1)

    def job(j, carry):
        r = plan[at + 2 + 5 * j]
        block = plan[at + 2 + 5 * j + 1]
        shift = plan[at + 2 + 5 * j + 2]
        start = plan[at + 2 + 5 * j + 3]
        slot = plan[at + 2 + 5 * j + 4]
        column = pl.multiple_of(block * N, N)
        fetch = [
            pltpu.make_async_copy(
                tile.at[:, :, pl.ds(column, 2 * N)], strips.at[depth], sems.at[2]
            ),
            pltpu.make_async_copy(
                other.at[:, :, pl.ds(column, 2 * N)], strips.at[1 - depth], sems.at[3]
            ),
            pltpu.make_async_copy(measured.at[slot], amplitude, sems.at[4]),
        ]
        for copy in fetch:
            copy.start()
        for copy in fetch:
            copy.wait()

        @pl.when(depth == 1)
        def _():
            src = pl.multiple_of(PAD + (plan[PREV_RIGHT + 1] + 8 * j) * 8, 8)
            for s in range(2):
                for c in range(2):
                    amplitude[pl.ds(128 * s + 64 * c, 64), :] = received[s, c, pl.ds(src, 64), :]

        low = jnp.where(depth == 0, r, 0)
        high = jnp.where(depth == 0, N, r)
        here = (row >= low) & (row < high)
        keep = lane >= shift
        base = jnp.where(depth == 0, 0, lax.div(r, 8))
        src = pl.multiple_of(PAD + (start - base) * 8, 8)

        def window(s):
            return [
                jnp.where(
                    here,
                    jnp.where(keep, strips[s, c, :, :N], strips[s, c, :, N:]),
                    received[s, c, pl.ds(src, N), :],
                )
                for c in range(2)
            ]

        def rolled(c):
            turned = pltpu.roll(probe[c], r, 0)
            return pltpu.roll(turned, jnp.where(shift == N, 0, shift), 1)

        p_re, p_im = rolled(0), rolled(1)
        o_re, o_im = window(0)
        w_re, w_im = propagate(
            p_re * o_re - p_im * o_im, p_re * o_im + p_im * o_re, lefts, rights, 0
        )
        o_re, o_im = window(1)
        f_re, f_im = transform(
            w_re * o_re - w_im * o_im, w_re * o_im + w_im * o_re, dft_left, dft_right, -1.0
        )
        factor = 1.0 - amplitude[...] / jnp.sqrt(f_re * f_re + f_im * f_im + 1.0)
        a_re, a_im = transform(f_re * factor, f_im * factor, dft_left, dft_right, 1.0)
        grads[1, 0] = w_re * a_re + w_im * a_im
        grads[1, 1] = w_re * a_im - w_im * a_re
        a_re, a_im = propagate(
            o_re * a_re + o_im * a_im, o_re * a_im - o_im * a_re, lefts, rights, 2
        )
        grads[0, 0] = p_re * a_re + p_im * a_im
        grads[0, 1] = p_re * a_im - p_im * a_re
        mine[j] = grads[depth]
        theirs[j] = grads[1 - depth]
        count = jnp.where(depth == 0, lax.div(r + 7, 8), 32 - lax.div(r, 8))

        def step(g, carry):
            src = pl.multiple_of((base + g) * 8, 8)
            dst = pl.multiple_of((start + g) * 8, 8)
            for c in range(2):
                g_same[c, pl.ds(dst, 8), :] = grads[depth, c, pl.ds(src, 8), :]
                g_other[c, pl.ds(dst, 8), :] = grads[1 - depth, c, pl.ds(src, 8), :]
            return carry

        lax.fori_loop(0, count, step, 0)
        return carry

    lax.fori_loop(0, plan[at], job, 0)


def gather_kernel(plan, g_other, g_same, mine, theirs, out):
    depth = lax.axis_index("depth")

    def clear(i, carry):
        at = pl.multiple_of(i * 8, 8)
        for c in range(2):
            out[c, pl.ds(at, 8), :] = jnp.zeros((8, out.shape[2]), jnp.float32)
        return carry

    lax.fori_loop(0, N // 8, clear, 0)
    row = lax.broadcasted_iota(jnp.int32, (8, N), 0)

    def add(source, at, j, lower, packed):
        r = plan[at + 2 + 5 * j]
        block = plan[at + 2 + 5 * j + 1]
        shift = plan[at + 2 + 5 * j + 2]
        start = plan[at + 2 + 5 * j + 3]
        first = 0 if lower else lax.div(r, 8)
        last = lax.div(r + 7, 8) if lower else 32
        keep = lanes() >= shift
        low = pl.multiple_of(block * N, N)
        high = pl.multiple_of(block * N + N, N)

        def step(g, carry):
            dst = pl.multiple_of(g * 8, 8)
            inside = (row + dst < r) if lower else (row + dst >= r)
            for c in range(2):
                if packed:
                    src = pl.multiple_of((start + g - first) * 8, 8)
                    value = source[c, pl.ds(src, 8), :]
                else:
                    value = source[j, c, pl.ds(dst, 8), :]
                out[c, pl.ds(dst, 8), pl.ds(low, N)] += jnp.where(inside & keep, value, 0.0)
                out[c, pl.ds(dst, 8), pl.ds(high, N)] += jnp.where(
                    inside & jnp.logical_not(keep), value, 0.0
                )
            return carry

        lax.fori_loop(first, last, step, 0)

    def run(source, at, lower, packed):
        def step(j, carry):
            add(source, at, j, lower, packed)
            return carry

        lax.fori_loop(0, plan[at], step, 0)

    @pl.when(depth == 0)
    def _():
        run(mine, OWN_LEFT, False, False)
        run(theirs, PREV_RIGHT, True, False)
        run(g_other, OWN_RIGHT, False, True)
        run(g_same, PREV_LEFT, True, True)

    @pl.when(depth == 1)
    def _():
        run(theirs, OWN_LEFT, False, False)
        run(mine, PREV_RIGHT, True, False)
        run(g_same, OWN_RIGHT, False, True)
        run(g_other, PREV_LEFT, True, True)


SMEM = pl.BlockSpec(memory_space=pltpu.SMEM)
VMEM = pl.BlockSpec(memory_space=pltpu.VMEM)
ANY = pl.BlockSpec(memory_space=pl.ANY)


def shape(*dims):
    return jax.ShapeDtypeStruct(dims, jnp.float32)


def shards(n_lat, object_slices, probe, measured, positions, counts):
    columns = object_slices.shape[3]
    tile = object_slices.reshape(object_slices.shape[1:])
    ahead = [(i, (i + 1) % n_lat) for i in range(n_lat)]
    prev_positions = lax.ppermute(positions, "lat", ahead)
    prev_counts = lax.ppermute(counts, "lat", ahead)

    def device(core, lat):
        return core * n_lat + lat % n_lat

    to_other = [(device(0, t), device(1, t + 1)) for t in range(n_lat)]
    to_other += [(device(1, t), device(0, t - 1)) for t in range(n_lat)]
    to_same = [(device(0, t), device(0, t - 1)) for t in range(n_lat)]
    to_same += [(device(1, t), device(1, t + 1)) for t in range(n_lat)]
    back_other = [(device(0, t), device(1, t + 1)) for t in range(n_lat)]
    back_other += [(device(1, t), device(0, t - 1)) for t in range(n_lat)]
    back_same = [(device(0, t), device(0, t + 1)) for t in range(n_lat)]
    back_same += [(device(1, t), device(1, t - 1)) for t in range(n_lat)]
    axes = ("depth", "lat")

    other = lax.ppermute(tile, "depth", [(0, 1), (1, 0)])
    plan, ahead_rows, behind_rows = pl.pallas_call(
        pack_kernel,
        name="pack",
        out_shape=(
            jax.ShapeDtypeStruct((4 * SPAN,), jnp.int32),
            shape(2, ROWS, N),
            shape(2, ROWS, N),
        ),
        in_specs=[SMEM, SMEM, SMEM, SMEM, VMEM, VMEM],
        out_specs=(SMEM, VMEM, VMEM),
        compiler_params=pltpu.CompilerParams(vmem_limit_bytes=40 << 20),
    )(positions, counts, prev_positions, prev_counts, tile, measured)

    core = lax.axis_index("depth")
    send_other = jnp.where(core == 0, ahead_rows, behind_rows)
    send_same = jnp.where(core == 0, behind_rows, ahead_rows)
    x_other = lax.ppermute(send_other, axes, to_other)
    x_same = lax.ppermute(send_same, axes, to_same)

    lefts, rights, dft_left, dft_right = (jnp.asarray(t) for t in tables())
    g_other, g_same, mine, theirs = pl.pallas_call(
        compute_kernel,
        name="compute",
        out_shape=(
            shape(2, ROWS, N),
            shape(2, ROWS, N),
            shape(MAX_JOBS, 2, N, N),
            shape(MAX_JOBS, 2, N, N),
        ),
        in_specs=[SMEM, ANY, ANY, ANY, ANY, ANY, VMEM, VMEM, VMEM, VMEM, VMEM],
        out_specs=(VMEM, VMEM, VMEM, VMEM),
        scratch_shapes=[
            pltpu.VMEM((2, 2, N, 2 * N), jnp.float32),
            pltpu.VMEM((2, 2, ROWS + 2 * PAD, N), jnp.float32),
            pltpu.VMEM((N, N), jnp.float32),
            pltpu.VMEM((2, 2, N, N), jnp.float32),
            pltpu.SemaphoreType.DMA((5,)),
        ],
        compiler_params=pltpu.CompilerParams(vmem_limit_bytes=50 << 20),
    )(plan, tile, other, x_other, x_same, measured, probe, lefts, rights, dft_left, dft_right)

    r_other = lax.ppermute(g_other, axes, back_other)
    r_same = lax.ppermute(g_same, axes, back_same)
    theirs = lax.ppermute(theirs, "depth", [(0, 1), (1, 0)])
    out = pl.pallas_call(
        gather_kernel,
        name="gather",
        out_shape=shape(2, N, columns),
        in_specs=[SMEM, VMEM, VMEM, VMEM, VMEM],
        out_specs=VMEM,
        compiler_params=pltpu.CompilerParams(vmem_limit_bytes=40 << 20),
    )(plan, r_other, r_same, mine, theirs)
    return out.reshape(object_slices.shape)


def solution(mesh):
    return jax.shard_map(
        functools.partial(shards, mesh.shape["lat"]),
        mesh=mesh,
        in_specs=(
            P("depth", None, "lat", None),
            P(),
            P("lat", None, None),
            P("lat", None),
            P("lat"),
        ),
        out_specs=P("depth", None, "lat", None),
        check_vma=False,
    )
```

```python
import functools

import jax
import jax.numpy as jnp
import ml_dtypes
import numpy as np
from jax import lax
from jax.experimental import pallas as pl
from jax.experimental.pallas import tpu as pltpu
from jax.sharding import PartitionSpec as P

N = 256
HALF = 128
STRENGTH = 8.0
MAX_JOBS = 3
BUDGET = 48
ROWS = 8 * BUDGET
PAD = 256
SPAN = 20


def split_bf16(a):
    hi = a.astype(np.float32).astype(ml_dtypes.bfloat16)
    lo = (a - hi.astype(np.float64)).astype(np.float32).astype(ml_dtypes.bfloat16)
    return hi, lo


def tables():
    index = np.arange(N)
    angle = 2.0 * np.pi * ((index[:, None] * index[None, :]) % N) / N
    dft = np.exp(-1j * angle) / 16.0
    centred = (index - N * (index >= HALF)) / N
    turn = np.exp(1j * np.pi * STRENGTH * centred**2)
    prop = np.conj(dft) @ (turn[:, None] * dft)
    c0, c1 = prop[:HALF, :HALF], prop[:HALF, HALF:]

    def real_form(m):
        return np.block([[m.real, -m.imag], [m.imag, m.real]])

    forms = [real_form(m) for m in ((c0 + c1) / 2, (c0 - c1) / 2, dft[0::2, :HALF], dft[1::2, :HALF])]
    forms = forms + [m.T for m in forms]
    return np.stack([np.stack(split_bf16(m)) for m in forms])


OWN_LEFT, OWN_RIGHT, PREV_LEFT, PREV_RIGHT = 0, SPAN, 2 * SPAN, 3 * SPAN


def choose_sides(rows_of, cols_of, live):
    up = [lax.div(rows_of[i] + 7, 8) for i in range(4)]
    down = [32 - lax.div(rows_of[i], 8) for i in range(4)]
    best = jnp.int32(1 << 20)
    pick = jnp.int32(0)
    for mask in range(16):
        right = [(mask >> i) & 1 for i in range(4)]
        n_right = sum(right)
        if n_right > MAX_JOBS:
            continue
        top = max([i + 1 for i in range(4) if right[i]], default=0)
        lefts = [jnp.where(live > i, up[i], 0) for i in range(4) if not right[i]]
        cost_left = sum(lefts, jnp.int32(0))
        cost_right = sum([down[i] + 8 for i in range(4) if right[i]], jnp.int32(0))
        widest = jnp.maximum(cost_left, cost_right)
        most = jnp.maximum(live - n_right, n_right)
        bad = (live < top) | (widest > BUDGET) | (most > MAX_JOBS)
        key = most * 64 + widest + jnp.where(bad, jnp.int32(1 << 16), 0)
        pick = jnp.where(key < best, mask, pick)
        best = jnp.minimum(key, best)
    blocks = [jnp.minimum(lax.div(cols_of[i], N), 6) for i in range(4)]
    sides = []
    for side in range(2):
        mine = [(live > i) & ((lax.shift_right_logical(pick, i) & 1) == side) for i in range(4)]
        size = up if side == 0 else down
        count, total = jnp.int32(0), jnp.int32(0)
        words = [[jnp.int32(0)] * 5 for _ in range(MAX_JOBS)]
        for i in range(4):
            fields = [rows_of[i], blocks[i], cols_of[i] - blocks[i] * N, total, jnp.int32(i)]
            for j in range(MAX_JOBS):
                here = mine[i] & (count == j)
                words[j] = [jnp.where(here, f, w) for f, w in zip(fields, words[j])]
            count = count + jnp.where(mine[i], 1, 0)
            total = total + jnp.where(mine[i], size[i], 0)
        sides.append([count, total] + [w for job in words for w in job])
    return sides


def lanes():
    return lax.broadcasted_iota(jnp.int32, (8, N), 1)


def announce_kernel(n_lat, pos, cnt, prev_pos, prev_cnt, send, recv):
    depth = lax.axis_index("depth")
    lat = lax.axis_index("lat")
    after = lax.rem(lat + 1, n_lat)
    before = lax.rem(lat + n_lat - 1, n_lat)
    barrier = pltpu.get_barrier_semaphore()
    for other in (after, before):
        pl.semaphore_signal(
            barrier, inc=1, device_id=(depth, other), device_id_type=pl.DeviceIdType.MESH
        )
    pl.semaphore_wait(barrier, 2)
    copies = [
        remote(pos, prev_pos, send.at[0], recv.at[0], depth, after),
        remote(cnt, prev_cnt, send.at[1], recv.at[1], depth, after),
    ]
    for copy in copies:
        copy.start()
    for copy in copies:
        copy.wait()


def pack_kernel(
    pos, cnt, prev_pos, prev_cnt, tile_hbm, measured_hbm, plan, ahead, behind,
    tile, measured, sems,
):
    depth = lax.axis_index("depth")
    loads = [
        pltpu.make_async_copy(tile_hbm, tile, sems.at[0]),
        pltpu.make_async_copy(measured_hbm, measured, sems.at[1]),
    ]
    for load in loads:
        load.start()
    own = choose_sides([pos[i, 0] for i in range(4)], [pos[i, 1] for i in range(4)], cnt[0])
    prev = choose_sides(
        [prev_pos[i, 0] for i in range(4)], [prev_pos[i, 1] for i in range(4)], prev_cnt[0]
    )
    for k, side in enumerate(own + prev):
        for w, word in enumerate(side):
            plan[k * SPAN + w] = word
    for load in loads:
        load.wait()

    def copy_rows(out, at, j, first, count):
        start = plan[at + 2 + 5 * j + 3]
        low = pl.multiple_of(plan[at + 2 + 5 * j + 1] * N, N)
        high = pl.multiple_of(plan[at + 2 + 5 * j + 1] * N + N, N)
        keep = lanes() >= plan[at + 2 + 5 * j + 2]

        def step(g, carry):
            src = pl.multiple_of((first + g) * 8, 8)
            dst = pl.multiple_of((start + g) * 8, 8)
            for c in range(2):
                out[c, pl.ds(dst, 8), :] = jnp.where(
                    keep, tile[c, pl.ds(src, 8), pl.ds(low, N)], tile[c, pl.ds(src, 8), pl.ds(high, N)]
                )
            return carry

        lax.fori_loop(0, count, step, 0)

    def right_job(j, carry):
        first = lax.div(plan[OWN_RIGHT + 2 + 5 * j], 8)
        copy_rows(ahead, OWN_RIGHT, j, first, 32 - first)
        slot = plan[OWN_RIGHT + 2 + 5 * j + 4]
        dst = pl.multiple_of((plan[OWN_RIGHT + 1] + 8 * j) * 8, 8)
        for c in range(2):
            src = pl.multiple_of(depth * HALF + 64 * c, 64)
            ahead[c, pl.ds(dst, 64), :] = measured[slot, pl.ds(src, 64), :]
        return carry

    lax.fori_loop(0, plan[OWN_RIGHT], right_job, 0)

    def left_job(j, carry):
        copy_rows(behind, PREV_LEFT, j, 0, lax.div(plan[PREV_LEFT + 2 + 5 * j] + 7, 8))
        return carry

    lax.fori_loop(0, plan[PREV_LEFT], left_job, 0)


def exchange_kernel(
    n_lat, ahead, behind, tile, received, other,
    row_send, row_recv, tile_send, tile_recv,
):
    depth = lax.axis_index("depth")
    lat = lax.axis_index("lat")
    after = lax.rem(lat + 1, n_lat)
    before = lax.rem(lat + n_lat - 1, n_lat)
    greet(depth, lat, after, before)
    pl.semaphore_wait(pltpu.get_barrier_semaphore(), 4)
    sends = [
        remote(ahead, received.at[depth], row_send.at[0], row_recv.at[depth], 1, after),
        remote(behind, received.at[depth], row_send.at[1], row_recv.at[depth], 0, before),
    ]
    for copy in sends:
        copy.start()
    swap = remote(tile, other, tile_send, tile_recv, 1 - depth, lat)
    swap.start()
    for copy in sends:
        copy.wait_send()
    for s in range(2):
        remote(ahead, received.at[s], row_send.at[0], row_recv.at[s], 1, after).wait_recv()
    swap.wait()


def remote(src, dst, send, recv, depth, lat):
    return pltpu.make_async_remote_copy(
        src_ref=src,
        dst_ref=dst,
        send_sem=send,
        recv_sem=recv,
        device_id=(depth, lat),
        device_id_type=pl.DeviceIdType.MESH,
    )


def greet(depth, lat, after, before):
    barrier = pltpu.get_barrier_semaphore()
    partners = [
        (depth, after),
        (depth, before),
        (1 - depth, jnp.where(depth == 0, after, before)),
        (1 - depth, lat),
    ]
    for partner in partners:
        pl.semaphore_signal(
            barrier, inc=1, device_id=partner, device_id_type=pl.DeviceIdType.MESH
        )


def return_kernel(
    n_lat, rows_hbm, theirs_hbm, received, partner,
    row_send, row_recv, swap_send, swap_recv,
):
    depth = lax.axis_index("depth")
    lat = lax.axis_index("lat")
    after = lax.rem(lat + 1, n_lat)
    before = lax.rem(lat + n_lat - 1, n_lat)
    greet(depth, lat, after, before)
    pl.semaphore_wait(pltpu.get_barrier_semaphore(), 4)
    target = jnp.where(depth == 0, after, before)
    sends = [
        remote(
            rows_hbm.at[s], received.at[depth], row_send.at[s], row_recv.at[depth], s, target
        )
        for s in range(2)
    ]
    for copy in sends:
        copy.start()
    swap = remote(theirs_hbm, partner, swap_send, swap_recv, 1 - depth, lat)
    swap.start()
    for copy in sends:
        copy.wait_send()
    for c in range(2):
        remote(
            rows_hbm.at[0], received.at[c], row_send.at[0], row_recv.at[c], 0, target
        ).wait_recv()
    swap.wait()


P_PLUS, P_MINUS, F_EVEN, F_ODD = 0, 1, 2, 3
TURNED = 4


def halves(x):
    hi = x.astype(jnp.bfloat16)
    lo = (x - hi.astype(jnp.float32)).astype(jnp.bfloat16)
    return hi, lo


def dot(a, b):
    return jnp.dot(a, b, preferred_element_type=jnp.float32)


def times_right(x, table, at):
    hi, lo = halves(x)
    return dot(
        jnp.concatenate([hi, lo, hi], axis=1),
        jnp.concatenate([table[at, 0], table[at, 0], table[at, 1]], axis=0),
    )


def times_left(table, at, x):
    hi, lo = halves(x)
    return dot(
        jnp.concatenate([table[at, 0], table[at, 0], table[at, 1]], axis=1),
        jnp.concatenate([hi, lo, hi], axis=0),
    )


def fold_columns(re, im):
    plus = jnp.concatenate([re[:, :HALF] + re[:, HALF:], im[:, :HALF] + im[:, HALF:]], axis=1)
    minus = jnp.concatenate([re[:, :HALF] - re[:, HALF:], im[:, :HALF] - im[:, HALF:]], axis=1)
    return plus, minus


def pair_columns(re, im):
    return (
        jnp.concatenate([re[:, :HALF], im[:, :HALF]], axis=1),
        jnp.concatenate([re[:, HALF:], im[:, HALF:]], axis=1),
    )


def fold_rows(re, im):
    plus = jnp.concatenate([re[:HALF] + re[HALF:], im[:HALF] + im[HALF:]], axis=0)
    minus = jnp.concatenate([re[:HALF] - re[HALF:], im[:HALF] - im[HALF:]], axis=0)
    return plus, minus


def pair_rows(re, im):
    return (
        jnp.concatenate([re[:HALF], im[:HALF]], axis=0),
        jnp.concatenate([re[HALF:], im[HALF:]], axis=0),
    )


def propagate(re, im, table, adjoint):
    left, right = (TURNED, 0) if adjoint else (0, TURNED)
    plus, minus = fold_columns(re, im)
    plus = times_right(plus, table, right + P_PLUS)
    minus = times_right(minus, table, right + P_MINUS)
    re, im = pair_columns(plus + minus, plus - minus)
    plus, minus = fold_rows(re, im)
    plus = times_left(table, left + P_PLUS, plus)
    minus = times_left(table, left + P_MINUS, minus)
    return pair_rows(plus + minus, plus - minus)


def to_spectrum(re, im, table):
    plus, minus = fold_columns(re, im)
    re, im = pair_columns(
        times_right(plus, table, TURNED + F_EVEN), times_right(minus, table, TURNED + F_ODD)
    )
    plus, minus = fold_rows(re, im)
    return pair_rows(times_left(table, F_EVEN, plus), times_left(table, F_ODD, minus))


def from_spectrum(re, im, table):
    even, odd = pair_columns(re, im)
    plus = times_right(even, table, F_EVEN)
    minus = times_right(odd, table, F_ODD)
    re, im = pair_columns(plus + minus, plus - minus)
    even, odd = pair_rows(re, im)
    plus = times_left(table, TURNED + F_EVEN, even)
    minus = times_left(table, TURNED + F_ODD, odd)
    return pair_rows(plus + minus, plus - minus)


def compute_kernel(
    plan, tile, other, rows_in, measured, probe, table,
    rows_out, mine, theirs,
    strips, received, amplitude, spread, grads, sems, fetch_sems, out_sems,
):
    depth = lax.axis_index("depth")
    at = jnp.where(depth == 0, OWN_LEFT, PREV_RIGHT)
    jobs = plan[at]

    def fetches(j):
        column = pl.multiple_of(plan[at + 2 + 5 * j + 1] * N, N)
        slot = plan[at + 2 + 5 * j + 4]
        return [
            pltpu.make_async_copy(
                tile.at[:, :, pl.ds(column, 2 * N)], strips.at[j, depth], fetch_sems.at[j, 0]
            ),
            pltpu.make_async_copy(
                other.at[:, :, pl.ds(column, 2 * N)], strips.at[j, 1 - depth], fetch_sems.at[j, 1]
            ),
            pltpu.make_async_copy(measured.at[slot], amplitude.at[j], fetch_sems.at[j, 2]),
        ]

    def stores(j):
        return [
            pltpu.make_async_copy(grads.at[j, depth], mine.at[j], out_sems.at[j, 0]),
            pltpu.make_async_copy(grads.at[j, 1 - depth], theirs.at[j], out_sems.at[j, 1]),
        ]

    copies = [
        pltpu.make_async_copy(rows_in.at[s], received.at[s, :, pl.ds(PAD, ROWS), :], sems.at[s])
        for s in range(2)
    ]
    for copy in copies:
        copy.start()

    def begin(j, carry):
        for copy in fetches(j):
            copy.start()
        return carry

    lax.fori_loop(0, jobs, begin, 0)
    row = lax.broadcasted_iota(jnp.int32, (N, N), 0)
    lane = lax.broadcasted_iota(jnp.int32, (N, N), 1)
    order = jnp.where(lane < HALF, 2 * lane, 2 * lane - (N - 1))
    shuffle = jnp.where(row == order, 1.0, 0.0).astype(jnp.bfloat16)
    for copy in copies:
        copy.wait()

    def job(j, carry):
        r = plan[at + 2 + 5 * j]
        shift = plan[at + 2 + 5 * j + 2]
        start = plan[at + 2 + 5 * j + 3]
        for copy in fetches(j):
            copy.wait()

        @pl.when(depth == 1)
        def _():
            src = pl.multiple_of(PAD + (plan[PREV_RIGHT + 1] + 8 * j) * 8, 8)
            for s in range(2):
                for c in range(2):
                    amplitude[j, pl.ds(128 * s + 64 * c, 64), :] = received[s, c, pl.ds(src, 64), :]

        low = jnp.where(depth == 0, r, 0)
        high = jnp.where(depth == 0, N, r)
        here = (row >= low) & (row < high)
        keep = lane >= shift
        base = jnp.where(depth == 0, 0, lax.div(r, 8))
        src = pl.multiple_of(PAD + (start - base) * 8, 8)

        def window(s):
            return [
                jnp.where(
                    here,
                    jnp.where(keep, strips[j, s, c, :, :N], strips[j, s, c, :, N:]),
                    received[s, c, pl.ds(src, N), :],
                )
                for c in range(2)
            ]

        def rolled(c):
            turned = pltpu.roll(probe[c], r, 0)
            return pltpu.roll(turned, jnp.where(shift == N, 0, shift), 1)

        p_re, p_im = rolled(0), rolled(1)
        o_re, o_im = window(0)
        w_re, w_im = propagate(
            p_re * o_re - p_im * o_im, p_re * o_im + p_im * o_re, table, False
        )
        o_re, o_im = window(1)
        f_re, f_im = to_spectrum(w_re * o_re - w_im * o_im, w_re * o_im + w_im * o_re, table)
        hi, lo = halves(amplitude[j])
        apart = dot(
            jnp.concatenate([hi, lo], axis=1), jnp.concatenate([shuffle, shuffle], axis=0)
        )
        for k in range(2):
            spread[k] = apart[:, HALF * k : HALF * k + HALF]
        apart = jnp.concatenate(
            [
                jnp.concatenate([spread[k, pl.ds(p, HALF, stride=2), :] for k in range(2)], axis=1)
                for p in range(2)
            ],
            axis=0,
        )
        factor = 1.0 - apart / jnp.sqrt(f_re * f_re + f_im * f_im + 1.0)
        a_re, a_im = from_spectrum(f_re * factor, f_im * factor, table)
        grads[j, 1, 0] = w_re * a_re + w_im * a_im
        grads[j, 1, 1] = w_re * a_im - w_im * a_re
        a_re, a_im = propagate(
            o_re * a_re + o_im * a_im, o_re * a_im - o_im * a_re, table, True
        )
        grads[j, 0, 0] = p_re * a_re + p_im * a_im
        grads[j, 0, 1] = p_re * a_im - p_im * a_re
        for copy in stores(j):
            copy.start()
        count = jnp.where(depth == 0, lax.div(r + 7, 8), 32 - lax.div(r, 8))

        def step(g, carry):
            src = pl.multiple_of((base + g) * 8, 8)
            dst = pl.multiple_of((start + g) * 8, 8)
            for s in range(2):
                for c in range(2):
                    rows_out[s, c, pl.ds(dst, 8), :] = grads[j, s, c, pl.ds(src, 8), :]
            return carry

        lax.fori_loop(0, count, step, 0)
        return carry

    lax.fori_loop(0, jobs, job, 0)

    def finish(j, carry):
        for copy in stores(j):
            copy.wait()
        return carry

    lax.fori_loop(0, jobs, finish, 0)


def gather_kernel(
    plan, rows_in, partner, mine, out,
    tile, rows, windows, sems, out_sems,
):
    depth = lax.axis_index("depth")
    copies = [
        pltpu.make_async_copy(mine, windows.at[depth], sems.at[0]),
        pltpu.make_async_copy(partner, windows.at[1 - depth], sems.at[1]),
        pltpu.make_async_copy(rows_in, rows, sems.at[2]),
    ]
    for copy in copies:
        copy.start()

    def clear(i, carry):
        at = pl.multiple_of(i * 8, 8)
        for c in range(2):
            tile[c, pl.ds(at, 8), :] = jnp.zeros((8, tile.shape[2]), jnp.float32)
        return carry

    lax.fori_loop(0, N // 8, clear, 0)
    for copy in copies:
        copy.wait()
    row = lax.broadcasted_iota(jnp.int32, (8, N), 0)

    def add(at, j, c, lower, packed):
        r = plan[at + 2 + 5 * j]
        block = plan[at + 2 + 5 * j + 1]
        start = plan[at + 2 + 5 * j + 3]
        first = 0 if lower else lax.div(r, 8)
        last = lax.div(r + 7, 8) if lower else 32
        keep = lanes() >= plan[at + 2 + 5 * j + 2]
        low = pl.multiple_of(block * N, N)
        high = pl.multiple_of(block * N + N, N)

        def step(g, carry):
            dst = pl.multiple_of(g * 8, 8)
            inside = (row + dst < r) if lower else (row + dst >= r)
            if packed:
                src = pl.multiple_of((start + g - first) * 8, 8)
                value = rows[0 if lower else 1, c, pl.ds(src, 8), :]
            else:
                value = windows[1 if lower else 0, j, c, pl.ds(dst, 8), :]
            value = jnp.where(inside, value, 0.0)
            tile[c, pl.ds(dst, 8), pl.ds(low, N)] += jnp.where(keep, value, 0.0)
            tile[c, pl.ds(dst, 8), pl.ds(high, N)] += jnp.where(keep, 0.0, value)
            return carry

        lax.fori_loop(first, last, step, 0)

    for c in range(2):
        for at, lower, packed in (
            (OWN_LEFT, False, False),
            (PREV_RIGHT, True, False),
            (OWN_RIGHT, False, True),
            (PREV_LEFT, True, True),
        ):

            def step(j, carry, at=at, lower=lower, packed=packed, c=c):
                add(at, j, c, lower, packed)
                return carry

            lax.fori_loop(0, plan[at], step, 0)
        pltpu.make_async_copy(tile.at[c], out.at[c], out_sems.at[c]).start()
    for c in range(2):
        pltpu.make_async_copy(tile.at[c], out.at[c], out_sems.at[c]).wait()


SMEM = pl.BlockSpec(memory_space=pltpu.SMEM)
VMEM = pl.BlockSpec(memory_space=pltpu.VMEM)
ANY = pl.BlockSpec(memory_space=pl.ANY)


def shape(*dims):
    return jax.ShapeDtypeStruct(dims, jnp.float32)


def shards(n_lat, object_slices, probe, measured, positions, counts):
    columns = object_slices.shape[3]
    tile = object_slices.reshape(object_slices.shape[1:])
    dma = pltpu.SemaphoreType.DMA
    prev_positions, prev_counts = pl.pallas_call(
        functools.partial(announce_kernel, n_lat),
        name="announce",
        out_shape=(
            jax.ShapeDtypeStruct(positions.shape, jnp.int32),
            jax.ShapeDtypeStruct(counts.shape, jnp.int32),
        ),
        in_specs=[ANY, ANY],
        out_specs=(ANY, ANY),
        scratch_shapes=[dma((2,)), dma((2,))],
        compiler_params=pltpu.CompilerParams(collective_id=2, has_side_effects=True),
    )(positions, counts)
    plan, ahead, behind = pl.pallas_call(
        pack_kernel,
        name="pack",
        out_shape=(
            jax.ShapeDtypeStruct((4 * SPAN,), jnp.int32),
            shape(2, ROWS, N),
            shape(2, ROWS, N),
        ),
        in_specs=[SMEM, SMEM, SMEM, SMEM, ANY, ANY],
        out_specs=(SMEM, VMEM, VMEM),
        scratch_shapes=[
            pltpu.VMEM((2, N, columns), jnp.float32),
            pltpu.VMEM((4, N, N), jnp.float32),
            dma((2,)),
        ],
        compiler_params=pltpu.CompilerParams(vmem_limit_bytes=40 << 20),
    )(positions, counts, prev_positions, prev_counts, tile, measured)
    rows_in, other = pl.pallas_call(
        functools.partial(exchange_kernel, n_lat),
        name="exchange",
        out_shape=(shape(2, 2, ROWS, N), shape(2, N, columns)),
        in_specs=[ANY, ANY, ANY],
        out_specs=(ANY, ANY),
        scratch_shapes=[dma((2,)), dma((2,)), dma, dma],
        compiler_params=pltpu.CompilerParams(collective_id=0, has_side_effects=True),
    )(ahead, behind, tile)

    table = jnp.asarray(tables())
    rows_out, mine, theirs = pl.pallas_call(
        compute_kernel,
        name="compute",
        out_shape=(
            shape(2, 2, ROWS, N),
            shape(MAX_JOBS, 2, N, N),
            shape(MAX_JOBS, 2, N, N),
        ),
        in_specs=[SMEM, ANY, ANY, ANY, ANY, VMEM, VMEM],
        out_specs=(VMEM, ANY, ANY),
        scratch_shapes=[
            pltpu.VMEM((MAX_JOBS, 2, 2, N, 2 * N), jnp.float32),
            pltpu.VMEM((2, 2, ROWS + 2 * PAD, N), jnp.float32),
            pltpu.VMEM((MAX_JOBS, N, N), jnp.float32),
            pltpu.VMEM((2, N, HALF), jnp.float32),
            pltpu.VMEM((MAX_JOBS, 2, 2, N, N), jnp.float32),
            dma((2,)), dma((MAX_JOBS, 3)), dma((MAX_JOBS, 2)),
        ],
        compiler_params=pltpu.CompilerParams(vmem_limit_bytes=50 << 20),
    )(plan, tile, other, rows_in, measured, probe, table)

    rows_back, partner = pl.pallas_call(
        functools.partial(return_kernel, n_lat),
        name="giveback",
        out_shape=(shape(2, 2, ROWS, N), shape(MAX_JOBS, 2, N, N)),
        in_specs=[ANY, ANY],
        out_specs=(ANY, ANY),
        scratch_shapes=[dma((2,)), dma((2,)), dma, dma],
        compiler_params=pltpu.CompilerParams(collective_id=1, has_side_effects=True),
    )(rows_out, theirs)

    out = pl.pallas_call(
        gather_kernel,
        name="gather",
        out_shape=shape(2, N, columns),
        in_specs=[SMEM, ANY, ANY, ANY],
        out_specs=ANY,
        scratch_shapes=[
            pltpu.VMEM((2, N, columns), jnp.float32),
            pltpu.VMEM((2, 2, ROWS, N), jnp.float32),
            pltpu.VMEM((2, MAX_JOBS, 2, N, N), jnp.float32),
            dma((3,)), dma((2,)),
        ],
        compiler_params=pltpu.CompilerParams(vmem_limit_bytes=40 << 20),
    )(plan, rows_back, partner, mine)
    return out.reshape(object_slices.shape)


def solution(mesh):
    return jax.shard_map(
        functools.partial(shards, mesh.shape["lat"]),
        mesh=mesh,
        in_specs=(
            P("depth", None, "lat", None),
            P(),
            P("lat", None, None),
            P("lat", None),
            P("lat"),
        ),
        out_specs=P("depth", None, "lat", None),
        check_vma=False,
    )
```

```python
import functools

import jax
import jax.numpy as jnp
import ml_dtypes
import numpy as np
from jax import lax
from jax.experimental import pallas as pl
from jax.experimental.pallas import tpu as pltpu
from jax.sharding import PartitionSpec as P

N = 256
HALF = 128
STRENGTH = 8.0
MAX_JOBS = 3
BUDGET = 48
ROWS = 8 * BUDGET
PAD = 256
SPAN = 20


def split_bf16(a):
    hi = a.astype(np.float32).astype(ml_dtypes.bfloat16)
    lo = (a - hi.astype(np.float64)).astype(np.float32).astype(ml_dtypes.bfloat16)
    return hi, lo


def tables():
    index = np.arange(N)
    angle = 2.0 * np.pi * ((index[:, None] * index[None, :]) % N) / N
    dft = np.exp(-1j * angle) / 16.0
    centred = (index - N * (index >= HALF)) / N
    turn = np.exp(1j * np.pi * STRENGTH * centred**2)
    prop = np.conj(dft) @ (turn[:, None] * dft)
    c0, c1 = prop[:HALF, :HALF], prop[:HALF, HALF:]

    def real_form(m):
        return np.block([[m.real, -m.imag], [m.imag, m.real]])

    forms = [real_form(m) for m in ((c0 + c1) / 2, (c0 - c1) / 2, dft[0::2, :HALF], dft[1::2, :HALF])]
    forms = forms + [m.T for m in forms]
    return np.stack([np.stack(split_bf16(m)) for m in forms])


OWN_LEFT, OWN_RIGHT, PREV_LEFT, PREV_RIGHT = 0, SPAN, 2 * SPAN, 3 * SPAN


def choose_sides(rows_of, cols_of, live):
    up = [lax.div(rows_of[i] + 7, 8) for i in range(4)]
    down = [32 - lax.div(rows_of[i], 8) for i in range(4)]
    best = jnp.int32(1 << 20)
    pick = jnp.int32(0)
    for mask in range(16):
        right = [(mask >> i) & 1 for i in range(4)]
        n_right = sum(right)
        if n_right > MAX_JOBS:
            continue
        top = max([i + 1 for i in range(4) if right[i]], default=0)
        lefts = [jnp.where(live > i, up[i], 0) for i in range(4) if not right[i]]
        cost_left = sum(lefts, jnp.int32(0))
        cost_right = sum([down[i] + 8 for i in range(4) if right[i]], jnp.int32(0))
        widest = jnp.maximum(cost_left, cost_right)
        most = jnp.maximum(live - n_right, n_right)
        bad = (live < top) | (widest > BUDGET) | (most > MAX_JOBS)
        key = most * 64 + widest + jnp.where(bad, jnp.int32(1 << 16), 0)
        pick = jnp.where(key < best, mask, pick)
        best = jnp.minimum(key, best)
    blocks = [jnp.minimum(lax.div(cols_of[i], N), 6) for i in range(4)]
    sides = []
    for side in range(2):
        mine = [(live > i) & ((lax.shift_right_logical(pick, i) & 1) == side) for i in range(4)]
        size = up if side == 0 else down
        count, total = jnp.int32(0), jnp.int32(0)
        words = [[jnp.int32(0)] * 5 for _ in range(MAX_JOBS)]
        for i in range(4):
            fields = [rows_of[i], blocks[i], cols_of[i] - blocks[i] * N, total, jnp.int32(i)]
            for j in range(MAX_JOBS):
                here = mine[i] & (count == j)
                words[j] = [jnp.where(here, f, w) for f, w in zip(fields, words[j])]
            count = count + jnp.where(mine[i], 1, 0)
            total = total + jnp.where(mine[i], size[i], 0)
        sides.append([count, total] + [w for job in words for w in job])
    return sides


def lanes():
    return lax.broadcasted_iota(jnp.int32, (8, N), 1)


def announce_kernel(
    n_lat, pos_hbm, cnt, tile_hbm, measured_hbm,
    pos, prev_pos, prev_cnt, tile, measured,
    send, recv, local,
):
    depth = lax.axis_index("depth")
    lat = lax.axis_index("lat")
    after = lax.rem(lat + 1, n_lat)
    before = lax.rem(lat + n_lat - 1, n_lat)
    barrier = pltpu.get_barrier_semaphore()
    for other in (after, before):
        pl.semaphore_signal(
            barrier, inc=1, device_id=(depth, other), device_id_type=pl.DeviceIdType.MESH
        )
    loads = [
        pltpu.make_async_copy(pos_hbm, pos, local.at[0]),
        pltpu.make_async_copy(tile_hbm, tile, local.at[1]),
        pltpu.make_async_copy(measured_hbm, measured, local.at[2]),
    ]
    for load in loads:
        load.start()
    pl.semaphore_wait(barrier, 2)
    copies = [
        remote(pos_hbm, prev_pos, send.at[0], recv.at[0], depth, after),
        remote(cnt, prev_cnt, send.at[1], recv.at[1], depth, after),
    ]
    for copy in copies:
        copy.start()
    for load in loads:
        load.wait()
    for copy in copies:
        copy.wait()


def pack_kernel(
    pos, cnt, prev_pos, prev_cnt, tile, measured, plan, ahead, behind
):
    depth = lax.axis_index("depth")
    own = choose_sides([pos[0, i] for i in range(4)], [pos[1, i] for i in range(4)], cnt[0])
    prev = choose_sides(
        [prev_pos[0, i] for i in range(4)], [prev_pos[1, i] for i in range(4)], prev_cnt[0]
    )
    for k, side in enumerate(own + prev):
        for w, word in enumerate(side):
            plan[k * SPAN + w] = word

    def copy_rows(out, at, j, first, count):
        start = plan[at + 2 + 5 * j + 3]
        low = pl.multiple_of(plan[at + 2 + 5 * j + 1] * N, N)
        high = pl.multiple_of(plan[at + 2 + 5 * j + 1] * N + N, N)
        keep = lanes() >= plan[at + 2 + 5 * j + 2]

        def step(g, carry):
            src = pl.multiple_of((first + g) * 8, 8)
            dst = pl.multiple_of((start + g) * 8, 8)
            for c in range(2):
                out[c, pl.ds(dst, 8), :] = jnp.where(
                    keep, tile[c, pl.ds(src, 8), pl.ds(low, N)], tile[c, pl.ds(src, 8), pl.ds(high, N)]
                )
            return carry

        lax.fori_loop(0, count, step, 0)

    def right_job(j, carry):
        first = lax.div(plan[OWN_RIGHT + 2 + 5 * j], 8)
        copy_rows(ahead, OWN_RIGHT, j, first, 32 - first)
        slot = plan[OWN_RIGHT + 2 + 5 * j + 4]
        dst = pl.multiple_of((plan[OWN_RIGHT + 1] + 8 * j) * 8, 8)
        for c in range(2):
            src = pl.multiple_of(depth * HALF + 64 * c, 64)
            ahead[c, pl.ds(dst, 64), :] = measured[slot, pl.ds(src, 64), :]
        return carry

    lax.fori_loop(0, plan[OWN_RIGHT], right_job, 0)

    def left_job(j, carry):
        copy_rows(behind, PREV_LEFT, j, 0, lax.div(plan[PREV_LEFT + 2 + 5 * j] + 7, 8))
        return carry

    lax.fori_loop(0, plan[PREV_LEFT], left_job, 0)


def exchange_kernel(
    n_lat, ahead, behind, tile, received, other,
    row_send, row_recv, tile_send, tile_recv,
):
    depth = lax.axis_index("depth")
    lat = lax.axis_index("lat")
    after = lax.rem(lat + 1, n_lat)
    before = lax.rem(lat + n_lat - 1, n_lat)
    greet(depth, lat, after, before)
    pl.semaphore_wait(pltpu.get_barrier_semaphore(), 4)

    def slot(s):
        return received.at[s, :, pl.ds(PAD, ROWS), :]

    sends = [
        remote(ahead, slot(depth), row_send.at[0], row_recv.at[depth], 1, after),
        remote(behind, slot(depth), row_send.at[1], row_recv.at[depth], 0, before),
    ]
    for copy in sends:
        copy.start()
    swap = remote(tile, other, tile_send, tile_recv, 1 - depth, lat)
    swap.start()
    for copy in sends:
        copy.wait_send()
    for s in range(2):
        remote(ahead, slot(s), row_send.at[0], row_recv.at[s], 1, after).wait_recv()
    swap.wait()


def remote(src, dst, send, recv, depth, lat):
    return pltpu.make_async_remote_copy(
        src_ref=src,
        dst_ref=dst,
        send_sem=send,
        recv_sem=recv,
        device_id=(depth, lat),
        device_id_type=pl.DeviceIdType.MESH,
    )


def greet(depth, lat, after, before):
    barrier = pltpu.get_barrier_semaphore()
    partners = [
        (depth, after),
        (depth, before),
        (1 - depth, jnp.where(depth == 0, after, before)),
        (1 - depth, lat),
    ]
    for partner in partners:
        pl.semaphore_signal(
            barrier, inc=1, device_id=partner, device_id_type=pl.DeviceIdType.MESH
        )


def return_kernel(
    n_lat, rows, windows, received, partner,
    row_send, row_recv, swap_send, swap_recv,
):
    depth = lax.axis_index("depth")
    lat = lax.axis_index("lat")
    after = lax.rem(lat + 1, n_lat)
    before = lax.rem(lat + n_lat - 1, n_lat)
    greet(depth, lat, after, before)
    pl.semaphore_wait(pltpu.get_barrier_semaphore(), 4)
    target = jnp.where(depth == 0, after, before)
    sends = [
        remote(rows.at[s], received.at[depth], row_send.at[s], row_recv.at[depth], s, target)
        for s in range(2)
    ]
    for copy in sends:
        copy.start()
    swap = remote(windows.at[1 - depth], partner, swap_send, swap_recv, 1 - depth, lat)
    swap.start()
    for copy in sends:
        copy.wait_send()
    for c in range(2):
        remote(
            rows.at[0], received.at[c], row_send.at[0], row_recv.at[c], 0, target
        ).wait_recv()
    swap.wait()


P_PLUS, P_MINUS, F_EVEN, F_ODD = 0, 1, 2, 3
TURNED = 4


def halves(x):
    hi = x.astype(jnp.bfloat16)
    lo = (x - hi.astype(jnp.float32)).astype(jnp.bfloat16)
    return hi, lo


def dot(a, b):
    return jnp.dot(a, b, preferred_element_type=jnp.float32)


def times_right(x, table, at):
    hi, lo = halves(x)
    return dot(
        jnp.concatenate([hi, lo, hi], axis=1),
        jnp.concatenate([table[at, 0], table[at, 0], table[at, 1]], axis=0),
    )


def times_left(table, at, x):
    hi, lo = halves(x)
    return dot(
        jnp.concatenate([table[at, 0], table[at, 0], table[at, 1]], axis=1),
        jnp.concatenate([hi, lo, hi], axis=0),
    )


def fold_columns(re, im):
    plus = jnp.concatenate([re[:, :HALF] + re[:, HALF:], im[:, :HALF] + im[:, HALF:]], axis=1)
    minus = jnp.concatenate([re[:, :HALF] - re[:, HALF:], im[:, :HALF] - im[:, HALF:]], axis=1)
    return plus, minus


def pair_columns(re, im):
    return (
        jnp.concatenate([re[:, :HALF], im[:, :HALF]], axis=1),
        jnp.concatenate([re[:, HALF:], im[:, HALF:]], axis=1),
    )


def fold_rows(re, im):
    plus = jnp.concatenate([re[:HALF] + re[HALF:], im[:HALF] + im[HALF:]], axis=0)
    minus = jnp.concatenate([re[:HALF] - re[HALF:], im[:HALF] - im[HALF:]], axis=0)
    return plus, minus


def pair_rows(re, im):
    return (
        jnp.concatenate([re[:HALF], im[:HALF]], axis=0),
        jnp.concatenate([re[HALF:], im[HALF:]], axis=0),
    )


def propagate(re, im, table, adjoint):
    left, right = (TURNED, 0) if adjoint else (0, TURNED)
    plus, minus = fold_columns(re, im)
    plus = times_right(plus, table, right + P_PLUS)
    minus = times_right(minus, table, right + P_MINUS)
    re, im = pair_columns(plus + minus, plus - minus)
    plus, minus = fold_rows(re, im)
    plus = times_left(table, left + P_PLUS, plus)
    minus = times_left(table, left + P_MINUS, minus)
    return pair_rows(plus + minus, plus - minus)


def to_spectrum(re, im, table):
    plus, minus = fold_columns(re, im)
    re, im = pair_columns(
        times_right(plus, table, TURNED + F_EVEN), times_right(minus, table, TURNED + F_ODD)
    )
    plus, minus = fold_rows(re, im)
    return pair_rows(times_left(table, F_EVEN, plus), times_left(table, F_ODD, minus))


def from_spectrum(re, im, table):
    even, odd = pair_columns(re, im)
    plus = times_right(even, table, F_EVEN)
    minus = times_right(odd, table, F_ODD)
    re, im = pair_columns(plus + minus, plus - minus)
    even, odd = pair_rows(re, im)
    plus = times_left(table, TURNED + F_EVEN, even)
    minus = times_left(table, TURNED + F_ODD, odd)
    return pair_rows(plus + minus, plus - minus)


def compute_kernel(
    plan, tile, other, received, measured, probe, table,
    rows_out, grads,
    amplitude, spread,
):
    depth = lax.axis_index("depth")
    at = jnp.where(depth == 0, OWN_LEFT, PREV_RIGHT)
    jobs = plan[at]
    row = lax.broadcasted_iota(jnp.int32, (N, N), 0)
    lane = lax.broadcasted_iota(jnp.int32, (N, N), 1)
    order = jnp.where(lane < HALF, 2 * lane, 2 * lane - (N - 1))
    shuffle = jnp.where(row == order, 1.0, 0.0).astype(jnp.bfloat16)

    def job(j, carry):
        r = plan[at + 2 + 5 * j]
        shift = plan[at + 2 + 5 * j + 2]
        start = plan[at + 2 + 5 * j + 3]
        column = pl.multiple_of(plan[at + 2 + 5 * j + 1] * N, N)
        slot = plan[at + 2 + 5 * j + 4]

        @pl.when(depth == 0)
        def _():
            amplitude[...] = measured[slot]

        @pl.when(depth == 1)
        def _():
            src = pl.multiple_of(PAD + (plan[PREV_RIGHT + 1] + 8 * j) * 8, 8)
            for s in range(2):
                for c in range(2):
                    amplitude[pl.ds(128 * s + 64 * c, 64), :] = received[s, c, pl.ds(src, 64), :]

        low = jnp.where(depth == 0, r, 0)
        high = jnp.where(depth == 0, N, r)
        here = (row >= low) & (row < high)
        keep = lane >= shift
        base = jnp.where(depth == 0, 0, lax.div(r, 8))
        src = pl.multiple_of(PAD + (start - base) * 8, 8)

        def window(s):
            near = depth == s
            left, right = pl.ds(column, N), pl.ds(pl.multiple_of(column + N, N), N)
            return [
                jnp.where(
                    here,
                    jnp.where(
                        keep,
                        jnp.where(near, tile[c, :, left], other[c, :, left]),
                        jnp.where(near, tile[c, :, right], other[c, :, right]),
                    ),
                    received[s, c, pl.ds(src, N), :],
                )
                for c in range(2)
            ]

        def rolled(c):
            turned = pltpu.roll(probe[c], r, 0)
            return pltpu.roll(turned, jnp.where(shift == N, 0, shift), 1)

        p_re, p_im = rolled(0), rolled(1)
        o_re, o_im = window(0)
        w_re, w_im = propagate(
            p_re * o_re - p_im * o_im, p_re * o_im + p_im * o_re, table, False
        )
        o_re, o_im = window(1)
        f_re, f_im = to_spectrum(w_re * o_re - w_im * o_im, w_re * o_im + w_im * o_re, table)
        hi, lo = halves(amplitude[...])
        apart = dot(
            jnp.concatenate([hi, lo], axis=1), jnp.concatenate([shuffle, shuffle], axis=0)
        )
        for k in range(2):
            spread[k] = apart[:, HALF * k : HALF * k + HALF]
        apart = jnp.concatenate(
            [
                jnp.concatenate([spread[k, pl.ds(p, HALF, stride=2), :] for k in range(2)], axis=1)
                for p in range(2)
            ],
            axis=0,
        )
        factor = 1.0 - apart / jnp.sqrt(f_re * f_re + f_im * f_im + 1.0)
        a_re, a_im = from_spectrum(f_re * factor, f_im * factor, table)
        grads[1, j, 0] = w_re * a_re + w_im * a_im
        grads[1, j, 1] = w_re * a_im - w_im * a_re
        a_re, a_im = propagate(
            o_re * a_re + o_im * a_im, o_re * a_im - o_im * a_re, table, True
        )
        grads[0, j, 0] = p_re * a_re + p_im * a_im
        grads[0, j, 1] = p_re * a_im - p_im * a_re
        count = jnp.where(depth == 0, lax.div(r + 7, 8), 32 - lax.div(r, 8))

        def step(g, carry):
            src = pl.multiple_of((base + g) * 8, 8)
            dst = pl.multiple_of((start + g) * 8, 8)
            for s in range(2):
                for c in range(2):
                    rows_out[s, c, pl.ds(dst, 8), :] = grads[s, j, c, pl.ds(src, 8), :]
            return carry

        lax.fori_loop(0, count, step, 0)
        return carry

    lax.fori_loop(0, jobs, job, 0)


def gather_kernel(plan, rows, partner, grads, out, tile, out_sems):
    depth = lax.axis_index("depth")

    def clear(i, carry):
        at = pl.multiple_of(i * 8, 8)
        for c in range(2):
            tile[c, pl.ds(at, 8), :] = jnp.zeros((8, tile.shape[2]), jnp.float32)
        return carry

    lax.fori_loop(0, N // 8, clear, 0)
    row = lax.broadcasted_iota(jnp.int32, (8, N), 0)

    def add(at, j, c, lower, packed, near):
        r = plan[at + 2 + 5 * j]
        block = plan[at + 2 + 5 * j + 1]
        start = plan[at + 2 + 5 * j + 3]
        first = 0 if lower else lax.div(r, 8)
        last = lax.div(r + 7, 8) if lower else 32
        keep = lanes() >= plan[at + 2 + 5 * j + 2]
        low = pl.multiple_of(block * N, N)
        high = pl.multiple_of(block * N + N, N)

        def step(g, carry):
            dst = pl.multiple_of(g * 8, 8)
            inside = (row + dst < r) if lower else (row + dst >= r)
            if packed:
                src = pl.multiple_of((start + g - first) * 8, 8)
                value = rows[0 if lower else 1, c, pl.ds(src, 8), :]
            else:
                value = grads[depth, j, c, pl.ds(dst, 8), :] if near else partner[j, c, pl.ds(dst, 8), :]
            value = jnp.where(inside, value, 0.0)
            tile[c, pl.ds(dst, 8), pl.ds(low, N)] += jnp.where(keep, value, 0.0)
            tile[c, pl.ds(dst, 8), pl.ds(high, N)] += jnp.where(keep, 0.0, value)
            return carry

        lax.fori_loop(first, last, step, 0)

    def run(at, c, lower, packed, near):
        def step(j, carry):
            add(at, j, c, lower, packed, near)
            return carry

        lax.fori_loop(0, plan[at], step, 0)

    for c in range(2):

        @pl.when(depth == 0)
        def _(c=c):
            run(OWN_LEFT, c, False, False, True)
            run(PREV_RIGHT, c, True, False, False)

        @pl.when(depth == 1)
        def _(c=c):
            run(OWN_LEFT, c, False, False, False)
            run(PREV_RIGHT, c, True, False, True)

        run(OWN_RIGHT, c, False, True, False)
        run(PREV_LEFT, c, True, True, False)
        pltpu.make_async_copy(tile.at[c], out.at[c], out_sems.at[c]).start()
    for c in range(2):
        pltpu.make_async_copy(tile.at[c], out.at[c], out_sems.at[c]).wait()


SMEM = pl.BlockSpec(memory_space=pltpu.SMEM)
VMEM = pl.BlockSpec(memory_space=pltpu.VMEM)
HBM = pl.BlockSpec(memory_space=pltpu.HBM)


def shape(*dims):
    return jax.ShapeDtypeStruct(dims, jnp.float32)


def shards(n_lat, object_slices, probe, measured, positions, counts):
    columns = object_slices.shape[3]
    tile = object_slices.reshape(object_slices.shape[1:])
    dma = pltpu.SemaphoreType.DMA
    positions = positions.T
    own_positions, prev_positions, prev_counts, tile, measured = pl.pallas_call(
        functools.partial(announce_kernel, n_lat),
        name="announce",
        out_shape=(
            jax.ShapeDtypeStruct(positions.shape, jnp.int32),
            jax.ShapeDtypeStruct(positions.shape, jnp.int32),
            jax.ShapeDtypeStruct(counts.shape, jnp.int32),
            shape(*tile.shape),
            shape(*measured.shape),
        ),
        in_specs=[HBM, HBM, HBM, HBM],
        out_specs=(VMEM, VMEM, VMEM, VMEM, VMEM),
        scratch_shapes=[dma((2,)), dma((2,)), dma((3,))],
        compiler_params=pltpu.CompilerParams(
            collective_id=2, has_side_effects=True, vmem_limit_bytes=8 << 20
        ),
    )(positions, counts, tile, measured)
    plan, ahead, behind = pl.pallas_call(
        pack_kernel,
        name="pack",
        out_shape=(
            jax.ShapeDtypeStruct((4 * SPAN,), jnp.int32),
            shape(2, ROWS, N),
            shape(2, ROWS, N),
        ),
        in_specs=[SMEM, SMEM, SMEM, SMEM, VMEM, VMEM],
        out_specs=(SMEM, VMEM, VMEM),
        compiler_params=pltpu.CompilerParams(vmem_limit_bytes=4 << 20),
    )(own_positions, counts, prev_positions, prev_counts, tile, measured)
    received, other = pl.pallas_call(
        functools.partial(exchange_kernel, n_lat),
        name="exchange",
        out_shape=(shape(2, 2, ROWS + 2 * PAD, N), shape(2, N, columns)),
        in_specs=[VMEM, VMEM, VMEM],
        out_specs=(VMEM, VMEM),
        scratch_shapes=[dma((2,)), dma((2,)), dma, dma],
        compiler_params=pltpu.CompilerParams(
            collective_id=0, has_side_effects=True, vmem_limit_bytes=12 << 20
        ),
    )(ahead, behind, tile)

    table = jnp.asarray(tables())
    rows_out, grads = pl.pallas_call(
        compute_kernel,
        name="compute",
        out_shape=(shape(2, 2, ROWS, N), shape(2, MAX_JOBS, 2, N, N)),
        in_specs=[SMEM, VMEM, VMEM, VMEM, VMEM, VMEM, VMEM],
        out_specs=(VMEM, VMEM),
        scratch_shapes=[
            pltpu.VMEM((N, N), jnp.float32),
            pltpu.VMEM((2, N, HALF), jnp.float32),
        ],
        compiler_params=pltpu.CompilerParams(vmem_limit_bytes=30 << 20),
    )(plan, tile, other, received, measured, probe, table)

    rows_back, partner = pl.pallas_call(
        functools.partial(return_kernel, n_lat),
        name="giveback",
        out_shape=(shape(2, 2, ROWS, N), shape(MAX_JOBS, 2, N, N)),
        in_specs=[VMEM, VMEM],
        out_specs=(VMEM, VMEM),
        scratch_shapes=[dma((2,)), dma((2,)), dma, dma],
        compiler_params=pltpu.CompilerParams(
            collective_id=1, has_side_effects=True, vmem_limit_bytes=12 << 20
        ),
    )(rows_out, grads)

    out = pl.pallas_call(
        gather_kernel,
        name="gather",
        out_shape=shape(2, N, columns),
        in_specs=[SMEM, VMEM, VMEM, VMEM],
        out_specs=HBM,
        scratch_shapes=[pltpu.VMEM((2, N, columns), jnp.float32), dma((2,))],
        compiler_params=pltpu.CompilerParams(vmem_limit_bytes=20 << 20),
    )(plan, rows_back, partner, grads)
    return out.reshape(object_slices.shape)


def solution(mesh):
    return jax.shard_map(
        functools.partial(shards, mesh.shape["lat"]),
        mesh=mesh,
        in_specs=(
            P("depth", None, "lat", None),
            P(),
            P("lat", None, None),
            P("lat", None),
            P("lat"),
        ),
        out_specs=P("depth", None, "lat", None),
        check_vma=False,
    )
```

```python
import functools

import jax
import jax.numpy as jnp
import ml_dtypes
import numpy as np
from jax import lax
from jax.experimental import pallas as pl
from jax.experimental.pallas import tpu as pltpu
from jax.sharding import PartitionSpec as P

N = 256
HALF = 128
STRENGTH = 8.0
MAX_JOBS = 3
BUDGET = 48
ROWS = 8 * BUDGET
PAD = 256
SPAN = 20


def split_bf16(a):
    hi = a.astype(np.float32).astype(ml_dtypes.bfloat16)
    lo = (a - hi.astype(np.float64)).astype(np.float32).astype(ml_dtypes.bfloat16)
    return hi, lo


def tables():
    index = np.arange(N)
    angle = 2.0 * np.pi * ((index[:, None] * index[None, :]) % N) / N
    dft = np.exp(-1j * angle) / 16.0
    centred = (index - N * (index >= HALF)) / N
    turn = np.exp(1j * np.pi * STRENGTH * centred**2)
    prop = np.conj(dft) @ (turn[:, None] * dft)
    c0, c1 = prop[:HALF, :HALF], prop[:HALF, HALF:]

    def real_form(m):
        return np.block([[m.real, -m.imag], [m.imag, m.real]])

    forms = [real_form(m) for m in ((c0 + c1) / 2, (c0 - c1) / 2, dft[0::2, :HALF], dft[1::2, :HALF])]
    forms = forms + [m.T for m in forms]
    return np.stack([np.stack(split_bf16(m)) for m in forms])


OWN_LEFT, OWN_RIGHT, PREV_LEFT, PREV_RIGHT = 0, SPAN, 2 * SPAN, 3 * SPAN


def choose_sides(rows_of, cols_of, live):
    up = [lax.div(rows_of[i] + 7, 8) for i in range(4)]
    down = [32 - lax.div(rows_of[i], 8) for i in range(4)]
    best = jnp.int32(1 << 20)
    pick = jnp.int32(0)
    for mask in range(16):
        right = [(mask >> i) & 1 for i in range(4)]
        n_right = sum(right)
        if n_right > MAX_JOBS:
            continue
        top = max([i + 1 for i in range(4) if right[i]], default=0)
        lefts = [jnp.where(live > i, up[i], 0) for i in range(4) if not right[i]]
        cost_left = sum(lefts, jnp.int32(0))
        cost_right = sum([down[i] + 8 for i in range(4) if right[i]], jnp.int32(0))
        widest = jnp.maximum(cost_left, cost_right)
        most = jnp.maximum(live - n_right, n_right)
        bad = (live < top) | (widest > BUDGET) | (most > MAX_JOBS)
        key = most * 64 + widest + jnp.where(bad, jnp.int32(1 << 16), 0)
        pick = jnp.where(key < best, mask, pick)
        best = jnp.minimum(key, best)
    blocks = [jnp.minimum(lax.div(cols_of[i], N), 6) for i in range(4)]
    sides = []
    for side in range(2):
        mine = [(live > i) & ((lax.shift_right_logical(pick, i) & 1) == side) for i in range(4)]
        size = up if side == 0 else down
        count, total = jnp.int32(0), jnp.int32(0)
        words = [[jnp.int32(0)] * 5 for _ in range(MAX_JOBS)]
        for i in range(4):
            fields = [rows_of[i], blocks[i], cols_of[i] - blocks[i] * N, total, jnp.int32(i)]
            for j in range(MAX_JOBS):
                here = mine[i] & (count == j)
                words[j] = [jnp.where(here, f, w) for f, w in zip(fields, words[j])]
            count = count + jnp.where(mine[i], 1, 0)
            total = total + jnp.where(mine[i], size[i], 0)
        sides.append([count, total] + [w for job in words for w in job])
    return sides


def lanes():
    return lax.broadcasted_iota(jnp.int32, (8, N), 1)


def announce_kernel(n_lat, pos, cnt, prev_pos, prev_cnt, send, recv):
    depth = lax.axis_index("depth")
    lat = lax.axis_index("lat")
    after = lax.rem(lat + 1, n_lat)
    before = lax.rem(lat + n_lat - 1, n_lat)
    barrier = pltpu.get_barrier_semaphore()
    for other in (after, before):
        pl.semaphore_signal(
            barrier, inc=1, device_id=(depth, other), device_id_type=pl.DeviceIdType.MESH
        )
    pl.semaphore_wait(barrier, 2)
    copies = [
        remote(pos, prev_pos, send.at[0], recv.at[0], depth, after),
        remote(cnt, prev_cnt, send.at[1], recv.at[1], depth, after),
    ]
    for copy in copies:
        copy.start()
    for copy in copies:
        copy.wait()


def pack_kernel(
    pos_hbm, cnt, prev_pos_hbm, prev_cnt, tile_hbm, measured_hbm, plan, ahead, behind,
    tile, measured, pos, prev_pos, sems,
):
    depth = lax.axis_index("depth")
    loads = [
        pltpu.make_async_copy(pos_hbm, pos, sems.at[0]),
        pltpu.make_async_copy(prev_pos_hbm, prev_pos, sems.at[1]),
        pltpu.make_async_copy(tile_hbm, tile, sems.at[2]),
        pltpu.make_async_copy(measured_hbm, measured, sems.at[3]),
    ]
    for load in loads:
        load.start()
    for load in loads[:2]:
        load.wait()
    own = choose_sides([pos[0, i] for i in range(4)], [pos[1, i] for i in range(4)], cnt[0])
    prev = choose_sides(
        [prev_pos[0, i] for i in range(4)], [prev_pos[1, i] for i in range(4)], prev_cnt[0]
    )
    for k, side in enumerate(own + prev):
        for w, word in enumerate(side):
            plan[k * SPAN + w] = word
    for load in loads[2:]:
        load.wait()

    def copy_rows(out, at, j, first, count):
        start = plan[at + 2 + 5 * j + 3]
        low = pl.multiple_of(plan[at + 2 + 5 * j + 1] * N, N)
        high = pl.multiple_of(plan[at + 2 + 5 * j + 1] * N + N, N)
        keep = lanes() >= plan[at + 2 + 5 * j + 2]

        def step(g, carry):
            src = pl.multiple_of((first + g) * 8, 8)
            dst = pl.multiple_of((start + g) * 8, 8)
            for c in range(2):
                out[c, pl.ds(dst, 8), :] = jnp.where(
                    keep, tile[c, pl.ds(src, 8), pl.ds(low, N)], tile[c, pl.ds(src, 8), pl.ds(high, N)]
                )
            return carry

        lax.fori_loop(0, count, step, 0)

    def right_job(j, carry):
        first = lax.div(plan[OWN_RIGHT + 2 + 5 * j], 8)
        copy_rows(ahead, OWN_RIGHT, j, first, 32 - first)
        slot = plan[OWN_RIGHT + 2 + 5 * j + 4]
        dst = pl.multiple_of((plan[OWN_RIGHT + 1] + 8 * j) * 8, 8)
        for c in range(2):
            src = pl.multiple_of(depth * HALF + 64 * c, 64)
            ahead[c, pl.ds(dst, 64), :] = measured[slot, pl.ds(src, 64), :]
        return carry

    lax.fori_loop(0, plan[OWN_RIGHT], right_job, 0)

    def left_job(j, carry):
        copy_rows(behind, PREV_LEFT, j, 0, lax.div(plan[PREV_LEFT + 2 + 5 * j] + 7, 8))
        return carry

    lax.fori_loop(0, plan[PREV_LEFT], left_job, 0)


def exchange_kernel(
    n_lat, ahead, behind, tile, received, other,
    row_send, row_recv, tile_send, tile_recv,
):
    depth = lax.axis_index("depth")
    lat = lax.axis_index("lat")
    after = lax.rem(lat + 1, n_lat)
    before = lax.rem(lat + n_lat - 1, n_lat)
    greet(depth, lat, after, before)
    pl.semaphore_wait(pltpu.get_barrier_semaphore(), 4)

    def slot(s):
        return received.at[s, :, pl.ds(PAD, ROWS), :]

    sends = [
        remote(ahead, slot(depth), row_send.at[0], row_recv.at[depth], 1, after),
        remote(behind, slot(depth), row_send.at[1], row_recv.at[depth], 0, before),
    ]
    for copy in sends:
        copy.start()
    swap = remote(tile, other, tile_send, tile_recv, 1 - depth, lat)
    swap.start()
    for copy in sends:
        copy.wait_send()
    for s in range(2):
        remote(ahead, slot(s), row_send.at[0], row_recv.at[s], 1, after).wait_recv()
    swap.wait()


def remote(src, dst, send, recv, depth, lat):
    return pltpu.make_async_remote_copy(
        src_ref=src,
        dst_ref=dst,
        send_sem=send,
        recv_sem=recv,
        device_id=(depth, lat),
        device_id_type=pl.DeviceIdType.MESH,
    )


def greet(depth, lat, after, before):
    barrier = pltpu.get_barrier_semaphore()
    partners = [
        (depth, after),
        (depth, before),
        (1 - depth, jnp.where(depth == 0, after, before)),
        (1 - depth, lat),
    ]
    for partner in partners:
        pl.semaphore_signal(
            barrier, inc=1, device_id=partner, device_id_type=pl.DeviceIdType.MESH
        )


def return_kernel(
    n_lat, rows, windows, received, partner,
    row_send, row_recv, swap_send, swap_recv,
):
    depth = lax.axis_index("depth")
    lat = lax.axis_index("lat")
    after = lax.rem(lat + 1, n_lat)
    before = lax.rem(lat + n_lat - 1, n_lat)
    greet(depth, lat, after, before)
    pl.semaphore_wait(pltpu.get_barrier_semaphore(), 4)
    target = jnp.where(depth == 0, after, before)
    sends = [
        remote(rows.at[s], received.at[depth], row_send.at[s], row_recv.at[depth], s, target)
        for s in range(2)
    ]
    for copy in sends:
        copy.start()
    swap = remote(windows.at[1 - depth], partner, swap_send, swap_recv, 1 - depth, lat)
    swap.start()
    for copy in sends:
        copy.wait_send()
    for c in range(2):
        remote(
            rows.at[0], received.at[c], row_send.at[0], row_recv.at[c], 0, target
        ).wait_recv()
    swap.wait()


P_PLUS, P_MINUS, F_EVEN, F_ODD = 0, 1, 2, 3
TURNED = 4


def halves(x):
    hi = x.astype(jnp.bfloat16)
    lo = (x - hi.astype(jnp.float32)).astype(jnp.bfloat16)
    return hi, lo


def dot(a, b):
    return jnp.dot(a, b, preferred_element_type=jnp.float32)


def times_right(x, table, at):
    hi, lo = halves(x)
    return dot(
        jnp.concatenate([hi, lo, hi], axis=1),
        jnp.concatenate([table[at, 0], table[at, 0], table[at, 1]], axis=0),
    )


def times_left(table, at, x):
    hi, lo = halves(x)
    return dot(
        jnp.concatenate([table[at, 0], table[at, 0], table[at, 1]], axis=1),
        jnp.concatenate([hi, lo, hi], axis=0),
    )


def fold_columns(re, im):
    plus = jnp.concatenate([re[:, :HALF] + re[:, HALF:], im[:, :HALF] + im[:, HALF:]], axis=1)
    minus = jnp.concatenate([re[:, :HALF] - re[:, HALF:], im[:, :HALF] - im[:, HALF:]], axis=1)
    return plus, minus


def pair_columns(re, im):
    return (
        jnp.concatenate([re[:, :HALF], im[:, :HALF]], axis=1),
        jnp.concatenate([re[:, HALF:], im[:, HALF:]], axis=1),
    )


def fold_rows(re, im):
    plus = jnp.concatenate([re[:HALF] + re[HALF:], im[:HALF] + im[HALF:]], axis=0)
    minus = jnp.concatenate([re[:HALF] - re[HALF:], im[:HALF] - im[HALF:]], axis=0)
    return plus, minus


def pair_rows(re, im):
    return (
        jnp.concatenate([re[:HALF], im[:HALF]], axis=0),
        jnp.concatenate([re[HALF:], im[HALF:]], axis=0),
    )


def product(u, v):
    return u[0] * v[0] - u[1] * v[1], u[0] * v[1] + u[1] * v[0]


def conj_product(u, v):
    return u[0] * v[0] + u[1] * v[1], u[0] * v[1] - u[1] * v[0]


def both_right(pairs, table, first, second):
    return [(times_right(p, table, first), times_right(m, table, second)) for p, m in pairs]


def both_left(pairs, table, first, second):
    return [(times_left(table, first, p), times_left(table, second, m)) for p, m in pairs]


def unfold(pairs):
    return [(p + m, p - m) for p, m in pairs]


def propagate(fields, table, adjoint):
    left, right = (TURNED, 0) if adjoint else (0, TURNED)
    pairs = [fold_columns(*f) for f in fields]
    pairs = unfold(both_right(pairs, table, right + P_PLUS, right + P_MINUS))
    pairs = [fold_rows(*pair_columns(*p)) for p in pairs]
    pairs = unfold(both_left(pairs, table, left + P_PLUS, left + P_MINUS))
    return [pair_rows(*p) for p in pairs]


def to_spectrum(fields, table):
    pairs = [fold_columns(*f) for f in fields]
    pairs = both_right(pairs, table, TURNED + F_EVEN, TURNED + F_ODD)
    pairs = [fold_rows(*pair_columns(*p)) for p in pairs]
    pairs = both_left(pairs, table, F_EVEN, F_ODD)
    return [pair_rows(*p) for p in pairs]


def from_spectrum(fields, table):
    pairs = [pair_columns(*f) for f in fields]
    pairs = unfold(both_right(pairs, table, F_EVEN, F_ODD))
    pairs = [pair_rows(*pair_columns(*p)) for p in pairs]
    pairs = unfold(both_left(pairs, table, TURNED + F_EVEN, TURNED + F_ODD))
    return [pair_rows(*p) for p in pairs]


def compute_kernel(
    plan, tile, other, received, measured, probe, table,
    rows_out, grads,
    amplitude, spread,
):
    depth = lax.axis_index("depth")
    at = jnp.where(depth == 0, OWN_LEFT, PREV_RIGHT)
    jobs = plan[at]
    row = lax.broadcasted_iota(jnp.int32, (N, N), 0)
    lane = lax.broadcasted_iota(jnp.int32, (N, N), 1)
    order = jnp.where(lane < HALF, 2 * lane, 2 * lane - (N - 1))
    shuffle = jnp.where(row == order, 1.0, 0.0).astype(jnp.bfloat16)

    def work(numbers):
        each = range(len(numbers))
        words = [[plan[at + 2 + 5 * j + w] for w in range(5)] for j in numbers]

        for k in each:
            _, _, _, _, slot = words[k]

            @pl.when(depth == 0)
            def _(k=k, slot=slot):
                amplitude[k] = measured[slot]

            @pl.when(depth == 1)
            def _(k=k):
                src = pl.multiple_of(PAD + (plan[PREV_RIGHT + 1] + 8 * numbers[k]) * 8, 8)
                for s in range(2):
                    for c in range(2):
                        amplitude[k, pl.ds(128 * s + 64 * c, 64), :] = received[
                            s, c, pl.ds(src, 64), :
                        ]

        def base_of(k):
            return jnp.where(depth == 0, 0, lax.div(words[k][0], 8))

        def window(k, s):
            r, block, shift, start, _ = words[k]
            here = (row >= jnp.where(depth == 0, r, 0)) & (row < jnp.where(depth == 0, N, r))
            keep = lane >= shift
            src = pl.multiple_of(PAD + (start - base_of(k)) * 8, 8)
            column = pl.multiple_of(block * N, N)
            left, right = pl.ds(column, N), pl.ds(pl.multiple_of(column + N, N), N)
            near = depth == s
            return [
                jnp.where(
                    here,
                    jnp.where(
                        keep,
                        jnp.where(near, tile[c, :, left], other[c, :, left]),
                        jnp.where(near, tile[c, :, right], other[c, :, right]),
                    ),
                    received[s, c, pl.ds(src, N), :],
                )
                for c in range(2)
            ]

        def rolled(k):
            r, _, shift, _, _ = words[k]
            return [
                pltpu.roll(pltpu.roll(probe[c], r, 0), jnp.where(shift == N, 0, shift), 1)
                for c in range(2)
            ]

        probes = [rolled(k) for k in each]
        waves = [product(p, window(k, 0)) for k, p in enumerate(probes)]
        waves = propagate(waves, table, False)
        slices = [window(k, 1) for k in each]
        spectra = to_spectrum([product(w, o) for w, o in zip(waves, slices)], table)
        backs = []
        for k in each:
            hi, lo = halves(amplitude[k])
            apart = dot(
                jnp.concatenate([hi, lo], axis=1), jnp.concatenate([shuffle, shuffle], axis=0)
            )
            for h in range(2):
                spread[k, h] = apart[:, HALF * h : HALF * h + HALF]
        for k in each:
            apart = jnp.concatenate(
                [
                    jnp.concatenate(
                        [spread[k, h, pl.ds(p, HALF, stride=2), :] for h in range(2)], axis=1
                    )
                    for p in range(2)
                ],
                axis=0,
            )
            re, im = spectra[k]
            factor = 1.0 - apart * lax.rsqrt(re * re + im * im + 1.0)
            backs.append((re * factor, im * factor))
        backs = from_spectrum(backs, table)
        for k in each:
            grads[1, numbers[k], 0], grads[1, numbers[k], 1] = conj_product(waves[k], backs[k])
        backs = [conj_product(o, b) for o, b in zip(slices, backs)]
        backs = propagate(backs, table, True)
        for k in each:
            grads[0, numbers[k], 0], grads[0, numbers[k], 1] = conj_product(probes[k], backs[k])
        for k in each:
            r, start = words[k][0], words[k][3]
            base = base_of(k)
            count = jnp.where(depth == 0, lax.div(r + 7, 8), 32 - lax.div(r, 8))

            def step(g, carry, k=k, base=base, start=start):
                src = pl.multiple_of((base + g) * 8, 8)
                dst = pl.multiple_of((start + g) * 8, 8)
                for s in range(2):
                    for c in range(2):
                        rows_out[s, c, pl.ds(dst, 8), :] = grads[
                            s, numbers[k], c, pl.ds(src, 8), :
                        ]
                return carry

            lax.fori_loop(0, count, step, 0)

    @pl.when(jobs >= 2)
    def _():
        work([0, 1])

    @pl.when(lax.rem(jobs, 2) == 1)
    def _():
        work([jobs - 1])


def gather_kernel(plan, rows, partner, grads, out, tile, out_sems):
    depth = lax.axis_index("depth")

    def clear(i, carry):
        at = pl.multiple_of(i * 8, 8)
        for c in range(2):
            tile[c, pl.ds(at, 8), :] = jnp.zeros((8, tile.shape[2]), jnp.float32)
        return carry

    lax.fori_loop(0, N // 8, clear, 0)
    row = lax.broadcasted_iota(jnp.int32, (8, N), 0)

    def add(at, j, c, lower, packed, near):
        r = plan[at + 2 + 5 * j]
        block = plan[at + 2 + 5 * j + 1]
        start = plan[at + 2 + 5 * j + 3]
        first = 0 if lower else lax.div(r, 8)
        last = lax.div(r + 7, 8) if lower else 32
        keep = lanes() >= plan[at + 2 + 5 * j + 2]
        low = pl.multiple_of(block * N, N)
        high = pl.multiple_of(block * N + N, N)

        def step(g, carry):
            dst = pl.multiple_of(g * 8, 8)
            inside = (row + dst < r) if lower else (row + dst >= r)
            if packed:
                src = pl.multiple_of((start + g - first) * 8, 8)
                value = rows[0 if lower else 1, c, pl.ds(src, 8), :]
            else:
                value = grads[depth, j, c, pl.ds(dst, 8), :] if near else partner[j, c, pl.ds(dst, 8), :]
            value = jnp.where(inside, value, 0.0)
            tile[c, pl.ds(dst, 8), pl.ds(low, N)] += jnp.where(keep, value, 0.0)
            tile[c, pl.ds(dst, 8), pl.ds(high, N)] += jnp.where(keep, 0.0, value)
            return carry

        lax.fori_loop(first, last, step, 0)

    def run(at, c, lower, packed, near):
        def step(j, carry):
            add(at, j, c, lower, packed, near)
            return carry

        lax.fori_loop(0, plan[at], step, 0)

    for c in range(2):

        @pl.when(depth == 0)
        def _(c=c):
            run(OWN_LEFT, c, False, False, True)
            run(PREV_RIGHT, c, True, False, False)

        @pl.when(depth == 1)
        def _(c=c):
            run(OWN_LEFT, c, False, False, False)
            run(PREV_RIGHT, c, True, False, True)

        run(OWN_RIGHT, c, False, True, False)
        run(PREV_LEFT, c, True, True, False)
        pltpu.make_async_copy(tile.at[c], out.at[c], out_sems.at[c]).start()
    for c in range(2):
        pltpu.make_async_copy(tile.at[c], out.at[c], out_sems.at[c]).wait()


SMEM = pl.BlockSpec(memory_space=pltpu.SMEM)
VMEM = pl.BlockSpec(memory_space=pltpu.VMEM)
HBM = pl.BlockSpec(memory_space=pltpu.HBM)


def shape(*dims):
    return jax.ShapeDtypeStruct(dims, jnp.float32)


def shards(n_lat, object_slices, probe, measured, positions, counts):
    columns = object_slices.shape[3]
    tile = object_slices.reshape(object_slices.shape[1:])
    dma = pltpu.SemaphoreType.DMA
    positions = positions.T
    prev_positions, prev_counts = pl.pallas_call(
        functools.partial(announce_kernel, n_lat),
        name="announce",
        out_shape=(
            jax.ShapeDtypeStruct(positions.shape, jnp.int32),
            jax.ShapeDtypeStruct(counts.shape, jnp.int32),
        ),
        in_specs=[HBM, HBM],
        out_specs=(HBM, HBM),
        scratch_shapes=[dma((2,)), dma((2,))],
        compiler_params=pltpu.CompilerParams(collective_id=2, has_side_effects=True),
    )(positions, counts)
    plan, ahead, behind = pl.pallas_call(
        pack_kernel,
        name="pack",
        out_shape=(
            jax.ShapeDtypeStruct((4 * SPAN,), jnp.int32),
            shape(2, ROWS, N),
            shape(2, ROWS, N),
        ),
        in_specs=[HBM, SMEM, HBM, SMEM, HBM, HBM],
        out_specs=(SMEM, VMEM, VMEM),
        scratch_shapes=[
            pltpu.VMEM((2, N, columns), jnp.float32),
            pltpu.VMEM((4, N, N), jnp.float32),
            pltpu.SMEM((2, 4), jnp.int32),
            pltpu.SMEM((2, 4), jnp.int32),
            dma((4,)),
        ],
        compiler_params=pltpu.CompilerParams(vmem_limit_bytes=51 << 20),
    )(positions, counts, prev_positions, prev_counts, tile, measured)
    received, other = pl.pallas_call(
        functools.partial(exchange_kernel, n_lat),
        name="exchange",
        out_shape=(shape(2, 2, ROWS + 2 * PAD, N), shape(2, N, columns)),
        in_specs=[VMEM, VMEM, HBM],
        out_specs=(VMEM, VMEM),
        scratch_shapes=[dma((2,)), dma((2,)), dma, dma],
        compiler_params=pltpu.CompilerParams(
            collective_id=0, has_side_effects=True, vmem_limit_bytes=12 << 20
        ),
    )(ahead, behind, tile)

    table = jnp.asarray(tables())
    rows_out, grads = pl.pallas_call(
        compute_kernel,
        name="compute",
        out_shape=(shape(2, 2, ROWS, N), shape(2, MAX_JOBS, 2, N, N)),
        in_specs=[SMEM, VMEM, VMEM, VMEM, VMEM, VMEM, VMEM],
        out_specs=(VMEM, VMEM),
        scratch_shapes=[
            pltpu.VMEM((2, N, N), jnp.float32),
            pltpu.VMEM((2, 2, N, HALF), jnp.float32),
        ],
        compiler_params=pltpu.CompilerParams(vmem_limit_bytes=30 << 20),
    )(plan, tile, other, received, measured, probe, table)

    rows_back, partner = pl.pallas_call(
        functools.partial(return_kernel, n_lat),
        name="giveback",
        out_shape=(shape(2, 2, ROWS, N), shape(MAX_JOBS, 2, N, N)),
        in_specs=[VMEM, VMEM],
        out_specs=(VMEM, VMEM),
        scratch_shapes=[dma((2,)), dma((2,)), dma, dma],
        compiler_params=pltpu.CompilerParams(
            collective_id=1, has_side_effects=True, vmem_limit_bytes=12 << 20
        ),
    )(rows_out, grads)

    out = pl.pallas_call(
        gather_kernel,
        name="gather",
        out_shape=shape(2, N, columns),
        in_specs=[SMEM, VMEM, VMEM, VMEM],
        out_specs=HBM,
        scratch_shapes=[pltpu.VMEM((2, N, columns), jnp.float32), dma((2,))],
        compiler_params=pltpu.CompilerParams(vmem_limit_bytes=20 << 20),
    )(plan, rows_back, partner, grads)
    return out.reshape(object_slices.shape)


def solution(mesh):
    return jax.shard_map(
        functools.partial(shards, mesh.shape["lat"]),
        mesh=mesh,
        in_specs=(
            P("depth", None, "lat", None),
            P(),
            P("lat", None, None),
            P("lat", None),
            P("lat"),
        ),
        out_specs=P("depth", None, "lat", None),
        check_vma=False,
    )
```

```python
import functools

import jax
import jax.numpy as jnp
import ml_dtypes
import numpy as np
from jax import lax
from jax.experimental import pallas as pl
from jax.experimental.pallas import tpu as pltpu
from jax.sharding import PartitionSpec as P

N = 256
HALF = 128
STRENGTH = 8.0
MAX_JOBS = 3
BUDGET = 48
ROWS = 8 * BUDGET
PAD = 256
CHUNK = 32
EASY = 30
RETURN_BUDGETS = tuple(range(30, 49, 3))
RETURN_BUDGETS = (32, 36, 40, 44, 48)
SPAN = 20


def split_bf16(a):
    hi = a.astype(np.float32).astype(ml_dtypes.bfloat16)
    lo = (a - hi.astype(np.float64)).astype(np.float32).astype(ml_dtypes.bfloat16)
    return hi, lo


def tables():
    index = np.arange(N)
    angle = 2.0 * np.pi * ((index[:, None] * index[None, :]) % N) / N
    dft = np.exp(-1j * angle) / 16.0
    centred = (index - N * (index >= HALF)) / N
    turn = np.exp(1j * np.pi * STRENGTH * centred**2)
    prop = np.conj(dft) @ (turn[:, None] * dft)
    c0, c1 = prop[:HALF, :HALF], prop[:HALF, HALF:]

    def real_form(m):
        return np.block([[m.real, -m.imag], [m.imag, m.real]])

    forms = [real_form(m) for m in ((c0 + c1) / 2, (c0 - c1) / 2, dft[0::2, :HALF], dft[1::2, :HALF])]
    forms = forms + [m.T for m in forms]
    return np.stack([np.stack(split_bf16(m)) for m in forms])


OWN_LEFT, OWN_RIGHT, PREV_LEFT, PREV_RIGHT = 0, SPAN, 2 * SPAN, 3 * SPAN


def choose_sides(rows_of, cols_of, live):
    up = [lax.div(rows_of[i] + 7, 8) for i in range(4)]
    down = [32 - lax.div(rows_of[i], 8) for i in range(4)]
    best = jnp.int32(1 << 20)
    pick = jnp.int32(0)
    for mask in range(16):
        right = [(mask >> i) & 1 for i in range(4)]
        n_right = sum(right)
        if n_right > MAX_JOBS:
            continue
        top = max([i + 1 for i in range(4) if right[i]], default=0)
        lefts = [jnp.where(live > i, up[i], 0) for i in range(4) if not right[i]]
        cost_left = sum(lefts, jnp.int32(0))
        cost_right = sum([down[i] + 8 for i in range(4) if right[i]], jnp.int32(0))
        widest = jnp.maximum(cost_left, cost_right)
        back = jnp.maximum(cost_left, cost_right - 8 * n_right)
        most = jnp.maximum(live - n_right, n_right)
        bad = (live < top) | (widest > BUDGET) | (most > MAX_JOBS)
        key = jnp.maximum(back, EASY) * 8 + most + jnp.where(bad, jnp.int32(1 << 16), 0)
        pick = jnp.where(key < best, mask, pick)
        best = jnp.minimum(key, best)
    blocks = [jnp.minimum(lax.div(cols_of[i], N), 6) for i in range(4)]
    sides = []
    for side in range(2):
        mine = [(live > i) & ((lax.shift_right_logical(pick, i) & 1) == side) for i in range(4)]
        size = up if side == 0 else down
        count, total = jnp.int32(0), jnp.int32(0)
        words = [[jnp.int32(0)] * 5 for _ in range(MAX_JOBS)]
        for i in range(4):
            fields = [rows_of[i], blocks[i], cols_of[i] - blocks[i] * N, total, jnp.int32(i)]
            for j in range(MAX_JOBS):
                here = mine[i] & (count == j)
                words[j] = [jnp.where(here, f, w) for f, w in zip(fields, words[j])]
            count = count + jnp.where(mine[i], 1, 0)
            total = total + jnp.where(mine[i], size[i], 0)
        sides.append([count, total] + [w for job in words for w in job])
    return sides


def lanes():
    return lax.broadcasted_iota(jnp.int32, (8, N), 1)


def announce_kernel(n_lat, pos, cnt, prev_pos, prev_cnt, send, recv):
    depth = lax.axis_index("depth")
    lat = lax.axis_index("lat")
    after = lax.rem(lat + 1, n_lat)
    before = lax.rem(lat + n_lat - 1, n_lat)
    barrier = pltpu.get_barrier_semaphore()
    for other in (after, before):
        pl.semaphore_signal(
            barrier, inc=1, device_id=(depth, other), device_id_type=pl.DeviceIdType.MESH
        )
    pl.semaphore_wait(barrier, 2)
    copies = [
        remote(pos, prev_pos, send.at[0], recv.at[0], depth, after),
        remote(cnt, prev_cnt, send.at[1], recv.at[1], depth, after),
    ]
    for copy in copies:
        copy.start()
    for copy in copies:
        copy.wait()


def pack_kernel(
    pos_hbm, cnt, prev_pos_hbm, prev_cnt, tile_hbm, measured_hbm, plan, packed, need,
    tile, measured, pos, prev_pos, sems,
):
    depth = lax.axis_index("depth")
    loads = [
        pltpu.make_async_copy(pos_hbm, pos, sems.at[0]),
        pltpu.make_async_copy(prev_pos_hbm, prev_pos, sems.at[1]),
        pltpu.make_async_copy(tile_hbm, tile, sems.at[2]),
        pltpu.make_async_copy(measured_hbm, measured, sems.at[3]),
    ]
    for load in loads:
        load.start()
    for load in loads[:2]:
        load.wait()
    own = choose_sides([pos[0, i] for i in range(4)], [pos[1, i] for i in range(4)], cnt[0])
    prev = choose_sides(
        [prev_pos[0, i] for i in range(4)], [prev_pos[1, i] for i in range(4)], prev_cnt[0]
    )
    for k, side in enumerate(own + prev):
        for w, word in enumerate(side):
            plan[k * SPAN + w] = word
    need[...] = jnp.full(need.shape, jnp.maximum(own[0][1], own[1][1]), jnp.int32)
    for load in loads[2:]:
        load.wait()

    def copy_rows(way, at, j, first, count):
        start = plan[at + 2 + 5 * j + 3]
        low = pl.multiple_of(plan[at + 2 + 5 * j + 1] * N, N)
        high = pl.multiple_of(plan[at + 2 + 5 * j + 1] * N + N, N)
        keep = lanes() >= plan[at + 2 + 5 * j + 2]

        def step(g, carry):
            for k in range(4):
                at_row = jnp.minimum(4 * g + k, count - 1)
                src = pl.multiple_of((first + at_row) * 8, 8)
                dst = pl.multiple_of((start + at_row) * 8, 8)
                for c in range(2):
                    packed[way, c, pl.ds(dst, 8), :] = jnp.where(
                        keep,
                        tile[c, pl.ds(src, 8), pl.ds(low, N)],
                        tile[c, pl.ds(src, 8), pl.ds(high, N)],
                    )
            return carry

        lax.fori_loop(0, lax.div(count + 3, 4), step, 0)

    def right_job(j, carry):
        first = lax.div(plan[OWN_RIGHT + 2 + 5 * j], 8)
        copy_rows(0, OWN_RIGHT, j, first, 32 - first)
        slot = plan[OWN_RIGHT + 2 + 5 * j + 4]
        dst = pl.multiple_of((plan[OWN_RIGHT + 1] + 8 * j) * 8, 8)
        for c in range(2):
            src = pl.multiple_of(depth * HALF + 64 * c, 64)
            packed[0, c, pl.ds(dst, 64), :] = measured[slot, pl.ds(src, 64), :]
        return carry

    lax.fori_loop(0, plan[OWN_RIGHT], right_job, 0)

    def left_job(j, carry):
        copy_rows(1, PREV_LEFT, j, 0, lax.div(plan[PREV_LEFT + 2 + 5 * j] + 7, 8))
        return carry

    lax.fori_loop(0, plan[PREV_LEFT], left_job, 0)


def exchange_kernel(
    n_lat, packed, tile, need, received, other, bucket,
    mine, theirs, row_send, row_recv, tile_send, tile_recv, need_send, need_recv,
):
    depth = lax.axis_index("depth")
    lat = lax.axis_index("lat")
    after = lax.rem(lat + 1, n_lat)
    before = lax.rem(lat + n_lat - 1, n_lat)
    greet(depth, lat, after, before)
    barrier = pltpu.get_barrier_semaphore()
    rings = []
    for unit in (1, 4, 16):
        digit = lax.rem(lax.div(lat, unit), 4)
        rings.append([lat + (lax.rem(digit + k, 4) - digit) * unit for k in range(1, 4)])
    for ring in rings:
        for mate in ring:
            pl.semaphore_signal(
                barrier, inc=1, device_id=(depth, mate), device_id_type=pl.DeviceIdType.MESH
            )
    pl.semaphore_wait(barrier, 13)

    def slot(s):
        return received.at[s, :, pl.ds(PAD, ROWS), :]

    def tell(turn):
        copies = [
            remote(
                mine.at[turn], theirs.at[turn, k], need_send.at[turn, k], need_recv.at[turn, k],
                depth, mate,
            )
            for k, mate in enumerate(rings[turn])
        ]
        for copy in copies:
            copy.start()
        return copies

    mine[0] = need[...]
    told = tell(0)
    sends = [
        remote(packed.at[0], slot(depth), row_send.at[0], row_recv.at[depth], 1, after),
        remote(packed.at[1], slot(depth), row_send.at[1], row_recv.at[depth], 0, before),
    ]
    for copy in sends:
        copy.start()
    swap = remote(tile, other, tile_send, tile_recv, 1 - depth, lat)
    swap.start()
    for turn in range(3):
        for copy in told:
            copy.wait()
        top = mine[turn]
        for k in range(3):
            top = jnp.maximum(top, theirs[turn, k])
        if turn < 2:
            mine[turn + 1] = top
            told = tell(turn + 1)
    place = jnp.zeros_like(top)
    for budget in RETURN_BUDGETS[:-1]:
        place = place + jnp.where(top > budget, 1, 0)
    bucket[...] = place
    for copy in sends:
        copy.wait_send()
    for s in range(2):
        remote(packed.at[0], slot(s), row_send.at[0], row_recv.at[s], 1, after).wait_recv()
    swap.wait()


def remote(src, dst, send, recv, depth, lat):
    return pltpu.make_async_remote_copy(
        src_ref=src,
        dst_ref=dst,
        send_sem=send,
        recv_sem=recv,
        device_id=(depth, lat),
        device_id_type=pl.DeviceIdType.MESH,
    )


def greet(depth, lat, after, before):
    barrier = pltpu.get_barrier_semaphore()
    partners = [
        (depth, after),
        (depth, before),
        (1 - depth, jnp.where(depth == 0, after, before)),
        (1 - depth, lat),
    ]
    for partner in partners:
        pl.semaphore_signal(
            barrier, inc=1, device_id=partner, device_id_type=pl.DeviceIdType.MESH
        )


def return_kernel(
    n_lat, count, rows, windows, received, partner,
    row_send, row_recv, swap_send, swap_recv,
):
    depth = lax.axis_index("depth")
    lat = lax.axis_index("lat")
    after = lax.rem(lat + 1, n_lat)
    before = lax.rem(lat + n_lat - 1, n_lat)
    greet(depth, lat, after, before)
    pl.semaphore_wait(pltpu.get_barrier_semaphore(), 4)
    target = jnp.where(depth == 0, after, before)

    def part(c):
        return received.at[c, :, pl.ds(CHUNK, count), :]

    def sent(s):
        return rows.at[s, :, pl.ds(0, count), :]

    sends = [
        remote(sent(s), part(depth), row_send.at[s], row_recv.at[depth], s, target)
        for s in range(2)
    ]
    for copy in sends:
        copy.start()
    swap = remote(windows.at[1 - depth], partner, swap_send, swap_recv, 1 - depth, lat)
    swap.start()
    for copy in sends:
        copy.wait_send()
    for c in range(2):
        remote(
            sent(0), part(c), row_send.at[0], row_recv.at[c], 0, target
        ).wait_recv()
    swap.wait()


P_PLUS, P_MINUS, F_EVEN, F_ODD = 0, 1, 2, 3
TURNED = 4


def halves(x):
    hi = x.astype(jnp.bfloat16)
    lo = (x - hi.astype(jnp.float32)).astype(jnp.bfloat16)
    return hi, lo


def dot(a, b):
    return jnp.dot(a, b, preferred_element_type=jnp.float32)


def times_right(x, table, at):
    hi, lo = halves(x)
    return dot(
        jnp.concatenate([hi, lo, hi], axis=1),
        jnp.concatenate([table[at, 0], table[at, 0], table[at, 1]], axis=0),
    )


def times_left(table, at, x):
    hi, lo = halves(x)
    return dot(
        jnp.concatenate([table[at, 0], table[at, 0], table[at, 1]], axis=1),
        jnp.concatenate([hi, lo, hi], axis=0),
    )


def fold_columns(re, im):
    plus = jnp.concatenate([re[:, :HALF] + re[:, HALF:], im[:, :HALF] + im[:, HALF:]], axis=1)
    minus = jnp.concatenate([re[:, :HALF] - re[:, HALF:], im[:, :HALF] - im[:, HALF:]], axis=1)
    return plus, minus


def pair_columns(re, im):
    return (
        jnp.concatenate([re[:, :HALF], im[:, :HALF]], axis=1),
        jnp.concatenate([re[:, HALF:], im[:, HALF:]], axis=1),
    )


def fold_rows(re, im):
    plus = jnp.concatenate([re[:HALF] + re[HALF:], im[:HALF] + im[HALF:]], axis=0)
    minus = jnp.concatenate([re[:HALF] - re[HALF:], im[:HALF] - im[HALF:]], axis=0)
    return plus, minus


def pair_rows(re, im):
    return (
        jnp.concatenate([re[:HALF], im[:HALF]], axis=0),
        jnp.concatenate([re[HALF:], im[HALF:]], axis=0),
    )


def product(u, v):
    return u[0] * v[0] - u[1] * v[1], u[0] * v[1] + u[1] * v[0]


def conj_product(u, v):
    return u[0] * v[0] + u[1] * v[1], u[0] * v[1] - u[1] * v[0]


def both_right(pairs, table, first, second):
    return [(times_right(p, table, first), times_right(m, table, second)) for p, m in pairs]


def both_left(pairs, table, first, second):
    return [(times_left(table, first, p), times_left(table, second, m)) for p, m in pairs]


def unfold(pairs):
    return [(p + m, p - m) for p, m in pairs]


def propagate(fields, table, adjoint):
    left, right = (TURNED, 0) if adjoint else (0, TURNED)
    pairs = [fold_columns(*f) for f in fields]
    pairs = unfold(both_right(pairs, table, right + P_PLUS, right + P_MINUS))
    pairs = [fold_rows(*pair_columns(*p)) for p in pairs]
    pairs = unfold(both_left(pairs, table, left + P_PLUS, left + P_MINUS))
    return [pair_rows(*p) for p in pairs]


def to_spectrum(fields, table):
    pairs = [fold_columns(*f) for f in fields]
    pairs = both_right(pairs, table, TURNED + F_EVEN, TURNED + F_ODD)
    pairs = [fold_rows(*pair_columns(*p)) for p in pairs]
    pairs = both_left(pairs, table, F_EVEN, F_ODD)
    return [pair_rows(*p) for p in pairs]


def from_spectrum(fields, table):
    pairs = [pair_columns(*f) for f in fields]
    pairs = unfold(both_right(pairs, table, F_EVEN, F_ODD))
    pairs = [pair_rows(*pair_columns(*p)) for p in pairs]
    pairs = unfold(both_left(pairs, table, TURNED + F_EVEN, TURNED + F_ODD))
    return [pair_rows(*p) for p in pairs]


def compute_kernel(
    plan, bucket, tile, other, received, measured, probe, table,
    rows_out, grads, choice,
    amplitude, spread,
):
    depth = lax.axis_index("depth")
    at = jnp.where(depth == 0, OWN_LEFT, PREV_RIGHT)
    jobs = plan[at]
    choice[0] = bucket[0, 0]
    row = lax.broadcasted_iota(jnp.int32, (N, N), 0)
    lane = lax.broadcasted_iota(jnp.int32, (N, N), 1)
    order = jnp.where(lane < HALF, 2 * lane, 2 * lane - (N - 1))
    shuffle = jnp.where(row == order, 1.0, 0.0).astype(jnp.bfloat16)

    def work(numbers):
        each = range(len(numbers))
        words = [[plan[at + 2 + 5 * j + w] for w in range(5)] for j in numbers]

        for k in each:
            _, _, _, _, slot = words[k]

            @pl.when(depth == 0)
            def _(k=k, slot=slot):
                amplitude[k] = measured[slot]

            @pl.when(depth == 1)
            def _(k=k):
                src = pl.multiple_of(PAD + (plan[PREV_RIGHT + 1] + 8 * numbers[k]) * 8, 8)
                for s in range(2):
                    for c in range(2):
                        amplitude[k, pl.ds(128 * s + 64 * c, 64), :] = received[
                            s, c, pl.ds(src, 64), :
                        ]

        def base_of(k):
            return jnp.where(depth == 0, 0, lax.div(words[k][0], 8))

        def window(k, s):
            r, block, shift, start, _ = words[k]
            here = (row >= jnp.where(depth == 0, r, 0)) & (row < jnp.where(depth == 0, N, r))
            keep = lane >= shift
            src = pl.multiple_of(PAD + (start - base_of(k)) * 8, 8)
            column = pl.multiple_of(block * N, N)
            left, right = pl.ds(column, N), pl.ds(pl.multiple_of(column + N, N), N)
            near = depth == s
            return [
                jnp.where(
                    here,
                    jnp.where(
                        keep,
                        jnp.where(near, tile[c, :, left], other[c, :, left]),
                        jnp.where(near, tile[c, :, right], other[c, :, right]),
                    ),
                    received[s, c, pl.ds(src, N), :],
                )
                for c in range(2)
            ]

        def rolled(k):
            r, _, shift, _, _ = words[k]
            return [
                pltpu.roll(pltpu.roll(probe[c], r, 0), jnp.where(shift == N, 0, shift), 1)
                for c in range(2)
            ]

        probes = [rolled(k) for k in each]
        waves = [product(p, window(k, 0)) for k, p in enumerate(probes)]
        waves = propagate(waves, table, False)
        slices = [window(k, 1) for k in each]
        spectra = to_spectrum([product(w, o) for w, o in zip(waves, slices)], table)
        backs = []
        for k in each:
            hi, lo = halves(amplitude[k])
            apart = dot(
                jnp.concatenate([hi, lo], axis=1), jnp.concatenate([shuffle, shuffle], axis=0)
            )
            for h in range(2):
                spread[k, h] = apart[:, HALF * h : HALF * h + HALF]
        for k in each:
            apart = jnp.concatenate(
                [
                    jnp.concatenate(
                        [spread[k, h, pl.ds(p, HALF, stride=2), :] for h in range(2)], axis=1
                    )
                    for p in range(2)
                ],
                axis=0,
            )
            re, im = spectra[k]
            factor = 1.0 - apart * lax.rsqrt(re * re + im * im + 1.0)
            backs.append((re * factor, im * factor))
        backs = from_spectrum(backs, table)
        for k in each:
            grads[1, numbers[k], 0], grads[1, numbers[k], 1] = conj_product(waves[k], backs[k])
        backs = [conj_product(o, b) for o, b in zip(slices, backs)]
        backs = propagate(backs, table, True)
        for k in each:
            grads[0, numbers[k], 0], grads[0, numbers[k], 1] = conj_product(probes[k], backs[k])
        for k in each:
            r, start = words[k][0], words[k][3]
            base = base_of(k)
            count = jnp.where(depth == 0, lax.div(r + 7, 8), 32 - lax.div(r, 8))

            def step(g, carry, k=k, base=base, start=start, count=count):
                for q in range(2):
                    at_row = jnp.minimum(2 * g + q, count - 1)
                    src = pl.multiple_of((base + at_row) * 8, 8)
                    dst = pl.multiple_of((start + at_row) * 8, 8)
                    for s in range(2):
                        for c in range(2):
                            rows_out[s, c, pl.ds(dst, 8), :] = grads[
                                s, numbers[k], c, pl.ds(src, 8), :
                            ]
                return carry

            lax.fori_loop(0, lax.div(count + 1, 2), step, 0)

    @pl.when(jobs >= 2)
    def _():
        work([0, 1])

    @pl.when(lax.rem(jobs, 2) == 1)
    def _():
        work([jobs - 1])


def gather_kernel(
    plan, rows_hbm, partner_hbm, grads, out, tile, rows, partner, in_sems, out_sems
):
    depth = lax.axis_index("depth")
    loads = [
        pltpu.make_async_copy(rows_hbm, rows, in_sems.at[0]),
        pltpu.make_async_copy(partner_hbm, partner, in_sems.at[1]),
    ]
    for load in loads:
        load.start()

    def clear(i, carry):
        at = pl.multiple_of(i * 8, 8)
        for c in range(2):
            tile[c, pl.ds(at, 8), :] = jnp.zeros((8, tile.shape[2]), jnp.float32)
        return carry

    lax.fori_loop(0, N // 8, clear, 0)
    for load in loads:
        load.wait()
    row = lax.broadcasted_iota(jnp.int32, (CHUNK, N), 0)
    lane = lax.broadcasted_iota(jnp.int32, (CHUNK, N), 1)

    def add(at, j, c, lower, packed, near):
        r = plan[at + 2 + 5 * j]
        block = plan[at + 2 + 5 * j + 1]
        start = plan[at + 2 + 5 * j + 3]
        first = 0 if lower else lax.div(r, CHUNK)
        last = lax.div(r + CHUNK - 1, CHUNK) if lower else N // CHUNK
        skip = 0 if lower else lax.div(r, 8)
        keep = lane >= plan[at + 2 + 5 * j + 2]
        low = pl.multiple_of(block * N, N)
        high = pl.multiple_of(block * N + N, N)

        def step(g, carry):
            dst = pl.multiple_of(g * CHUNK, CHUNK)
            inside = (row + dst < r) if lower else (row + dst >= r)
            if packed:
                src = pl.multiple_of(CHUNK + (start - skip) * 8 + g * CHUNK, 8)
                value = rows[0 if lower else 1, c, pl.ds(src, CHUNK), :]
            elif near:
                value = grads[depth, j, c, pl.ds(dst, CHUNK), :]
            else:
                value = partner[j, c, pl.ds(dst, CHUNK), :]
            value = jnp.where(inside, value, 0.0)
            tile[c, pl.ds(dst, CHUNK), pl.ds(low, N)] += jnp.where(keep, value, 0.0)
            tile[c, pl.ds(dst, CHUNK), pl.ds(high, N)] += jnp.where(keep, 0.0, value)
            return carry

        lax.fori_loop(first, last, step, 0)

    def run(at, c, lower, packed, near):
        def step(j, carry):
            add(at, j, c, lower, packed, near)
            return carry

        lax.fori_loop(0, plan[at], step, 0)

    for c in range(2):

        @pl.when(depth == 0)
        def _(c=c):
            run(OWN_LEFT, c, False, False, True)
            run(PREV_RIGHT, c, True, False, False)

        @pl.when(depth == 1)
        def _(c=c):
            run(OWN_LEFT, c, False, False, False)
            run(PREV_RIGHT, c, True, False, True)

        run(OWN_RIGHT, c, False, True, False)
        run(PREV_LEFT, c, True, True, False)
        pltpu.make_async_copy(tile.at[c], out.at[c], out_sems.at[c]).start()
    for c in range(2):
        pltpu.make_async_copy(tile.at[c], out.at[c], out_sems.at[c]).wait()


SMEM = pl.BlockSpec(memory_space=pltpu.SMEM)
VMEM = pl.BlockSpec(memory_space=pltpu.VMEM)
HBM = pl.BlockSpec(memory_space=pltpu.HBM)


def shape(*dims):
    return jax.ShapeDtypeStruct(dims, jnp.float32)


def shards(n_lat, object_slices, probe, measured, positions, counts):
    columns = object_slices.shape[3]
    tile = object_slices.reshape(object_slices.shape[1:])
    dma = pltpu.SemaphoreType.DMA
    positions = positions.T
    prev_positions, prev_counts = pl.pallas_call(
        functools.partial(announce_kernel, n_lat),
        name="announce",
        out_shape=(
            jax.ShapeDtypeStruct(positions.shape, jnp.int32),
            jax.ShapeDtypeStruct(counts.shape, jnp.int32),
        ),
        in_specs=[HBM, HBM],
        out_specs=(HBM, HBM),
        scratch_shapes=[dma((2,)), dma((2,))],
        compiler_params=pltpu.CompilerParams(collective_id=2, has_side_effects=True),
    )(positions, counts)
    plan, packed, need = pl.pallas_call(
        pack_kernel,
        name="pack",
        out_shape=(
            jax.ShapeDtypeStruct((4 * SPAN,), jnp.int32),
            shape(2, 2, ROWS, N),
            jax.ShapeDtypeStruct((8, 128), jnp.int32),
        ),
        in_specs=[HBM, SMEM, HBM, SMEM, HBM, HBM],
        out_specs=(SMEM, VMEM, VMEM),
        scratch_shapes=[
            pltpu.VMEM((2, N, columns), jnp.float32),
            pltpu.VMEM((4, N, N), jnp.float32),
            pltpu.SMEM((2, 4), jnp.int32),
            pltpu.SMEM((2, 4), jnp.int32),
            dma((4,)),
        ],
        compiler_params=pltpu.CompilerParams(vmem_limit_bytes=51 << 20),
    )(positions, counts, prev_positions, prev_counts, tile, measured)
    received, other, bucket = pl.pallas_call(
        functools.partial(exchange_kernel, n_lat),
        name="exchange",
        out_shape=(
            shape(2, 2, ROWS + 2 * PAD, N),
            shape(2, N, columns),
            jax.ShapeDtypeStruct((8, 128), jnp.int32),
        ),
        in_specs=[VMEM, HBM, VMEM],
        out_specs=(VMEM, VMEM, VMEM),
        scratch_shapes=[
            pltpu.VMEM((3, 8, 128), jnp.int32),
            pltpu.VMEM((3, 3, 8, 128), jnp.int32),
            dma((2,)), dma((2,)), dma, dma, dma((3, 3)), dma((3, 3)),
        ],
        compiler_params=pltpu.CompilerParams(
            collective_id=0, has_side_effects=True, vmem_limit_bytes=12 << 20
        ),
    )(packed, tile, need)

    table = jnp.asarray(tables())
    rows_out, grads, choice = pl.pallas_call(
        compute_kernel,
        name="compute",
        out_shape=(
            shape(2, 2, ROWS, N),
            shape(2, MAX_JOBS, 2, N, N),
            jax.ShapeDtypeStruct((1,), jnp.int32),
        ),
        in_specs=[SMEM, SMEM, VMEM, VMEM, VMEM, VMEM, VMEM, VMEM],
        out_specs=(VMEM, VMEM, SMEM),
        scratch_shapes=[
            pltpu.VMEM((2, N, N), jnp.float32),
            pltpu.VMEM((2, 2, N, HALF), jnp.float32),
        ],
        compiler_params=pltpu.CompilerParams(vmem_limit_bytes=30 << 20),
    )(plan, bucket, tile, other, received, measured, probe, table)

    def give_back(budget):
        return pl.pallas_call(
            functools.partial(return_kernel, n_lat, 8 * budget),
            name="giveback%d" % budget,
            out_shape=(shape(2, 2, ROWS + 2 * CHUNK, N), shape(MAX_JOBS, 2, N, N)),
            in_specs=[VMEM, VMEM],
            out_specs=(VMEM, VMEM),
            scratch_shapes=[dma((2,)), dma((2,)), dma, dma],
            compiler_params=pltpu.CompilerParams(
                collective_id=3 + RETURN_BUDGETS.index(budget),
                has_side_effects=True,
                vmem_limit_bytes=12 << 20,
            ),
        )

    rows_back, partner = lax.switch(
        choice[0], [give_back(b) for b in RETURN_BUDGETS], rows_out, grads
    )

    out = pl.pallas_call(
        gather_kernel,
        name="gather",
        out_shape=shape(2, N, columns),
        in_specs=[SMEM, HBM, HBM, VMEM],
        out_specs=HBM,
        scratch_shapes=[
            pltpu.VMEM((2, N, columns), jnp.float32),
            pltpu.VMEM((2, 2, ROWS + 2 * CHUNK, N), jnp.float32),
            pltpu.VMEM((MAX_JOBS, 2, N, N), jnp.float32),
            dma((2,)), dma((2,)),
        ],
        compiler_params=pltpu.CompilerParams(vmem_limit_bytes=20 << 20),
    )(plan, rows_back, partner, grads)
    return out.reshape(object_slices.shape)


def solution(mesh):
    return jax.shard_map(
        functools.partial(shards, mesh.shape["lat"]),
        mesh=mesh,
        in_specs=(
            P("depth", None, "lat", None),
            P(),
            P("lat", None, None),
            P("lat", None),
            P("lat"),
        ),
        out_specs=P("depth", None, "lat", None),
        check_vma=False,
    )
```

```python
import functools

import jax
import jax.numpy as jnp
import ml_dtypes
import numpy as np
from jax import lax
from jax.experimental import pallas as pl
from jax.experimental.pallas import tpu as pltpu
from jax.sharding import PartitionSpec as P

N = 256
HALF = 128
STRENGTH = 8.0
MAX_JOBS = 3
BUDGET = 48
ROWS = 8 * BUDGET
PAD = 256
SPAN = 20


def split_bf16(a):
    hi = a.astype(np.float32).astype(ml_dtypes.bfloat16)
    lo = (a - hi.astype(np.float64)).astype(np.float32).astype(ml_dtypes.bfloat16)
    return hi, lo


def tables():
    index = np.arange(N)
    angle = 2.0 * np.pi * ((index[:, None] * index[None, :]) % N) / N
    dft = np.exp(-1j * angle) / 16.0
    centred = (index - N * (index >= HALF)) / N
    turn = np.exp(1j * np.pi * STRENGTH * centred**2)
    prop = np.conj(dft) @ (turn[:, None] * dft)
    c0, c1 = prop[:HALF, :HALF], prop[:HALF, HALF:]

    def real_form(m):
        return np.block([[m.real, -m.imag], [m.imag, m.real]])

    forms = [real_form(m) for m in ((c0 + c1) / 2, (c0 - c1) / 2, dft[0::2, :HALF], dft[1::2, :HALF])]
    forms = forms + [m.T for m in forms]
    return np.stack([np.stack(split_bf16(m)) for m in forms])


OWN_LEFT, OWN_RIGHT, PREV_LEFT, PREV_RIGHT = 0, SPAN, 2 * SPAN, 3 * SPAN


def choose_sides(rows_of, cols_of, live):
    up = [lax.div(rows_of[i] + 7, 8) for i in range(4)]
    down = [32 - lax.div(rows_of[i], 8) for i in range(4)]
    best = jnp.int32(1 << 20)
    pick = jnp.int32(0)
    for mask in range(16):
        right = [(mask >> i) & 1 for i in range(4)]
        n_right = sum(right)
        if n_right > MAX_JOBS:
            continue
        top = max([i + 1 for i in range(4) if right[i]], default=0)
        lefts = [jnp.where(live > i, up[i], 0) for i in range(4) if not right[i]]
        cost_left = sum(lefts, jnp.int32(0))
        cost_right = sum([down[i] + 8 for i in range(4) if right[i]], jnp.int32(0))
        widest = jnp.maximum(cost_left, cost_right)
        most = jnp.maximum(live - n_right, n_right)
        bad = (live < top) | (widest > BUDGET) | (most > MAX_JOBS)
        key = most * 64 + widest + jnp.where(bad, jnp.int32(1 << 16), 0)
        pick = jnp.where(key < best, mask, pick)
        best = jnp.minimum(key, best)
    blocks = [jnp.minimum(lax.div(cols_of[i], N), 6) for i in range(4)]
    sides = []
    for side in range(2):
        mine = [(live > i) & ((lax.shift_right_logical(pick, i) & 1) == side) for i in range(4)]
        size = up if side == 0 else down
        count, total = jnp.int32(0), jnp.int32(0)
        words = [[jnp.int32(0)] * 5 for _ in range(MAX_JOBS)]
        for i in range(4):
            fields = [rows_of[i], blocks[i], cols_of[i] - blocks[i] * N, total, jnp.int32(i)]
            for j in range(MAX_JOBS):
                here = mine[i] & (count == j)
                words[j] = [jnp.where(here, f, w) for f, w in zip(fields, words[j])]
            count = count + jnp.where(mine[i], 1, 0)
            total = total + jnp.where(mine[i], size[i], 0)
        sides.append([count, total] + [w for job in words for w in job])
    return sides


def lanes():
    return lax.broadcasted_iota(jnp.int32, (8, N), 1)


def announce_kernel(
    n_lat, pos_hbm, cnt, tile_hbm, measured_hbm,
    pos, prev_pos, prev_cnt, tile, apart,
    measured, spread, send, recv, local,
):
    depth = lax.axis_index("depth")
    lat = lax.axis_index("lat")
    after = lax.rem(lat + 1, n_lat)
    before = lax.rem(lat + n_lat - 1, n_lat)
    barrier = pltpu.get_barrier_semaphore()
    for other in (after, before):
        pl.semaphore_signal(
            barrier, inc=1, device_id=(depth, other), device_id_type=pl.DeviceIdType.MESH
        )
    loads = [
        pltpu.make_async_copy(measured_hbm, measured, local.at[0]),
        pltpu.make_async_copy(tile_hbm, tile, local.at[1]),
        pltpu.make_async_copy(pos_hbm, pos, local.at[2]),
    ]
    for load in loads:
        load.start()
    pl.semaphore_wait(barrier, 2)
    copies = [
        remote(pos_hbm, prev_pos, send.at[0], recv.at[0], depth, after),
        remote(cnt, prev_cnt, send.at[1], recv.at[1], depth, after),
    ]
    for copy in copies:
        copy.start()
    row = lax.broadcasted_iota(jnp.int32, (N, N), 0)
    lane = lax.broadcasted_iota(jnp.int32, (N, N), 1)
    order = jnp.where(lane < HALF, 2 * lane, 2 * lane - (N - 1))
    shuffle = jnp.where(row == order, 1.0, 0.0).astype(jnp.bfloat16)
    loads[0].wait()
    for slot in range(4):
        hi, lo = halves(measured[slot])
        columns = dot(
            jnp.concatenate([hi, lo], axis=1), jnp.concatenate([shuffle, shuffle], axis=0)
        )
        for h in range(2):
            spread[h] = columns[:, HALF * h : HALF * h + HALF]
        for p in range(2):
            for h in range(2):
                apart[slot, HALF * p : HALF * p + HALF, HALF * h : HALF * h + HALF] = spread[
                    h, pl.ds(p, HALF, stride=2), :
                ]
    for load in loads[1:]:
        load.wait()
    for copy in copies:
        copy.wait()


def pack_kernel(
    pos, cnt, prev_pos, prev_cnt, tile, measured, plan, ahead, behind
):
    depth = lax.axis_index("depth")
    own = choose_sides([pos[0, i] for i in range(4)], [pos[1, i] for i in range(4)], cnt[0])
    prev = choose_sides(
        [prev_pos[0, i] for i in range(4)], [prev_pos[1, i] for i in range(4)], prev_cnt[0]
    )
    for k, side in enumerate(own + prev):
        for w, word in enumerate(side):
            plan[k * SPAN + w] = word

    def copy_rows(out, at, j, first, count):
        start = plan[at + 2 + 5 * j + 3]
        low = pl.multiple_of(plan[at + 2 + 5 * j + 1] * N, N)
        high = pl.multiple_of(plan[at + 2 + 5 * j + 1] * N + N, N)
        keep = lanes() >= plan[at + 2 + 5 * j + 2]

        def step(g, carry):
            for k in range(4):
                granule = jnp.minimum(4 * g + k, count - 1)
                src = pl.multiple_of((first + granule) * 8, 8)
                dst = pl.multiple_of((start + granule) * 8, 8)
                for c in range(2):
                    out[c, pl.ds(dst, 8), :] = jnp.where(
                        keep,
                        tile[c, pl.ds(src, 8), pl.ds(low, N)],
                        tile[c, pl.ds(src, 8), pl.ds(high, N)],
                    )
            return carry

        lax.fori_loop(0, lax.div(count + 3, 4), step, 0)

    def right_job(j, carry):
        first = lax.div(plan[OWN_RIGHT + 2 + 5 * j], 8)
        copy_rows(ahead, OWN_RIGHT, j, first, 32 - first)
        slot = plan[OWN_RIGHT + 2 + 5 * j + 4]
        dst = pl.multiple_of((plan[OWN_RIGHT + 1] + 8 * j) * 8, 8)
        for c in range(2):
            src = pl.multiple_of(depth * HALF + 64 * c, 64)
            ahead[c, pl.ds(dst, 64), :] = measured[slot, pl.ds(src, 64), :]
        return carry

    lax.fori_loop(0, plan[OWN_RIGHT], right_job, 0)

    def left_job(j, carry):
        copy_rows(behind, PREV_LEFT, j, 0, lax.div(plan[PREV_LEFT + 2 + 5 * j] + 7, 8))
        return carry

    lax.fori_loop(0, plan[PREV_LEFT], left_job, 0)


def exchange_kernel(
    n_lat, ahead, behind, tile, received, other,
    row_send, row_recv, tile_send, tile_recv,
):
    depth = lax.axis_index("depth")
    lat = lax.axis_index("lat")
    after = lax.rem(lat + 1, n_lat)
    before = lax.rem(lat + n_lat - 1, n_lat)
    greet(depth, lat, after, before)
    pl.semaphore_wait(pltpu.get_barrier_semaphore(), 4)

    def slot(s):
        return received.at[s, :, pl.ds(PAD, ROWS), :]

    sends = [
        remote(ahead, slot(depth), row_send.at[0], row_recv.at[depth], 1, after),
        remote(behind, slot(depth), row_send.at[1], row_recv.at[depth], 0, before),
    ]
    for copy in sends:
        copy.start()
    swap = remote(tile, other, tile_send, tile_recv, 1 - depth, lat)
    swap.start()
    for copy in sends:
        copy.wait_send()
    for s in range(2):
        remote(ahead, slot(s), row_send.at[0], row_recv.at[s], 1, after).wait_recv()
    swap.wait()


def remote(src, dst, send, recv, depth, lat):
    return pltpu.make_async_remote_copy(
        src_ref=src,
        dst_ref=dst,
        send_sem=send,
        recv_sem=recv,
        device_id=(depth, lat),
        device_id_type=pl.DeviceIdType.MESH,
    )


def greet(depth, lat, after, before):
    barrier = pltpu.get_barrier_semaphore()
    partners = [
        (depth, after),
        (depth, before),
        (1 - depth, jnp.where(depth == 0, after, before)),
        (1 - depth, lat),
    ]
    for partner in partners:
        pl.semaphore_signal(
            barrier, inc=1, device_id=partner, device_id_type=pl.DeviceIdType.MESH
        )


def return_kernel(
    n_lat, rows, windows, received, partner,
    row_send, row_recv, swap_send, swap_recv,
):
    depth = lax.axis_index("depth")
    lat = lax.axis_index("lat")
    after = lax.rem(lat + 1, n_lat)
    before = lax.rem(lat + n_lat - 1, n_lat)
    greet(depth, lat, after, before)
    pl.semaphore_wait(pltpu.get_barrier_semaphore(), 4)
    target = jnp.where(depth == 0, after, before)
    sends = [
        remote(rows.at[s], received.at[depth], row_send.at[s], row_recv.at[depth], s, target)
        for s in range(2)
    ]
    for copy in sends:
        copy.start()
    swap = remote(windows.at[1 - depth], partner, swap_send, swap_recv, 1 - depth, lat)
    swap.start()
    for copy in sends:
        copy.wait_send()
    for c in range(2):
        remote(
            rows.at[0], received.at[c], row_send.at[0], row_recv.at[c], 0, target
        ).wait_recv()
    swap.wait()


P_PLUS, P_MINUS, F_EVEN, F_ODD = 0, 1, 2, 3
TURNED = 4


def halves(x):
    hi = x.astype(jnp.bfloat16)
    lo = (x - hi.astype(jnp.float32)).astype(jnp.bfloat16)
    return hi, lo


def dot(a, b):
    return jnp.dot(a, b, preferred_element_type=jnp.float32)


def times_right(x, table, at):
    hi, lo = halves(x)
    return dot(
        jnp.concatenate([hi, lo, hi], axis=1),
        jnp.concatenate([table[at, 0], table[at, 0], table[at, 1]], axis=0),
    )


def times_left(table, at, x):
    hi, lo = halves(x)
    return dot(
        jnp.concatenate([table[at, 0], table[at, 0], table[at, 1]], axis=1),
        jnp.concatenate([hi, lo, hi], axis=0),
    )


def fold_columns(re, im):
    plus = jnp.concatenate([re[:, :HALF] + re[:, HALF:], im[:, :HALF] + im[:, HALF:]], axis=1)
    minus = jnp.concatenate([re[:, :HALF] - re[:, HALF:], im[:, :HALF] - im[:, HALF:]], axis=1)
    return plus, minus


def pair_columns(re, im):
    return (
        jnp.concatenate([re[:, :HALF], im[:, :HALF]], axis=1),
        jnp.concatenate([re[:, HALF:], im[:, HALF:]], axis=1),
    )


def fold_rows(re, im):
    plus = jnp.concatenate([re[:HALF] + re[HALF:], im[:HALF] + im[HALF:]], axis=0)
    minus = jnp.concatenate([re[:HALF] - re[HALF:], im[:HALF] - im[HALF:]], axis=0)
    return plus, minus


def pair_rows(re, im):
    return (
        jnp.concatenate([re[:HALF], im[:HALF]], axis=0),
        jnp.concatenate([re[HALF:], im[HALF:]], axis=0),
    )


def product(u, v):
    return u[0] * v[0] - u[1] * v[1], u[0] * v[1] + u[1] * v[0]


def conj_product(u, v):
    return u[0] * v[0] + u[1] * v[1], u[0] * v[1] - u[1] * v[0]


def both_right(pairs, table, first, second):
    return [(times_right(p, table, first), times_right(m, table, second)) for p, m in pairs]


def both_left(pairs, table, first, second):
    return [(times_left(table, first, p), times_left(table, second, m)) for p, m in pairs]


def unfold(pairs):
    return [(p + m, p - m) for p, m in pairs]


def propagate(fields, table, adjoint):
    left, right = (TURNED, 0) if adjoint else (0, TURNED)
    pairs = [fold_columns(*f) for f in fields]
    pairs = unfold(both_right(pairs, table, right + P_PLUS, right + P_MINUS))
    pairs = [fold_rows(*pair_columns(*p)) for p in pairs]
    pairs = unfold(both_left(pairs, table, left + P_PLUS, left + P_MINUS))
    return [pair_rows(*p) for p in pairs]


def to_spectrum(fields, table):
    pairs = [fold_columns(*f) for f in fields]
    pairs = both_right(pairs, table, TURNED + F_EVEN, TURNED + F_ODD)
    pairs = [fold_rows(*pair_columns(*p)) for p in pairs]
    pairs = both_left(pairs, table, F_EVEN, F_ODD)
    return [pair_rows(*p) for p in pairs]


def from_spectrum(fields, table):
    pairs = [pair_columns(*f) for f in fields]
    pairs = unfold(both_right(pairs, table, F_EVEN, F_ODD))
    pairs = [pair_rows(*pair_columns(*p)) for p in pairs]
    pairs = unfold(both_left(pairs, table, TURNED + F_EVEN, TURNED + F_ODD))
    return [pair_rows(*p) for p in pairs]


def compute_kernel(
    plan, tile, other, received, measured, probe, table,
    rows_out, grads,
    amplitude,
):
    depth = lax.axis_index("depth")
    at = jnp.where(depth == 0, OWN_LEFT, PREV_RIGHT)
    jobs = plan[at]
    row = lax.broadcasted_iota(jnp.int32, (N, N), 0)
    lane = lax.broadcasted_iota(jnp.int32, (N, N), 1)

    def work(numbers):
        each = range(len(numbers))
        words = [[plan[at + 2 + 5 * j + w] for w in range(5)] for j in numbers]

        for k in each:
            _, _, _, _, slot = words[k]

            @pl.when(depth == 0)
            def _(k=k, slot=slot):
                amplitude[k] = measured[slot]

            @pl.when(depth == 1)
            def _(k=k):
                src = pl.multiple_of(PAD + (plan[PREV_RIGHT + 1] + 8 * numbers[k]) * 8, 8)
                for s in range(2):
                    for c in range(2):
                        amplitude[k, pl.ds(128 * s + 64 * c, 64), :] = received[
                            s, c, pl.ds(src, 64), :
                        ]

        def base_of(k):
            return jnp.where(depth == 0, 0, lax.div(words[k][0], 8))

        def window(k, s):
            r, block, shift, start, _ = words[k]
            here = (row >= jnp.where(depth == 0, r, 0)) & (row < jnp.where(depth == 0, N, r))
            keep = lane >= shift
            src = pl.multiple_of(PAD + (start - base_of(k)) * 8, 8)
            column = pl.multiple_of(block * N, N)
            left, right = pl.ds(column, N), pl.ds(pl.multiple_of(column + N, N), N)
            near = depth == s
            return [
                jnp.where(
                    here,
                    jnp.where(
                        keep,
                        jnp.where(near, tile[c, :, left], other[c, :, left]),
                        jnp.where(near, tile[c, :, right], other[c, :, right]),
                    ),
                    received[s, c, pl.ds(src, N), :],
                )
                for c in range(2)
            ]

        def rolled(k):
            r, _, shift, _, _ = words[k]
            return [
                pltpu.roll(pltpu.roll(probe[c], r, 0), jnp.where(shift == N, 0, shift), 1)
                for c in range(2)
            ]

        probes = [rolled(k) for k in each]
        waves = [product(p, window(k, 0)) for k, p in enumerate(probes)]
        waves = propagate(waves, table, False)
        slices = [window(k, 1) for k in each]
        spectra = to_spectrum([product(w, o) for w, o in zip(waves, slices)], table)
        backs = []
        for k in each:
            re, im = spectra[k]
            factor = 1.0 - amplitude[k] * lax.rsqrt(re * re + im * im + 1.0)
            backs.append((re * factor, im * factor))
        backs = from_spectrum(backs, table)
        for k in each:
            grads[1, numbers[k], 0], grads[1, numbers[k], 1] = conj_product(waves[k], backs[k])
        backs = [conj_product(o, b) for o, b in zip(slices, backs)]
        backs = propagate(backs, table, True)
        for k in each:
            grads[0, numbers[k], 0], grads[0, numbers[k], 1] = conj_product(probes[k], backs[k])
        for k in each:
            r, start = words[k][0], words[k][3]
            base = base_of(k)
            count = jnp.where(depth == 0, lax.div(r + 7, 8), 32 - lax.div(r, 8))

            def step(g, carry, k=k, base=base, start=start):
                src = pl.multiple_of((base + g) * 8, 8)
                dst = pl.multiple_of((start + g) * 8, 8)
                for s in range(2):
                    for c in range(2):
                        rows_out[s, c, pl.ds(dst, 8), :] = grads[
                            s, numbers[k], c, pl.ds(src, 8), :
                        ]
                return carry

            lax.fori_loop(0, count, step, 0)

    @pl.when(jobs >= 2)
    def _():
        work([0, 1])

    @pl.when(lax.rem(jobs, 2) == 1)
    def _():
        work([jobs - 1])


def gather_kernel(plan, rows, partner, grads, out, tile, out_sems):
    depth = lax.axis_index("depth")

    def clear(i, carry):
        at = pl.multiple_of(i * 8, 8)
        for c in range(2):
            tile[c, pl.ds(at, 8), :] = jnp.zeros((8, tile.shape[2]), jnp.float32)
        return carry

    lax.fori_loop(0, N // 8, clear, 0)
    row = lax.broadcasted_iota(jnp.int32, (8, N), 0)

    def add(at, j, c, lower, packed, near):
        r = plan[at + 2 + 5 * j]
        block = plan[at + 2 + 5 * j + 1]
        start = plan[at + 2 + 5 * j + 3]
        first = 0 if lower else lax.div(r, 8)
        last = lax.div(r + 7, 8) if lower else 32
        keep = lanes() >= plan[at + 2 + 5 * j + 2]
        low = pl.multiple_of(block * N, N)
        high = pl.multiple_of(block * N + N, N)

        def step(g, carry):
            dst = pl.multiple_of(g * 8, 8)
            inside = (row + dst < r) if lower else (row + dst >= r)
            if packed:
                src = pl.multiple_of((start + g - first) * 8, 8)
                value = rows[0 if lower else 1, c, pl.ds(src, 8), :]
            else:
                value = grads[depth, j, c, pl.ds(dst, 8), :] if near else partner[j, c, pl.ds(dst, 8), :]
            value = jnp.where(inside, value, 0.0)
            tile[c, pl.ds(dst, 8), pl.ds(low, N)] += jnp.where(keep, value, 0.0)
            tile[c, pl.ds(dst, 8), pl.ds(high, N)] += jnp.where(keep, 0.0, value)
            return carry

        lax.fori_loop(first, last, step, 0)

    def run(at, c, lower, packed, near):
        def step(j, carry):
            add(at, j, c, lower, packed, near)
            return carry

        lax.fori_loop(0, plan[at], step, 0)

    for c in range(2):

        @pl.when(depth == 0)
        def _(c=c):
            run(OWN_LEFT, c, False, False, True)
            run(PREV_RIGHT, c, True, False, False)

        @pl.when(depth == 1)
        def _(c=c):
            run(OWN_LEFT, c, False, False, False)
            run(PREV_RIGHT, c, True, False, True)

        run(OWN_RIGHT, c, False, True, False)
        run(PREV_LEFT, c, True, True, False)
        pltpu.make_async_copy(tile.at[c], out.at[c], out_sems.at[c]).start()
    for c in range(2):
        pltpu.make_async_copy(tile.at[c], out.at[c], out_sems.at[c]).wait()


SMEM = pl.BlockSpec(memory_space=pltpu.SMEM)
VMEM = pl.BlockSpec(memory_space=pltpu.VMEM)
HBM = pl.BlockSpec(memory_space=pltpu.HBM)


def shape(*dims):
    return jax.ShapeDtypeStruct(dims, jnp.float32)


def shards(n_lat, object_slices, probe, measured, positions, counts):
    columns = object_slices.shape[3]
    tile = object_slices.reshape(object_slices.shape[1:])
    dma = pltpu.SemaphoreType.DMA
    positions = positions.T
    positions, prev_positions, prev_counts, tile, measured = pl.pallas_call(
        functools.partial(announce_kernel, n_lat),
        name="announce",
        out_shape=(
            jax.ShapeDtypeStruct(positions.shape, jnp.int32),
            jax.ShapeDtypeStruct(positions.shape, jnp.int32),
            jax.ShapeDtypeStruct(counts.shape, jnp.int32),
            shape(*tile.shape),
            shape(*measured.shape),
        ),
        in_specs=[HBM, HBM, HBM, HBM],
        out_specs=(VMEM, VMEM, VMEM, VMEM, VMEM),
        scratch_shapes=[
            pltpu.VMEM((4, N, N), jnp.float32),
            pltpu.VMEM((2, N, HALF), jnp.float32),
            dma((2,)), dma((2,)), dma((3,)),
        ],
        compiler_params=pltpu.CompilerParams(
            collective_id=2, has_side_effects=True, vmem_limit_bytes=46 << 20
        ),
    )(positions, counts, tile, measured)
    plan, ahead, behind = pl.pallas_call(
        pack_kernel,
        name="pack",
        out_shape=(
            jax.ShapeDtypeStruct((4 * SPAN,), jnp.int32),
            shape(2, ROWS, N),
            shape(2, ROWS, N),
        ),
        in_specs=[SMEM, SMEM, SMEM, SMEM, VMEM, VMEM],
        out_specs=(SMEM, VMEM, VMEM),
        compiler_params=pltpu.CompilerParams(vmem_limit_bytes=4 << 20),
    )(positions, counts, prev_positions, prev_counts, tile, measured)
    received, other = pl.pallas_call(
        functools.partial(exchange_kernel, n_lat),
        name="exchange",
        out_shape=(shape(2, 2, ROWS + 2 * PAD, N), shape(2, N, columns)),
        in_specs=[VMEM, VMEM, VMEM],
        out_specs=(VMEM, VMEM),
        scratch_shapes=[dma((2,)), dma((2,)), dma, dma],
        compiler_params=pltpu.CompilerParams(
            collective_id=0, has_side_effects=True, vmem_limit_bytes=12 << 20
        ),
    )(ahead, behind, tile)

    table = jnp.asarray(tables())
    rows_out, grads = pl.pallas_call(
        compute_kernel,
        name="compute",
        out_shape=(shape(2, 2, ROWS, N), shape(2, MAX_JOBS, 2, N, N)),
        in_specs=[SMEM, VMEM, VMEM, VMEM, VMEM, VMEM, VMEM],
        out_specs=(VMEM, VMEM),
        scratch_shapes=[pltpu.VMEM((2, N, N), jnp.float32)],
        compiler_params=pltpu.CompilerParams(vmem_limit_bytes=30 << 20),
    )(plan, tile, other, received, measured, probe, table)

    rows_back, partner = pl.pallas_call(
        functools.partial(return_kernel, n_lat),
        name="giveback",
        out_shape=(shape(2, 2, ROWS, N), shape(MAX_JOBS, 2, N, N)),
        in_specs=[VMEM, VMEM],
        out_specs=(VMEM, VMEM),
        scratch_shapes=[dma((2,)), dma((2,)), dma, dma],
        compiler_params=pltpu.CompilerParams(
            collective_id=1, has_side_effects=True, vmem_limit_bytes=12 << 20
        ),
    )(rows_out, grads)

    out = pl.pallas_call(
        gather_kernel,
        name="gather",
        out_shape=shape(2, N, columns),
        in_specs=[SMEM, VMEM, VMEM, VMEM],
        out_specs=HBM,
        scratch_shapes=[pltpu.VMEM((2, N, columns), jnp.float32), dma((2,))],
        compiler_params=pltpu.CompilerParams(vmem_limit_bytes=20 << 20),
    )(plan, rows_back, partner, grads)
    return out.reshape(object_slices.shape)


def solution(mesh):
    return jax.shard_map(
        functools.partial(shards, mesh.shape["lat"]),
        mesh=mesh,
        in_specs=(
            P("depth", None, "lat", None),
            P(),
            P("lat", None, None),
            P("lat", None),
            P("lat"),
        ),
        out_specs=P("depth", None, "lat", None),
        check_vma=False,
    )
```

```python
import functools

import jax
import jax.numpy as jnp
import ml_dtypes
import numpy as np
from jax import lax
from jax.experimental import pallas as pl
from jax.experimental.pallas import tpu as pltpu
from jax.sharding import PartitionSpec as P

N = 256
HALF = 128
STRENGTH = 8.0
MAX_JOBS = 3
BUDGET = 48
ROWS = 8 * BUDGET
PAD = 256
CHUNK = 32
SPAN = 20


def split_bf16(a):
    hi = a.astype(np.float32).astype(ml_dtypes.bfloat16)
    lo = (a - hi.astype(np.float64)).astype(np.float32).astype(ml_dtypes.bfloat16)
    return hi, lo


def tables():
    index = np.arange(N)
    angle = 2.0 * np.pi * ((index[:, None] * index[None, :]) % N) / N
    dft = np.exp(-1j * angle) / 16.0
    centred = (index - N * (index >= HALF)) / N
    turn = np.exp(1j * np.pi * STRENGTH * centred**2)
    prop = np.conj(dft) @ (turn[:, None] * dft)
    c0, c1 = prop[:HALF, :HALF], prop[:HALF, HALF:]

    def real_form(m):
        return np.block([[m.real, -m.imag], [m.imag, m.real]])

    forms = [real_form(m) for m in ((c0 + c1) / 2, (c0 - c1) / 2, dft[0::2, :HALF], dft[1::2, :HALF])]
    forms = forms + [m.T for m in forms]
    return np.stack([np.stack(split_bf16(m)) for m in forms])


OWN_LEFT, OWN_RIGHT, PREV_LEFT, PREV_RIGHT = 0, SPAN, 2 * SPAN, 3 * SPAN


def choose_sides(rows_of, cols_of, live):
    up = [lax.div(rows_of[i] + 7, 8) for i in range(4)]
    down = [32 - lax.div(rows_of[i], 8) for i in range(4)]
    best = jnp.int32(1 << 20)
    pick = jnp.int32(0)
    for mask in range(16):
        right = [(mask >> i) & 1 for i in range(4)]
        n_right = sum(right)
        if n_right > MAX_JOBS:
            continue
        top = max([i + 1 for i in range(4) if right[i]], default=0)
        lefts = [jnp.where(live > i, up[i], 0) for i in range(4) if not right[i]]
        cost_left = sum(lefts, jnp.int32(0))
        cost_right = sum([down[i] + 8 for i in range(4) if right[i]], jnp.int32(0))
        widest = jnp.maximum(cost_left, cost_right)
        most = jnp.maximum(live - n_right, n_right)
        bad = (live < top) | (widest > BUDGET) | (most > MAX_JOBS)
        key = most * 64 + widest + jnp.where(bad, jnp.int32(1 << 16), 0)
        pick = jnp.where(key < best, mask, pick)
        best = jnp.minimum(key, best)
    blocks = [jnp.minimum(lax.div(cols_of[i], N), 6) for i in range(4)]
    sides = []
    for side in range(2):
        mine = [(live > i) & ((lax.shift_right_logical(pick, i) & 1) == side) for i in range(4)]
        size = up if side == 0 else down
        count, total = jnp.int32(0), jnp.int32(0)
        words = [[jnp.int32(0)] * 5 for _ in range(MAX_JOBS)]
        for i in range(4):
            fields = [rows_of[i], blocks[i], cols_of[i] - blocks[i] * N, total, jnp.int32(i)]
            for j in range(MAX_JOBS):
                here = mine[i] & (count == j)
                words[j] = [jnp.where(here, f, w) for f, w in zip(fields, words[j])]
            count = count + jnp.where(mine[i], 1, 0)
            total = total + jnp.where(mine[i], size[i], 0)
        sides.append([count, total] + [w for job in words for w in job])
    return sides


def lanes():
    return lax.broadcasted_iota(jnp.int32, (8, N), 1)


def announce_kernel(
    n_lat, pos_hbm, cnt, tile_hbm, measured_hbm,
    pos, prev_pos, prev_cnt, tile, apart,
    measured, spread, send, recv, local,
):
    depth = lax.axis_index("depth")
    lat = lax.axis_index("lat")
    after = lax.rem(lat + 1, n_lat)
    before = lax.rem(lat + n_lat - 1, n_lat)
    barrier = pltpu.get_barrier_semaphore()
    for other in (after, before):
        pl.semaphore_signal(
            barrier, inc=1, device_id=(depth, other), device_id_type=pl.DeviceIdType.MESH
        )
    loads = [
        pltpu.make_async_copy(measured_hbm, measured, local.at[0]),
        pltpu.make_async_copy(tile_hbm, tile, local.at[1]),
        pltpu.make_async_copy(pos_hbm, pos, local.at[2]),
    ]
    for load in loads:
        load.start()
    pl.semaphore_wait(barrier, 2)
    copies = [
        remote(pos_hbm, prev_pos, send.at[0], recv.at[0], depth, after),
        remote(cnt, prev_cnt, send.at[1], recv.at[1], depth, after),
    ]
    for copy in copies:
        copy.start()
    row = lax.broadcasted_iota(jnp.int32, (N, N), 0)
    lane = lax.broadcasted_iota(jnp.int32, (N, N), 1)
    order = jnp.where(lane < HALF, 2 * lane, 2 * lane - (N - 1))
    shuffle = jnp.where(row == order, 1.0, 0.0).astype(jnp.bfloat16)
    loads[0].wait()
    for slot in range(4):
        hi, lo = halves(measured[slot])
        columns = dot(
            jnp.concatenate([hi, lo], axis=1), jnp.concatenate([shuffle, shuffle], axis=0)
        )
        for h in range(2):
            spread[h] = columns[:, HALF * h : HALF * h + HALF]
        for p in range(2):
            for h in range(2):
                apart[slot, HALF * p : HALF * p + HALF, HALF * h : HALF * h + HALF] = spread[
                    h, pl.ds(p, HALF, stride=2), :
                ]
    for load in loads[1:]:
        load.wait()
    for copy in copies:
        copy.wait()


def pack_kernel(
    pos, cnt, prev_pos, prev_cnt, tile, measured, plan, ahead, behind
):
    depth = lax.axis_index("depth")
    own = choose_sides([pos[0, i] for i in range(4)], [pos[1, i] for i in range(4)], cnt[0])
    prev = choose_sides(
        [prev_pos[0, i] for i in range(4)], [prev_pos[1, i] for i in range(4)], prev_cnt[0]
    )
    for k, side in enumerate(own + prev):
        for w, word in enumerate(side):
            plan[k * SPAN + w] = word

    def copy_rows(out, at, j, first, count):
        start = plan[at + 2 + 5 * j + 3]
        low = pl.multiple_of(plan[at + 2 + 5 * j + 1] * N, N)
        high = pl.multiple_of(plan[at + 2 + 5 * j + 1] * N + N, N)
        keep = lanes() >= plan[at + 2 + 5 * j + 2]

        def step(g, carry):
            for k in range(4):
                granule = jnp.minimum(4 * g + k, count - 1)
                src = pl.multiple_of((first + granule) * 8, 8)
                dst = pl.multiple_of((start + granule) * 8, 8)
                for c in range(2):
                    out[c, pl.ds(dst, 8), :] = jnp.where(
                        keep,
                        tile[c, pl.ds(src, 8), pl.ds(low, N)],
                        tile[c, pl.ds(src, 8), pl.ds(high, N)],
                    )
            return carry

        lax.fori_loop(0, lax.div(count + 3, 4), step, 0)

    def right_job(j, carry):
        first = lax.div(plan[OWN_RIGHT + 2 + 5 * j], 8)
        copy_rows(ahead, OWN_RIGHT, j, first, 32 - first)
        slot = plan[OWN_RIGHT + 2 + 5 * j + 4]
        dst = pl.multiple_of((plan[OWN_RIGHT + 1] + 8 * j) * 8, 8)
        for c in range(2):
            src = pl.multiple_of(depth * HALF + 64 * c, 64)
            ahead[c, pl.ds(dst, 64), :] = measured[slot, pl.ds(src, 64), :]
        return carry

    lax.fori_loop(0, plan[OWN_RIGHT], right_job, 0)

    def left_job(j, carry):
        copy_rows(behind, PREV_LEFT, j, 0, lax.div(plan[PREV_LEFT + 2 + 5 * j] + 7, 8))
        return carry

    lax.fori_loop(0, plan[PREV_LEFT], left_job, 0)


def exchange_kernel(
    n_lat, ahead, behind, tile, received, other,
    row_send, row_recv, tile_send, tile_recv,
):
    depth = lax.axis_index("depth")
    lat = lax.axis_index("lat")
    after = lax.rem(lat + 1, n_lat)
    before = lax.rem(lat + n_lat - 1, n_lat)
    greet(depth, lat, after, before)
    pl.semaphore_wait(pltpu.get_barrier_semaphore(), 4)

    def slot(s):
        return received.at[s, :, pl.ds(PAD, ROWS), :]

    sends = [
        remote(ahead, slot(depth), row_send.at[0], row_recv.at[depth], 1, after),
        remote(behind, slot(depth), row_send.at[1], row_recv.at[depth], 0, before),
    ]
    for copy in sends:
        copy.start()
    swap = remote(tile, other, tile_send, tile_recv, 1 - depth, lat)
    swap.start()
    for copy in sends:
        copy.wait_send()
    for s in range(2):
        remote(ahead, slot(s), row_send.at[0], row_recv.at[s], 1, after).wait_recv()
    swap.wait()


def remote(src, dst, send, recv, depth, lat):
    return pltpu.make_async_remote_copy(
        src_ref=src,
        dst_ref=dst,
        send_sem=send,
        recv_sem=recv,
        device_id=(depth, lat),
        device_id_type=pl.DeviceIdType.MESH,
    )


def greet(depth, lat, after, before):
    barrier = pltpu.get_barrier_semaphore()
    partners = [
        (depth, after),
        (depth, before),
        (1 - depth, jnp.where(depth == 0, after, before)),
        (1 - depth, lat),
    ]
    for partner in partners:
        pl.semaphore_signal(
            barrier, inc=1, device_id=partner, device_id_type=pl.DeviceIdType.MESH
        )


def return_kernel(
    n_lat, plan, rows, windows, received, tile,
    partner, row_send, row_recv, swap_send, swap_recv,
):
    depth = lax.axis_index("depth")
    lat = lax.axis_index("lat")
    after = lax.rem(lat + 1, n_lat)
    before = lax.rem(lat + n_lat - 1, n_lat)
    greet(depth, lat, after, before)
    pl.semaphore_wait(pltpu.get_barrier_semaphore(), 4)
    target = jnp.where(depth == 0, after, before)

    def part(c):
        return received.at[c, :, pl.ds(CHUNK, ROWS), :]

    sends = [
        remote(rows.at[s], part(depth), row_send.at[s], row_recv.at[depth], s, target)
        for s in range(2)
    ]
    for copy in sends:
        copy.start()
    swap = remote(windows.at[1 - depth], partner, swap_send, swap_recv, 1 - depth, lat)
    swap.start()
    sum_windows(plan, depth, lambda j, c, at: windows[depth, j, c, at, :], tile, True)
    swap.wait()
    sum_windows(plan, 1 - depth, lambda j, c, at: partner[j, c, at, :], tile, False)
    for copy in sends:
        copy.wait_send()
    for c in range(2):
        remote(rows.at[0], part(c), row_send.at[0], row_recv.at[c], 0, target).wait_recv()


def sum_windows(plan, core, read, tile, first):
    at = jnp.where(core == 0, OWN_LEFT, PREV_RIGHT)
    row = lax.broadcasted_iota(jnp.int32, (8, N), 0)
    lane = lanes()
    jobs = []
    for j in range(MAX_JOBS):
        r = plan[at + 2 + 5 * j]
        low = jnp.where(core == 0, r, 0)
        high = jnp.where(plan[at] > j, jnp.where(core == 0, N, r), 0)
        jobs.append((low, high, plan[at + 2 + 5 * j + 1] * N + plan[at + 2 + 5 * j + 2]))

    def step(g, carry):
        dst = pl.ds(pl.multiple_of(g * 8, 8), 8)
        here = row + g * 8
        for c in range(2):
            values = [
                jnp.where((here >= low) & (here < high), read(j, c, dst), 0.0)
                for j, (low, high, _) in enumerate(jobs)
            ]
            for q in range(tile.shape[2] // N):
                total = None if first else tile[c, dst, q * N : q * N + N]
                for value, (_, _, column) in zip(values, jobs):
                    offset = lane + (q * N - column)
                    inside = (offset >= 0) & (offset < N)
                    value = jnp.where(inside, value, 0.0)
                    total = value if total is None else total + value
                tile[c, dst, q * N : q * N + N] = total
        return carry

    lax.fori_loop(0, N // 8, step, 0)


P_PLUS, P_MINUS, F_EVEN, F_ODD = 0, 1, 2, 3
TURNED = 4


def halves(x):
    hi = x.astype(jnp.bfloat16)
    lo = (x - hi.astype(jnp.float32)).astype(jnp.bfloat16)
    return hi, lo


def dot(a, b):
    return jnp.dot(a, b, preferred_element_type=jnp.float32)


def times_right(x, table, at):
    hi, lo = halves(x)
    return dot(
        jnp.concatenate([hi, lo, hi], axis=1),
        jnp.concatenate([table[at, 0], table[at, 0], table[at, 1]], axis=0),
    )


def times_left(table, at, x):
    hi, lo = halves(x)
    return dot(
        jnp.concatenate([table[at, 0], table[at, 0], table[at, 1]], axis=1),
        jnp.concatenate([hi, lo, hi], axis=0),
    )


def fold_columns(re, im):
    plus = jnp.concatenate([re[:, :HALF] + re[:, HALF:], im[:, :HALF] + im[:, HALF:]], axis=1)
    minus = jnp.concatenate([re[:, :HALF] - re[:, HALF:], im[:, :HALF] - im[:, HALF:]], axis=1)
    return plus, minus


def pair_columns(re, im):
    return (
        jnp.concatenate([re[:, :HALF], im[:, :HALF]], axis=1),
        jnp.concatenate([re[:, HALF:], im[:, HALF:]], axis=1),
    )


def fold_rows(re, im):
    plus = jnp.concatenate([re[:HALF] + re[HALF:], im[:HALF] + im[HALF:]], axis=0)
    minus = jnp.concatenate([re[:HALF] - re[HALF:], im[:HALF] - im[HALF:]], axis=0)
    return plus, minus


def pair_rows(re, im):
    return (
        jnp.concatenate([re[:HALF], im[:HALF]], axis=0),
        jnp.concatenate([re[HALF:], im[HALF:]], axis=0),
    )


def product(u, v):
    return u[0] * v[0] - u[1] * v[1], u[0] * v[1] + u[1] * v[0]


def conj_product(u, v):
    return u[0] * v[0] + u[1] * v[1], u[0] * v[1] - u[1] * v[0]


def both_right(pairs, table, first, second):
    return [(times_right(p, table, first), times_right(m, table, second)) for p, m in pairs]


def both_left(pairs, table, first, second):
    return [(times_left(table, first, p), times_left(table, second, m)) for p, m in pairs]


def unfold(pairs):
    return [(p + m, p - m) for p, m in pairs]


def propagate(fields, table, adjoint):
    left, right = (TURNED, 0) if adjoint else (0, TURNED)
    pairs = [fold_columns(*f) for f in fields]
    pairs = unfold(both_right(pairs, table, right + P_PLUS, right + P_MINUS))
    pairs = [fold_rows(*pair_columns(*p)) for p in pairs]
    pairs = unfold(both_left(pairs, table, left + P_PLUS, left + P_MINUS))
    return [pair_rows(*p) for p in pairs]


def to_spectrum(fields, table):
    pairs = [fold_columns(*f) for f in fields]
    pairs = both_right(pairs, table, TURNED + F_EVEN, TURNED + F_ODD)
    pairs = [fold_rows(*pair_columns(*p)) for p in pairs]
    pairs = both_left(pairs, table, F_EVEN, F_ODD)
    return [pair_rows(*p) for p in pairs]


def from_spectrum(fields, table):
    pairs = [pair_columns(*f) for f in fields]
    pairs = unfold(both_right(pairs, table, F_EVEN, F_ODD))
    pairs = [pair_rows(*pair_columns(*p)) for p in pairs]
    pairs = unfold(both_left(pairs, table, TURNED + F_EVEN, TURNED + F_ODD))
    return [pair_rows(*p) for p in pairs]


def compute_kernel(
    plan, tile, other, received, measured, probe, table,
    rows_out, grads,
    amplitude,
):
    depth = lax.axis_index("depth")
    at = jnp.where(depth == 0, OWN_LEFT, PREV_RIGHT)
    jobs = plan[at]
    row = lax.broadcasted_iota(jnp.int32, (N, N), 0)
    lane = lax.broadcasted_iota(jnp.int32, (N, N), 1)

    def work(numbers):
        each = range(len(numbers))
        words = [[plan[at + 2 + 5 * j + w] for w in range(5)] for j in numbers]

        for k in each:
            _, _, _, _, slot = words[k]

            @pl.when(depth == 0)
            def _(k=k, slot=slot):
                amplitude[k] = measured[slot]

            @pl.when(depth == 1)
            def _(k=k):
                src = pl.multiple_of(PAD + (plan[PREV_RIGHT + 1] + 8 * numbers[k]) * 8, 8)
                for s in range(2):
                    for c in range(2):
                        amplitude[k, pl.ds(128 * s + 64 * c, 64), :] = received[
                            s, c, pl.ds(src, 64), :
                        ]

        def base_of(k):
            return jnp.where(depth == 0, 0, lax.div(words[k][0], 8))

        def window(k, s):
            r, block, shift, start, _ = words[k]
            here = (row >= jnp.where(depth == 0, r, 0)) & (row < jnp.where(depth == 0, N, r))
            keep = lane >= shift
            src = pl.multiple_of(PAD + (start - base_of(k)) * 8, 8)
            column = pl.multiple_of(block * N, N)
            left, right = pl.ds(column, N), pl.ds(pl.multiple_of(column + N, N), N)
            near = depth == s
            return [
                jnp.where(
                    here,
                    jnp.where(
                        keep,
                        jnp.where(near, tile[c, :, left], other[c, :, left]),
                        jnp.where(near, tile[c, :, right], other[c, :, right]),
                    ),
                    received[s, c, pl.ds(src, N), :],
                )
                for c in range(2)
            ]

        def rolled(k):
            r, _, shift, _, _ = words[k]
            return [
                pltpu.roll(pltpu.roll(probe[c], r, 0), jnp.where(shift == N, 0, shift), 1)
                for c in range(2)
            ]

        probes = [rolled(k) for k in each]
        waves = [product(p, window(k, 0)) for k, p in enumerate(probes)]
        waves = propagate(waves, table, False)
        slices = [window(k, 1) for k in each]
        spectra = to_spectrum([product(w, o) for w, o in zip(waves, slices)], table)
        backs = []
        for k in each:
            re, im = spectra[k]
            factor = 1.0 - amplitude[k] * lax.rsqrt(re * re + im * im + 1.0)
            backs.append((re * factor, im * factor))
        backs = from_spectrum(backs, table)
        for k in each:
            grads[1, numbers[k], 0], grads[1, numbers[k], 1] = conj_product(waves[k], backs[k])
        backs = [conj_product(o, b) for o, b in zip(slices, backs)]
        backs = propagate(backs, table, True)
        for k in each:
            grads[0, numbers[k], 0], grads[0, numbers[k], 1] = conj_product(probes[k], backs[k])
        for k in each:
            r, start = words[k][0], words[k][3]
            base = base_of(k)
            count = jnp.where(depth == 0, lax.div(r + 7, 8), 32 - lax.div(r, 8))

            def step(g, carry, k=k, base=base, start=start):
                src = pl.multiple_of((base + g) * 8, 8)
                dst = pl.multiple_of((start + g) * 8, 8)
                for s in range(2):
                    for c in range(2):
                        rows_out[s, c, pl.ds(dst, 8), :] = grads[
                            s, numbers[k], c, pl.ds(src, 8), :
                        ]
                return carry

            lax.fori_loop(0, count, step, 0)

    @pl.when(jobs >= 2)
    def _():
        work([0, 1])

    @pl.when(lax.rem(jobs, 2) == 1)
    def _():
        work([jobs - 1])


def gather_kernel(plan, rows, tile_in, out, tile, out_sems):
    row = lax.broadcasted_iota(jnp.int32, (CHUNK, N), 0)
    lane = lax.broadcasted_iota(jnp.int32, (CHUNK, N), 1)

    def add(at, j, c, lower):
        r = plan[at + 2 + 5 * j]
        start = plan[at + 2 + 5 * j + 3]
        first = 0 if lower else lax.div(r, CHUNK)
        last = lax.div(r + CHUNK - 1, CHUNK) if lower else N // CHUNK
        skip = 0 if lower else lax.div(r, 8)
        keep = lane >= plan[at + 2 + 5 * j + 2]
        low = pl.multiple_of(plan[at + 2 + 5 * j + 1] * N, N)
        high = pl.multiple_of(plan[at + 2 + 5 * j + 1] * N + N, N)

        def step(g, carry):
            dst = pl.multiple_of(g * CHUNK, CHUNK)
            inside = (row + dst < r) if lower else (row + dst >= r)
            src = pl.multiple_of(CHUNK + (start - skip) * 8 + g * CHUNK, 8)
            value = jnp.where(inside, rows[0 if lower else 1, c, pl.ds(src, CHUNK), :], 0.0)
            tile[c, pl.ds(dst, CHUNK), pl.ds(low, N)] += jnp.where(keep, value, 0.0)
            tile[c, pl.ds(dst, CHUNK), pl.ds(high, N)] += jnp.where(keep, 0.0, value)
            return carry

        lax.fori_loop(first, last, step, 0)

    for c in range(2):
        for at, lower in ((OWN_RIGHT, False), (PREV_LEFT, True)):

            def step(j, carry, at=at, lower=lower, c=c):
                add(at, j, c, lower)
                return carry

            lax.fori_loop(0, plan[at], step, 0)
        pltpu.make_async_copy(tile.at[c], out.at[c], out_sems.at[c]).start()
    for c in range(2):
        pltpu.make_async_copy(tile.at[c], out.at[c], out_sems.at[c]).wait()


SMEM = pl.BlockSpec(memory_space=pltpu.SMEM)
VMEM = pl.BlockSpec(memory_space=pltpu.VMEM)
HBM = pl.BlockSpec(memory_space=pltpu.HBM)


def shape(*dims):
    return jax.ShapeDtypeStruct(dims, jnp.float32)


def shards(n_lat, object_slices, probe, measured, positions, counts):
    columns = object_slices.shape[3]
    tile = object_slices.reshape(object_slices.shape[1:])
    dma = pltpu.SemaphoreType.DMA
    positions = positions.T
    positions, prev_positions, prev_counts, tile, measured = pl.pallas_call(
        functools.partial(announce_kernel, n_lat),
        name="announce",
        out_shape=(
            jax.ShapeDtypeStruct(positions.shape, jnp.int32),
            jax.ShapeDtypeStruct(positions.shape, jnp.int32),
            jax.ShapeDtypeStruct(counts.shape, jnp.int32),
            shape(*tile.shape),
            shape(*measured.shape),
        ),
        in_specs=[HBM, HBM, HBM, HBM],
        out_specs=(VMEM, VMEM, VMEM, VMEM, VMEM),
        scratch_shapes=[
            pltpu.VMEM((4, N, N), jnp.float32),
            pltpu.VMEM((2, N, HALF), jnp.float32),
            dma((2,)), dma((2,)), dma((3,)),
        ],
        compiler_params=pltpu.CompilerParams(
            collective_id=2, has_side_effects=True, vmem_limit_bytes=46 << 20
        ),
    )(positions, counts, tile, measured)
    plan, ahead, behind = pl.pallas_call(
        pack_kernel,
        name="pack",
        out_shape=(
            jax.ShapeDtypeStruct((4 * SPAN,), jnp.int32),
            shape(2, ROWS, N),
            shape(2, ROWS, N),
        ),
        in_specs=[SMEM, SMEM, SMEM, SMEM, VMEM, VMEM],
        out_specs=(SMEM, VMEM, VMEM),
        compiler_params=pltpu.CompilerParams(vmem_limit_bytes=4 << 20),
    )(positions, counts, prev_positions, prev_counts, tile, measured)
    received, other = pl.pallas_call(
        functools.partial(exchange_kernel, n_lat),
        name="exchange",
        out_shape=(shape(2, 2, ROWS + 2 * PAD, N), shape(2, N, columns)),
        in_specs=[VMEM, VMEM, VMEM],
        out_specs=(VMEM, VMEM),
        scratch_shapes=[dma((2,)), dma((2,)), dma, dma],
        compiler_params=pltpu.CompilerParams(
            collective_id=0, has_side_effects=True, vmem_limit_bytes=12 << 20
        ),
    )(ahead, behind, tile)

    table = jnp.asarray(tables())
    rows_out, grads = pl.pallas_call(
        compute_kernel,
        name="compute",
        out_shape=(shape(2, 2, ROWS, N), shape(2, MAX_JOBS, 2, N, N)),
        in_specs=[SMEM, VMEM, VMEM, VMEM, VMEM, VMEM, VMEM],
        out_specs=(VMEM, VMEM),
        scratch_shapes=[pltpu.VMEM((2, N, N), jnp.float32)],
        compiler_params=pltpu.CompilerParams(vmem_limit_bytes=30 << 20),
    )(plan, tile, other, received, measured, probe, table)

    rows_back, tile = pl.pallas_call(
        functools.partial(return_kernel, n_lat),
        name="giveback",
        out_shape=(shape(2, 2, ROWS + 2 * CHUNK, N), shape(2, N, columns)),
        in_specs=[SMEM, VMEM, VMEM],
        out_specs=(VMEM, VMEM),
        scratch_shapes=[
            pltpu.VMEM((MAX_JOBS, 2, N, N), jnp.float32),
            dma((2,)), dma((2,)), dma, dma,
        ],
        compiler_params=pltpu.CompilerParams(
            collective_id=1, has_side_effects=True, vmem_limit_bytes=12 << 20
        ),
    )(plan, rows_out, grads)

    out, _ = pl.pallas_call(
        gather_kernel,
        name="gather",
        out_shape=(shape(2, N, columns), shape(2, N, columns)),
        in_specs=[SMEM, VMEM, VMEM],
        out_specs=(HBM, VMEM),
        scratch_shapes=[dma((2,))],
        input_output_aliases={2: 1},
        compiler_params=pltpu.CompilerParams(vmem_limit_bytes=12 << 20),
    )(plan, rows_back, tile)
    return out.reshape(object_slices.shape)


def solution(mesh):
    return jax.shard_map(
        functools.partial(shards, mesh.shape["lat"]),
        mesh=mesh,
        in_specs=(
            P("depth", None, "lat", None),
            P(),
            P("lat", None, None),
            P("lat", None),
            P("lat"),
        ),
        out_specs=P("depth", None, "lat", None),
        check_vma=False,
    )
```

```python
import functools

import jax
import jax.numpy as jnp
import ml_dtypes
import numpy as np
from jax import lax
from jax.experimental import pallas as pl
from jax.experimental.pallas import tpu as pltpu
from jax.sharding import PartitionSpec as P

N = 256
HALF = 128
STRENGTH = 8.0
MAX_JOBS = 3
BUDGET = 48
ROWS = 8 * BUDGET
PAD = 256
CHUNK = 32
SPAN = 20


def split_bf16(a):
    hi = a.astype(np.float32).astype(ml_dtypes.bfloat16)
    lo = (a - hi.astype(np.float64)).astype(np.float32).astype(ml_dtypes.bfloat16)
    return hi, lo


def tables():
    index = np.arange(N)
    angle = 2.0 * np.pi * ((index[:, None] * index[None, :]) % N) / N
    dft = np.exp(-1j * angle) / 16.0
    centred = (index - N * (index >= HALF)) / N
    turn = np.exp(1j * np.pi * STRENGTH * centred**2)
    prop = np.conj(dft) @ (turn[:, None] * dft)
    c0, c1 = prop[:HALF, :HALF], prop[:HALF, HALF:]

    def real_form(m):
        return np.block([[m.real, -m.imag], [m.imag, m.real]])

    forms = [real_form(m) for m in ((c0 + c1) / 2, (c0 - c1) / 2, dft[0::2, :HALF], dft[1::2, :HALF])]
    forms = forms + [m.T for m in forms]
    return np.stack([np.stack(split_bf16(m)) for m in forms])


OWN_LEFT, OWN_RIGHT, PREV_LEFT, PREV_RIGHT = 0, SPAN, 2 * SPAN, 3 * SPAN


def choose_sides(rows_of, cols_of, live):
    up = [lax.div(rows_of[i] + 7, 8) for i in range(4)]
    down = [32 - lax.div(rows_of[i], 8) for i in range(4)]
    best = jnp.int32(1 << 20)
    pick = jnp.int32(0)
    for mask in range(16):
        right = [(mask >> i) & 1 for i in range(4)]
        n_right = sum(right)
        if n_right > MAX_JOBS:
            continue
        top = max([i + 1 for i in range(4) if right[i]], default=0)
        lefts = [jnp.where(live > i, up[i], 0) for i in range(4) if not right[i]]
        cost_left = sum(lefts, jnp.int32(0))
        cost_right = sum([down[i] + 8 for i in range(4) if right[i]], jnp.int32(0))
        widest = jnp.maximum(cost_left, cost_right)
        most = jnp.maximum(live - n_right, n_right)
        bad = (live < top) | (widest > BUDGET) | (most > MAX_JOBS)
        key = most * 64 + widest + jnp.where(bad, jnp.int32(1 << 16), 0)
        pick = jnp.where(key < best, mask, pick)
        best = jnp.minimum(key, best)
    blocks = [jnp.minimum(lax.div(cols_of[i], N), 6) for i in range(4)]
    sides = []
    for side in range(2):
        mine = [(live > i) & ((lax.shift_right_logical(pick, i) & 1) == side) for i in range(4)]
        size = up if side == 0 else down
        count, total = jnp.int32(0), jnp.int32(0)
        words = [[jnp.int32(0)] * 5 for _ in range(MAX_JOBS)]
        for i in range(4):
            fields = [rows_of[i], blocks[i], cols_of[i] - blocks[i] * N, total, jnp.int32(i)]
            for j in range(MAX_JOBS):
                here = mine[i] & (count == j)
                words[j] = [jnp.where(here, f, w) for f, w in zip(fields, words[j])]
            count = count + jnp.where(mine[i], 1, 0)
            total = total + jnp.where(mine[i], size[i], 0)
        sides.append([count, total] + [w for job in words for w in job])
    return sides


def lanes():
    return lax.broadcasted_iota(jnp.int32, (8, N), 1)


def announce_kernel(
    n_lat, pos_hbm, cnt, tile_hbm, measured_hbm,
    pos, prev_pos, prev_cnt, tile, apart,
    measured, spread, send, recv, local,
):
    depth = lax.axis_index("depth")
    lat = lax.axis_index("lat")
    after = lax.rem(lat + 1, n_lat)
    before = lax.rem(lat + n_lat - 1, n_lat)
    barrier = pltpu.get_barrier_semaphore()
    for other in (after, before):
        pl.semaphore_signal(
            barrier, inc=1, device_id=(depth, other), device_id_type=pl.DeviceIdType.MESH
        )
    loads = [
        pltpu.make_async_copy(measured_hbm, measured, local.at[0]),
        pltpu.make_async_copy(tile_hbm, tile, local.at[1]),
        pltpu.make_async_copy(pos_hbm, pos, local.at[2]),
    ]
    for load in loads:
        load.start()
    pl.semaphore_wait(barrier, 2)
    copies = [
        remote(pos_hbm, prev_pos, send.at[0], recv.at[0], depth, after),
        remote(cnt, prev_cnt, send.at[1], recv.at[1], depth, after),
    ]
    for copy in copies:
        copy.start()
    row = lax.broadcasted_iota(jnp.int32, (N, N), 0)
    lane = lax.broadcasted_iota(jnp.int32, (N, N), 1)
    order = jnp.where(lane < HALF, 2 * lane, 2 * lane - (N - 1))
    shuffle = jnp.where(row == order, 1.0, 0.0).astype(jnp.bfloat16)
    loads[0].wait()
    for slot in range(4):
        hi, lo = halves(measured[slot])
        columns = dot(
            jnp.concatenate([hi, lo], axis=1), jnp.concatenate([shuffle, shuffle], axis=0)
        )
        for h in range(2):
            spread[h] = columns[:, HALF * h : HALF * h + HALF]
        for p in range(2):
            for h in range(2):
                apart[slot, HALF * p : HALF * p + HALF, HALF * h : HALF * h + HALF] = spread[
                    h, pl.ds(p, HALF, stride=2), :
                ]
    for load in loads[1:]:
        load.wait()
    for copy in copies:
        copy.wait()


def pack_kernel(
    pos, cnt, prev_pos, prev_cnt, tile, measured, plan, ahead, behind
):
    depth = lax.axis_index("depth")
    own = choose_sides([pos[0, i] for i in range(4)], [pos[1, i] for i in range(4)], cnt[0])
    prev = choose_sides(
        [prev_pos[0, i] for i in range(4)], [prev_pos[1, i] for i in range(4)], prev_cnt[0]
    )
    for k, side in enumerate(own + prev):
        for w, word in enumerate(side):
            plan[k * SPAN + w] = word

    def copy_rows(out, at, j, first, count):
        start = plan[at + 2 + 5 * j + 3]
        low = pl.multiple_of(plan[at + 2 + 5 * j + 1] * N, N)
        high = pl.multiple_of(plan[at + 2 + 5 * j + 1] * N + N, N)
        keep = lanes() >= plan[at + 2 + 5 * j + 2]

        def step(g, carry):
            for k in range(4):
                granule = jnp.minimum(4 * g + k, count - 1)
                src = pl.multiple_of((first + granule) * 8, 8)
                dst = pl.multiple_of((start + granule) * 8, 8)
                for c in range(2):
                    out[c, pl.ds(dst, 8), :] = jnp.where(
                        keep,
                        tile[c, pl.ds(src, 8), pl.ds(low, N)],
                        tile[c, pl.ds(src, 8), pl.ds(high, N)],
                    )
            return carry

        lax.fori_loop(0, lax.div(count + 3, 4), step, 0)

    def right_job(j, carry):
        first = lax.div(plan[OWN_RIGHT + 2 + 5 * j], 8)
        copy_rows(ahead, OWN_RIGHT, j, first, 32 - first)
        slot = plan[OWN_RIGHT + 2 + 5 * j + 4]
        dst = pl.multiple_of((plan[OWN_RIGHT + 1] + 8 * j) * 8, 8)
        for c in range(2):
            src = pl.multiple_of(depth * HALF + 64 * c, 64)
            ahead[c, pl.ds(dst, 64), :] = measured[slot, pl.ds(src, 64), :]
        return carry

    lax.fori_loop(0, plan[OWN_RIGHT], right_job, 0)

    def left_job(j, carry):
        copy_rows(behind, PREV_LEFT, j, 0, lax.div(plan[PREV_LEFT + 2 + 5 * j] + 7, 8))
        return carry

    lax.fori_loop(0, plan[PREV_LEFT], left_job, 0)


def exchange_kernel(
    n_lat, plan, ahead, behind, tile, probe, received, windows, probes,
    other, row_send, row_recv, tile_send, tile_recv,
):
    depth = lax.axis_index("depth")
    lat = lax.axis_index("lat")
    after = lax.rem(lat + 1, n_lat)
    before = lax.rem(lat + n_lat - 1, n_lat)
    greet(depth, lat, after, before)
    pl.semaphore_wait(pltpu.get_barrier_semaphore(), 4)

    def slot(s):
        return received.at[s, :, pl.ds(PAD, ROWS), :]

    sends = [
        remote(ahead, slot(depth), row_send.at[0], row_recv.at[depth], 1, after),
        remote(behind, slot(depth), row_send.at[1], row_recv.at[depth], 0, before),
    ]
    for copy in sends:
        copy.start()
    swap = remote(tile, other, tile_send, tile_recv, 1 - depth, lat)
    swap.start()
    at = jnp.where(depth == 0, OWN_LEFT, PREV_RIGHT)
    for j in range(MAX_JOBS):
        shift = plan[at + 2 + 5 * j + 2]
        shift = jnp.where(shift == N, 0, shift)
        for c in range(2):
            probes[j, c] = pltpu.roll(pltpu.roll(probe[c], plan[at + 2 + 5 * j], 0), shift, 1)
    pick_columns(plan, at, tile, windows, depth)
    swap.wait()
    pick_columns(plan, at, other, windows, 1 - depth)
    for copy in sends:
        copy.wait_send()
    for s in range(2):
        remote(ahead, slot(s), row_send.at[0], row_recv.at[s], 1, after).wait_recv()


def pick_columns(plan, at, source, windows, s):
    lane = lanes()
    columns = [
        plan[at + 2 + 5 * j + 1] * N + plan[at + 2 + 5 * j + 2] for j in range(MAX_JOBS)
    ]

    def step(g, carry):
        rows = pl.ds(pl.multiple_of(g * 8, 8), 8)
        for c in range(2):
            picked = [jnp.zeros((8, N), jnp.float32)] * MAX_JOBS
            for q in range(source.shape[2] // N):
                value = source[c, rows, q * N : q * N + N]
                for j, column in enumerate(columns):
                    offset = lane + (q * N - column)
                    picked[j] = jnp.where((offset >= 0) & (offset < N), value, picked[j])
            for j in range(MAX_JOBS):
                windows[s, j, c, rows, :] = picked[j]
        return carry

    lax.fori_loop(0, N // 8, step, 0)


def remote(src, dst, send, recv, depth, lat):
    return pltpu.make_async_remote_copy(
        src_ref=src,
        dst_ref=dst,
        send_sem=send,
        recv_sem=recv,
        device_id=(depth, lat),
        device_id_type=pl.DeviceIdType.MESH,
    )


def greet(depth, lat, after, before):
    barrier = pltpu.get_barrier_semaphore()
    partners = [
        (depth, after),
        (depth, before),
        (1 - depth, jnp.where(depth == 0, after, before)),
        (1 - depth, lat),
    ]
    for partner in partners:
        pl.semaphore_signal(
            barrier, inc=1, device_id=partner, device_id_type=pl.DeviceIdType.MESH
        )


def return_kernel(
    n_lat, plan, rows, windows, received, tile,
    partner, row_send, row_recv, swap_send, swap_recv,
):
    depth = lax.axis_index("depth")
    lat = lax.axis_index("lat")
    after = lax.rem(lat + 1, n_lat)
    before = lax.rem(lat + n_lat - 1, n_lat)
    greet(depth, lat, after, before)
    pl.semaphore_wait(pltpu.get_barrier_semaphore(), 4)
    target = jnp.where(depth == 0, after, before)

    def part(c):
        return received.at[c, :, pl.ds(CHUNK, ROWS), :]

    sends = [
        remote(rows.at[s], part(depth), row_send.at[s], row_recv.at[depth], s, target)
        for s in range(2)
    ]
    for copy in sends:
        copy.start()
    swap = remote(windows.at[1 - depth], partner, swap_send, swap_recv, 1 - depth, lat)
    swap.start()
    sum_windows(plan, depth, lambda j, c, at: windows[depth, j, c, at, :], tile, True)
    swap.wait()
    sum_windows(plan, 1 - depth, lambda j, c, at: partner[j, c, at, :], tile, False)
    for copy in sends:
        copy.wait_send()
    for c in range(2):
        remote(rows.at[0], part(c), row_send.at[0], row_recv.at[c], 0, target).wait_recv()


def sum_windows(plan, core, read, tile, first):
    at = jnp.where(core == 0, OWN_LEFT, PREV_RIGHT)
    row = lax.broadcasted_iota(jnp.int32, (8, N), 0)
    lane = lanes()
    jobs = []
    for j in range(MAX_JOBS):
        r = plan[at + 2 + 5 * j]
        low = jnp.where(core == 0, r, 0)
        high = jnp.where(plan[at] > j, jnp.where(core == 0, N, r), 0)
        jobs.append((low, high, plan[at + 2 + 5 * j + 1] * N + plan[at + 2 + 5 * j + 2]))

    def step(g, carry):
        dst = pl.ds(pl.multiple_of(g * 8, 8), 8)
        here = row + g * 8
        for c in range(2):
            values = [
                jnp.where((here >= low) & (here < high), read(j, c, dst), 0.0)
                for j, (low, high, _) in enumerate(jobs)
            ]
            for q in range(tile.shape[2] // N):
                total = None if first else tile[c, dst, q * N : q * N + N]
                for value, (_, _, column) in zip(values, jobs):
                    offset = lane + (q * N - column)
                    inside = (offset >= 0) & (offset < N)
                    value = jnp.where(inside, value, 0.0)
                    total = value if total is None else total + value
                tile[c, dst, q * N : q * N + N] = total
        return carry

    lax.fori_loop(0, N // 8, step, 0)


P_PLUS, P_MINUS, F_EVEN, F_ODD = 0, 1, 2, 3
TURNED = 4


def halves(x):
    hi = x.astype(jnp.bfloat16)
    lo = (x - hi.astype(jnp.float32)).astype(jnp.bfloat16)
    return hi, lo


def dot(a, b):
    return jnp.dot(a, b, preferred_element_type=jnp.float32)


def times_right(x, table, at):
    hi, lo = halves(x)
    return dot(
        jnp.concatenate([hi, lo, hi], axis=1),
        jnp.concatenate([table[at, 0], table[at, 0], table[at, 1]], axis=0),
    )


def times_left(table, at, x):
    hi, lo = halves(x)
    return dot(
        jnp.concatenate([table[at, 0], table[at, 0], table[at, 1]], axis=1),
        jnp.concatenate([hi, lo, hi], axis=0),
    )


def fold_columns(re, im):
    plus = jnp.concatenate([re[:, :HALF] + re[:, HALF:], im[:, :HALF] + im[:, HALF:]], axis=1)
    minus = jnp.concatenate([re[:, :HALF] - re[:, HALF:], im[:, :HALF] - im[:, HALF:]], axis=1)
    return plus, minus


def pair_columns(re, im):
    return (
        jnp.concatenate([re[:, :HALF], im[:, :HALF]], axis=1),
        jnp.concatenate([re[:, HALF:], im[:, HALF:]], axis=1),
    )


def fold_rows(re, im):
    plus = jnp.concatenate([re[:HALF] + re[HALF:], im[:HALF] + im[HALF:]], axis=0)
    minus = jnp.concatenate([re[:HALF] - re[HALF:], im[:HALF] - im[HALF:]], axis=0)
    return plus, minus


def pair_rows(re, im):
    return (
        jnp.concatenate([re[:HALF], im[:HALF]], axis=0),
        jnp.concatenate([re[HALF:], im[HALF:]], axis=0),
    )


def product(u, v):
    return u[0] * v[0] - u[1] * v[1], u[0] * v[1] + u[1] * v[0]


def conj_product(u, v):
    return u[0] * v[0] + u[1] * v[1], u[0] * v[1] - u[1] * v[0]


def both_right(pairs, table, first, second):
    return [(times_right(p, table, first), times_right(m, table, second)) for p, m in pairs]


def both_left(pairs, table, first, second):
    return [(times_left(table, first, p), times_left(table, second, m)) for p, m in pairs]


def unfold(pairs):
    return [(p + m, p - m) for p, m in pairs]


def propagate(fields, table, adjoint):
    left, right = (TURNED, 0) if adjoint else (0, TURNED)
    pairs = [fold_columns(*f) for f in fields]
    pairs = unfold(both_right(pairs, table, right + P_PLUS, right + P_MINUS))
    pairs = [fold_rows(*pair_columns(*p)) for p in pairs]
    pairs = unfold(both_left(pairs, table, left + P_PLUS, left + P_MINUS))
    return [pair_rows(*p) for p in pairs]


def to_spectrum(fields, table):
    pairs = [fold_columns(*f) for f in fields]
    pairs = both_right(pairs, table, TURNED + F_EVEN, TURNED + F_ODD)
    pairs = [fold_rows(*pair_columns(*p)) for p in pairs]
    pairs = both_left(pairs, table, F_EVEN, F_ODD)
    return [pair_rows(*p) for p in pairs]


def from_spectrum(fields, table):
    pairs = [pair_columns(*f) for f in fields]
    pairs = unfold(both_right(pairs, table, F_EVEN, F_ODD))
    pairs = [pair_rows(*pair_columns(*p)) for p in pairs]
    pairs = unfold(both_left(pairs, table, TURNED + F_EVEN, TURNED + F_ODD))
    return [pair_rows(*p) for p in pairs]


def compute_kernel(
    plan, windows, probes, received, measured, table,
    rows_out, grads,
    amplitude,
):
    depth = lax.axis_index("depth")
    at = jnp.where(depth == 0, OWN_LEFT, PREV_RIGHT)
    jobs = plan[at]
    row = lax.broadcasted_iota(jnp.int32, (N, N), 0)

    def work(numbers):
        each = range(len(numbers))
        words = [[plan[at + 2 + 5 * j + w] for w in range(5)] for j in numbers]

        for k in each:
            _, _, _, _, slot = words[k]

            @pl.when(depth == 0)
            def _(k=k, slot=slot):
                amplitude[k] = measured[slot]

            @pl.when(depth == 1)
            def _(k=k):
                src = pl.multiple_of(PAD + (plan[PREV_RIGHT + 1] + 8 * numbers[k]) * 8, 8)
                for s in range(2):
                    for c in range(2):
                        amplitude[k, pl.ds(128 * s + 64 * c, 64), :] = received[
                            s, c, pl.ds(src, 64), :
                        ]

        def base_of(k):
            return jnp.where(depth == 0, 0, lax.div(words[k][0], 8))

        def window(k, s):
            r, _, _, start, _ = words[k]
            here = (row >= jnp.where(depth == 0, r, 0)) & (row < jnp.where(depth == 0, N, r))
            src = pl.multiple_of(PAD + (start - base_of(k)) * 8, 8)
            return [
                jnp.where(here, windows[s, numbers[k], c], received[s, c, pl.ds(src, N), :])
                for c in range(2)
            ]

        turned = [[probes[j, c] for c in range(2)] for j in numbers]
        waves = [product(p, window(k, 0)) for k, p in enumerate(turned)]
        waves = propagate(waves, table, False)
        slices = [window(k, 1) for k in each]
        spectra = to_spectrum([product(w, o) for w, o in zip(waves, slices)], table)
        backs = []
        for k in each:
            re, im = spectra[k]
            factor = 1.0 - amplitude[k] * lax.rsqrt(re * re + im * im + 1.0)
            backs.append((re * factor, im * factor))
        backs = from_spectrum(backs, table)
        for k in each:
            grads[1, numbers[k], 0], grads[1, numbers[k], 1] = conj_product(waves[k], backs[k])
        backs = [conj_product(o, b) for o, b in zip(slices, backs)]
        backs = propagate(backs, table, True)
        for k in each:
            grads[0, numbers[k], 0], grads[0, numbers[k], 1] = conj_product(turned[k], backs[k])
        for k in each:
            r, start = words[k][0], words[k][3]
            base = base_of(k)
            count = jnp.where(depth == 0, lax.div(r + 7, 8), 32 - lax.div(r, 8))

            def step(g, carry, k=k, base=base, start=start):
                src = pl.multiple_of((base + g) * 8, 8)
                dst = pl.multiple_of((start + g) * 8, 8)
                for s in range(2):
                    for c in range(2):
                        rows_out[s, c, pl.ds(dst, 8), :] = grads[
                            s, numbers[k], c, pl.ds(src, 8), :
                        ]
                return carry

            lax.fori_loop(0, count, step, 0)

    @pl.when(jobs >= 2)
    def _():
        work([0, 1])

    @pl.when(lax.rem(jobs, 2) == 1)
    def _():
        work([jobs - 1])


def gather_kernel(plan, rows, tile_in, out, tile, out_sems):
    row = lax.broadcasted_iota(jnp.int32, (CHUNK, N), 0)
    lane = lax.broadcasted_iota(jnp.int32, (CHUNK, N), 1)

    def add(at, j, c, lower):
        r = plan[at + 2 + 5 * j]
        start = plan[at + 2 + 5 * j + 3]
        first = 0 if lower else lax.div(r, CHUNK)
        last = lax.div(r + CHUNK - 1, CHUNK) if lower else N // CHUNK
        skip = 0 if lower else lax.div(r, 8)
        keep = lane >= plan[at + 2 + 5 * j + 2]
        low = pl.multiple_of(plan[at + 2 + 5 * j + 1] * N, N)
        high = pl.multiple_of(plan[at + 2 + 5 * j + 1] * N + N, N)

        def step(g, carry):
            dst = pl.multiple_of(g * CHUNK, CHUNK)
            inside = (row + dst < r) if lower else (row + dst >= r)
            src = pl.multiple_of(CHUNK + (start - skip) * 8 + g * CHUNK, 8)
            value = jnp.where(inside, rows[0 if lower else 1, c, pl.ds(src, CHUNK), :], 0.0)
            tile[c, pl.ds(dst, CHUNK), pl.ds(low, N)] += jnp.where(keep, value, 0.0)
            tile[c, pl.ds(dst, CHUNK), pl.ds(high, N)] += jnp.where(keep, 0.0, value)
            return carry

        lax.fori_loop(first, last, step, 0)

    for c in range(2):
        for at, lower in ((OWN_RIGHT, False), (PREV_LEFT, True)):

            def step(j, carry, at=at, lower=lower, c=c):
                add(at, j, c, lower)
                return carry

            lax.fori_loop(0, plan[at], step, 0)
        pltpu.make_async_copy(tile.at[c], out.at[c], out_sems.at[c]).start()
    for c in range(2):
        pltpu.make_async_copy(tile.at[c], out.at[c], out_sems.at[c]).wait()


SMEM = pl.BlockSpec(memory_space=pltpu.SMEM)
VMEM = pl.BlockSpec(memory_space=pltpu.VMEM)
HBM = pl.BlockSpec(memory_space=pltpu.HBM)


def shape(*dims):
    return jax.ShapeDtypeStruct(dims, jnp.float32)


def shards(n_lat, object_slices, probe, measured, positions, counts):
    columns = object_slices.shape[3]
    tile = object_slices.reshape(object_slices.shape[1:])
    dma = pltpu.SemaphoreType.DMA
    positions = positions.T
    positions, prev_positions, prev_counts, tile, measured = pl.pallas_call(
        functools.partial(announce_kernel, n_lat),
        name="announce",
        out_shape=(
            jax.ShapeDtypeStruct(positions.shape, jnp.int32),
            jax.ShapeDtypeStruct(positions.shape, jnp.int32),
            jax.ShapeDtypeStruct(counts.shape, jnp.int32),
            shape(*tile.shape),
            shape(*measured.shape),
        ),
        in_specs=[HBM, HBM, HBM, HBM],
        out_specs=(VMEM, VMEM, VMEM, VMEM, VMEM),
        scratch_shapes=[
            pltpu.VMEM((4, N, N), jnp.float32),
            pltpu.VMEM((2, N, HALF), jnp.float32),
            dma((2,)), dma((2,)), dma((3,)),
        ],
        compiler_params=pltpu.CompilerParams(
            collective_id=2, has_side_effects=True, vmem_limit_bytes=46 << 20
        ),
    )(positions, counts, tile, measured)
    plan, ahead, behind = pl.pallas_call(
        pack_kernel,
        name="pack",
        out_shape=(
            jax.ShapeDtypeStruct((4 * SPAN,), jnp.int32),
            shape(2, ROWS, N),
            shape(2, ROWS, N),
        ),
        in_specs=[SMEM, SMEM, SMEM, SMEM, VMEM, VMEM],
        out_specs=(SMEM, VMEM, VMEM),
        compiler_params=pltpu.CompilerParams(vmem_limit_bytes=4 << 20),
    )(positions, counts, prev_positions, prev_counts, tile, measured)
    received, windows, probes = pl.pallas_call(
        functools.partial(exchange_kernel, n_lat),
        name="exchange",
        out_shape=(
            shape(2, 2, ROWS + 2 * PAD, N),
            shape(2, MAX_JOBS, 2, N, N),
            shape(MAX_JOBS, 2, N, N),
        ),
        in_specs=[SMEM, VMEM, VMEM, VMEM, VMEM],
        out_specs=(VMEM, VMEM, VMEM),
        scratch_shapes=[
            pltpu.VMEM((2, N, columns), jnp.float32),
            dma((2,)), dma((2,)), dma, dma,
        ],
        compiler_params=pltpu.CompilerParams(
            collective_id=0, has_side_effects=True, vmem_limit_bytes=12 << 20
        ),
    )(plan, ahead, behind, tile, probe)

    table = jnp.asarray(tables())
    rows_out, grads = pl.pallas_call(
        compute_kernel,
        name="compute",
        out_shape=(shape(2, 2, ROWS, N), shape(2, MAX_JOBS, 2, N, N)),
        in_specs=[SMEM, VMEM, VMEM, VMEM, VMEM, VMEM],
        out_specs=(VMEM, VMEM),
        scratch_shapes=[pltpu.VMEM((2, N, N), jnp.float32)],
        compiler_params=pltpu.CompilerParams(vmem_limit_bytes=30 << 20),
    )(plan, windows, probes, received, measured, table)

    rows_back, tile = pl.pallas_call(
        functools.partial(return_kernel, n_lat),
        name="giveback",
        out_shape=(shape(2, 2, ROWS + 2 * CHUNK, N), shape(2, N, columns)),
        in_specs=[SMEM, VMEM, VMEM],
        out_specs=(VMEM, VMEM),
        scratch_shapes=[
            pltpu.VMEM((MAX_JOBS, 2, N, N), jnp.float32),
            dma((2,)), dma((2,)), dma, dma,
        ],
        compiler_params=pltpu.CompilerParams(
            collective_id=1, has_side_effects=True, vmem_limit_bytes=12 << 20
        ),
    )(plan, rows_out, grads)

    out, _ = pl.pallas_call(
        gather_kernel,
        name="gather",
        out_shape=(shape(2, N, columns), shape(2, N, columns)),
        in_specs=[SMEM, VMEM, VMEM],
        out_specs=(HBM, VMEM),
        scratch_shapes=[dma((2,))],
        input_output_aliases={2: 1},
        compiler_params=pltpu.CompilerParams(vmem_limit_bytes=12 << 20),
    )(plan, rows_back, tile)
    return out.reshape(object_slices.shape)


def solution(mesh):
    return jax.shard_map(
        functools.partial(shards, mesh.shape["lat"]),
        mesh=mesh,
        in_specs=(
            P("depth", None, "lat", None),
            P(),
            P("lat", None, None),
            P("lat", None),
            P("lat"),
        ),
        out_specs=P("depth", None, "lat", None),
        check_vma=False,
    )
```

```python
import functools

import jax
import jax.numpy as jnp
import ml_dtypes
import numpy as np
from jax import lax
from jax.experimental import pallas as pl
from jax.experimental.pallas import tpu as pltpu
from jax.sharding import PartitionSpec as P

N = 256
HALF = 128
STRENGTH = 8.0
MAX_JOBS = 3
BUDGET = 48
ROWS = 8 * BUDGET
PAD = 256
CHUNK = 32
SPAN = 20


def split_bf16(a):
    hi = a.astype(np.float32).astype(ml_dtypes.bfloat16)
    lo = (a - hi.astype(np.float64)).astype(np.float32).astype(ml_dtypes.bfloat16)
    return hi, lo


def tables():
    index = np.arange(N)
    angle = 2.0 * np.pi * ((index[:, None] * index[None, :]) % N) / N
    dft = np.exp(-1j * angle) / 16.0
    centred = (index - N * (index >= HALF)) / N
    turn = np.exp(1j * np.pi * STRENGTH * centred**2)
    prop = np.conj(dft) @ (turn[:, None] * dft)
    c0, c1 = prop[:HALF, :HALF], prop[:HALF, HALF:]

    def real_form(m):
        return np.block([[m.real, -m.imag], [m.imag, m.real]])

    forms = [real_form(m) for m in ((c0 + c1) / 2, (c0 - c1) / 2, dft[0::2, :HALF], dft[1::2, :HALF])]
    forms = forms + [m.T for m in forms]
    return np.stack([np.stack(split_bf16(m)) for m in forms])


OWN_LEFT, OWN_RIGHT, PREV_LEFT, PREV_RIGHT = 0, SPAN, 2 * SPAN, 3 * SPAN


def choose_sides(rows_of, cols_of, live):
    up = [lax.div(rows_of[i] + 7, 8) for i in range(4)]
    down = [32 - lax.div(rows_of[i], 8) for i in range(4)]
    best = jnp.int32(1 << 20)
    pick = jnp.int32(0)
    for mask in range(16):
        right = [(mask >> i) & 1 for i in range(4)]
        n_right = sum(right)
        if n_right > MAX_JOBS:
            continue
        top = max([i + 1 for i in range(4) if right[i]], default=0)
        lefts = [jnp.where(live > i, up[i], 0) for i in range(4) if not right[i]]
        cost_left = sum(lefts, jnp.int32(0))
        cost_right = sum([down[i] + 8 for i in range(4) if right[i]], jnp.int32(0))
        widest = jnp.maximum(cost_left, cost_right)
        most = jnp.maximum(live - n_right, n_right)
        bad = (live < top) | (widest > BUDGET) | (most > MAX_JOBS)
        key = most * 64 + widest + jnp.where(bad, jnp.int32(1 << 16), 0)
        pick = jnp.where(key < best, mask, pick)
        best = jnp.minimum(key, best)
    blocks = [jnp.minimum(lax.div(cols_of[i], N), 6) for i in range(4)]
    sides = []
    for side in range(2):
        mine = [(live > i) & ((lax.shift_right_logical(pick, i) & 1) == side) for i in range(4)]
        size = up if side == 0 else down
        count, total = jnp.int32(0), jnp.int32(0)
        words = [[jnp.int32(0)] * 5 for _ in range(MAX_JOBS)]
        for i in range(4):
            fields = [rows_of[i], blocks[i], cols_of[i] - blocks[i] * N, total, jnp.int32(i)]
            for j in range(MAX_JOBS):
                here = mine[i] & (count == j)
                words[j] = [jnp.where(here, f, w) for f, w in zip(fields, words[j])]
            count = count + jnp.where(mine[i], 1, 0)
            total = total + jnp.where(mine[i], size[i], 0)
        sides.append([count, total] + [w for job in words for w in job])
    return sides


def lanes():
    return lax.broadcasted_iota(jnp.int32, (8, N), 1)


def announce_kernel(
    n_lat, pos_hbm, cnt, tile_hbm, measured_hbm,
    own_plan, prev_pos, prev_cnt, tile, apart,
    measured, spread, pos, live, send, recv, local,
):
    depth = lax.axis_index("depth")
    lat = lax.axis_index("lat")
    after = lax.rem(lat + 1, n_lat)
    before = lax.rem(lat + n_lat - 1, n_lat)
    barrier = pltpu.get_barrier_semaphore()
    for other in (after, before):
        pl.semaphore_signal(
            barrier, inc=1, device_id=(depth, other), device_id_type=pl.DeviceIdType.MESH
        )
    loads = [
        pltpu.make_async_copy(measured_hbm, measured, local.at[0]),
        pltpu.make_async_copy(tile_hbm, tile, local.at[1]),
        pltpu.make_async_copy(pos_hbm, pos, local.at[2]),
        pltpu.make_async_copy(cnt, live, local.at[3]),
    ]
    for load in loads:
        load.start()
    pl.semaphore_wait(barrier, 2)
    copies = [
        remote(pos_hbm, prev_pos, send.at[0], recv.at[0], depth, after),
        remote(cnt, prev_cnt, send.at[1], recv.at[1], depth, after),
    ]
    for copy in copies:
        copy.start()
    row = lax.broadcasted_iota(jnp.int32, (N, N), 0)
    lane = lax.broadcasted_iota(jnp.int32, (N, N), 1)
    order = jnp.where(lane < HALF, 2 * lane, 2 * lane - (N - 1))
    shuffle = jnp.where(row == order, 1.0, 0.0).astype(jnp.bfloat16)
    loads[0].wait()
    for slot in range(4):
        hi, lo = halves(measured[slot])
        columns = dot(
            jnp.concatenate([hi, lo], axis=1), jnp.concatenate([shuffle, shuffle], axis=0)
        )
        for h in range(2):
            spread[h] = columns[:, HALF * h : HALF * h + HALF]
        for p in range(2):
            for h in range(2):
                apart[slot, HALF * p : HALF * p + HALF, HALF * h : HALF * h + HALF] = spread[
                    h, pl.ds(p, HALF, stride=2), :
                ]
    for load in loads[2:]:
        load.wait()
    own = choose_sides([pos[0, i] for i in range(4)], [pos[1, i] for i in range(4)], live[0])
    for k, side in enumerate(own):
        for w, word in enumerate(side):
            own_plan[k * SPAN + w] = word
    loads[1].wait()
    for copy in copies:
        copy.wait()


def pack_kernel(
    own_plan, prev_pos, prev_cnt, tile, measured, plan, ahead, behind
):
    depth = lax.axis_index("depth")
    prev = choose_sides(
        [prev_pos[0, i] for i in range(4)], [prev_pos[1, i] for i in range(4)], prev_cnt[0]
    )
    for k, side in enumerate(prev):
        for w, word in enumerate(side):
            plan[k * SPAN + w] = own_plan[k * SPAN + w]
            plan[PREV_LEFT + k * SPAN + w] = word

    def copy_rows(out, at, j, first, count):
        start = plan[at + 2 + 5 * j + 3]
        low = pl.multiple_of(plan[at + 2 + 5 * j + 1] * N, N)
        high = pl.multiple_of(plan[at + 2 + 5 * j + 1] * N + N, N)
        keep = lanes() >= plan[at + 2 + 5 * j + 2]

        def step(g, carry):
            for k in range(4):
                granule = jnp.minimum(4 * g + k, count - 1)
                src = pl.multiple_of((first + granule) * 8, 8)
                dst = pl.multiple_of((start + granule) * 8, 8)
                for c in range(2):
                    out[c, pl.ds(dst, 8), :] = jnp.where(
                        keep,
                        tile[c, pl.ds(src, 8), pl.ds(low, N)],
                        tile[c, pl.ds(src, 8), pl.ds(high, N)],
                    )
            return carry

        lax.fori_loop(0, lax.div(count + 3, 4), step, 0)

    def right_job(j, carry):
        first = lax.div(plan[OWN_RIGHT + 2 + 5 * j], 8)
        copy_rows(ahead, OWN_RIGHT, j, first, 32 - first)
        slot = plan[OWN_RIGHT + 2 + 5 * j + 4]
        dst = pl.multiple_of((plan[OWN_RIGHT + 1] + 8 * j) * 8, 8)
        for c in range(2):
            src = pl.multiple_of(depth * HALF + 64 * c, 64)
            ahead[c, pl.ds(dst, 64), :] = measured[slot, pl.ds(src, 64), :]
        return carry

    lax.fori_loop(0, plan[OWN_RIGHT], right_job, 0)

    def left_job(j, carry):
        copy_rows(behind, PREV_LEFT, j, 0, lax.div(plan[PREV_LEFT + 2 + 5 * j] + 7, 8))
        return carry

    lax.fori_loop(0, plan[PREV_LEFT], left_job, 0)


def exchange_kernel(
    n_lat, plan, ahead, behind, tile, probe, received, windows, probes,
    other, row_send, row_recv, tile_send, tile_recv,
):
    depth = lax.axis_index("depth")
    lat = lax.axis_index("lat")
    after = lax.rem(lat + 1, n_lat)
    before = lax.rem(lat + n_lat - 1, n_lat)
    greet(depth, lat, after, before)
    pl.semaphore_wait(pltpu.get_barrier_semaphore(), 4)

    def slot(s):
        return received.at[s, :, pl.ds(PAD, ROWS), :]

    sends = [
        remote(ahead, slot(depth), row_send.at[0], row_recv.at[depth], 1, after),
        remote(behind, slot(depth), row_send.at[1], row_recv.at[depth], 0, before),
    ]
    for copy in sends:
        copy.start()
    swap = remote(tile, other, tile_send, tile_recv, 1 - depth, lat)
    swap.start()
    at = jnp.where(depth == 0, OWN_LEFT, PREV_RIGHT)
    for j in range(MAX_JOBS):
        shift = plan[at + 2 + 5 * j + 2]
        shift = jnp.where(shift == N, 0, shift)
        for c in range(2):
            probes[j, c] = pltpu.roll(pltpu.roll(probe[c], plan[at + 2 + 5 * j], 0), shift, 1)
    pick_columns(plan, at, tile, windows, depth)
    swap.wait()
    pick_columns(plan, at, other, windows, 1 - depth)
    for copy in sends:
        copy.wait_send()
    for s in range(2):
        remote(ahead, slot(s), row_send.at[0], row_recv.at[s], 1, after).wait_recv()


def pick_columns(plan, at, source, windows, s):
    lane = lanes()
    columns = [
        plan[at + 2 + 5 * j + 1] * N + plan[at + 2 + 5 * j + 2] for j in range(MAX_JOBS)
    ]

    def step(g, carry):
        rows = pl.ds(pl.multiple_of(g * 8, 8), 8)
        for c in range(2):
            picked = [jnp.zeros((8, N), jnp.float32)] * MAX_JOBS
            for q in range(source.shape[2] // N):
                value = source[c, rows, q * N : q * N + N]
                for j, column in enumerate(columns):
                    offset = lane + (q * N - column)
                    picked[j] = jnp.where((offset >= 0) & (offset < N), value, picked[j])
            for j in range(MAX_JOBS):
                windows[s, j, c, rows, :] = picked[j]
        return carry

    lax.fori_loop(0, N // 8, step, 0)


def remote(src, dst, send, recv, depth, lat):
    return pltpu.make_async_remote_copy(
        src_ref=src,
        dst_ref=dst,
        send_sem=send,
        recv_sem=recv,
        device_id=(depth, lat),
        device_id_type=pl.DeviceIdType.MESH,
    )


def greet(depth, lat, after, before):
    barrier = pltpu.get_barrier_semaphore()
    partners = [
        (depth, after),
        (depth, before),
        (1 - depth, jnp.where(depth == 0, after, before)),
        (1 - depth, lat),
    ]
    for partner in partners:
        pl.semaphore_signal(
            barrier, inc=1, device_id=partner, device_id_type=pl.DeviceIdType.MESH
        )


def return_kernel(
    n_lat, plan, rows, windows, received, tile,
    partner, row_send, row_recv, swap_send, swap_recv,
):
    depth = lax.axis_index("depth")
    lat = lax.axis_index("lat")
    after = lax.rem(lat + 1, n_lat)
    before = lax.rem(lat + n_lat - 1, n_lat)
    greet(depth, lat, after, before)
    pl.semaphore_wait(pltpu.get_barrier_semaphore(), 4)
    target = jnp.where(depth == 0, after, before)

    def part(c):
        return received.at[c, :, pl.ds(CHUNK, ROWS), :]

    sends = [
        remote(rows.at[s], part(depth), row_send.at[s], row_recv.at[depth], s, target)
        for s in range(2)
    ]
    for copy in sends:
        copy.start()
    swap = remote(windows.at[1 - depth], partner, swap_send, swap_recv, 1 - depth, lat)
    swap.start()
    sum_windows(plan, depth, lambda j, c, at: windows[depth, j, c, at, :], tile, True)
    swap.wait()
    sum_windows(plan, 1 - depth, lambda j, c, at: partner[j, c, at, :], tile, False)
    for copy in sends:
        copy.wait_send()
    for c in range(2):
        remote(rows.at[0], part(c), row_send.at[0], row_recv.at[c], 0, target).wait_recv()


def sum_windows(plan, core, read, tile, first):
    at = jnp.where(core == 0, OWN_LEFT, PREV_RIGHT)
    row = lax.broadcasted_iota(jnp.int32, (8, N), 0)
    lane = lanes()
    jobs = []
    for j in range(MAX_JOBS):
        r = plan[at + 2 + 5 * j]
        low = jnp.where(core == 0, r, 0)
        high = jnp.where(plan[at] > j, jnp.where(core == 0, N, r), 0)
        jobs.append((low, high, plan[at + 2 + 5 * j + 1] * N + plan[at + 2 + 5 * j + 2]))

    def step(g, carry):
        dst = pl.ds(pl.multiple_of(g * 8, 8), 8)
        here = row + g * 8
        for c in range(2):
            values = [
                jnp.where((here >= low) & (here < high), read(j, c, dst), 0.0)
                for j, (low, high, _) in enumerate(jobs)
            ]
            for q in range(tile.shape[2] // N):
                total = None if first else tile[c, dst, q * N : q * N + N]
                for value, (_, _, column) in zip(values, jobs):
                    offset = lane + (q * N - column)
                    inside = (offset >= 0) & (offset < N)
                    value = jnp.where(inside, value, 0.0)
                    total = value if total is None else total + value
                tile[c, dst, q * N : q * N + N] = total
        return carry

    lax.fori_loop(0, N // 8, step, 0)


P_PLUS, P_MINUS, F_EVEN, F_ODD = 0, 1, 2, 3
TURNED = 4


def halves(x):
    hi = x.astype(jnp.bfloat16)
    lo = (x - hi.astype(jnp.float32)).astype(jnp.bfloat16)
    return hi, lo


def dot(a, b):
    return jnp.dot(a, b, preferred_element_type=jnp.float32)


def times_right(x, table, at):
    hi, lo = halves(x)
    return dot(
        jnp.concatenate([hi, lo, hi], axis=1),
        jnp.concatenate([table[at, 0], table[at, 0], table[at, 1]], axis=0),
    )


def times_left(table, at, x):
    hi, lo = halves(x)
    return dot(
        jnp.concatenate([table[at, 0], table[at, 0], table[at, 1]], axis=1),
        jnp.concatenate([hi, lo, hi], axis=0),
    )


def fold_columns(re, im):
    plus = jnp.concatenate([re[:, :HALF] + re[:, HALF:], im[:, :HALF] + im[:, HALF:]], axis=1)
    minus = jnp.concatenate([re[:, :HALF] - re[:, HALF:], im[:, :HALF] - im[:, HALF:]], axis=1)
    return plus, minus


def pair_columns(re, im):
    return (
        jnp.concatenate([re[:, :HALF], im[:, :HALF]], axis=1),
        jnp.concatenate([re[:, HALF:], im[:, HALF:]], axis=1),
    )


def fold_rows(re, im):
    plus = jnp.concatenate([re[:HALF] + re[HALF:], im[:HALF] + im[HALF:]], axis=0)
    minus = jnp.concatenate([re[:HALF] - re[HALF:], im[:HALF] - im[HALF:]], axis=0)
    return plus, minus


def pair_rows(re, im):
    return (
        jnp.concatenate([re[:HALF], im[:HALF]], axis=0),
        jnp.concatenate([re[HALF:], im[HALF:]], axis=0),
    )


def product(u, v):
    return u[0] * v[0] - u[1] * v[1], u[0] * v[1] + u[1] * v[0]


def conj_product(u, v):
    return u[0] * v[0] + u[1] * v[1], u[0] * v[1] - u[1] * v[0]


def both_right(pairs, table, first, second):
    return [(times_right(p, table, first), times_right(m, table, second)) for p, m in pairs]


def both_left(pairs, table, first, second):
    return [(times_left(table, first, p), times_left(table, second, m)) for p, m in pairs]


def unfold(pairs):
    return [(p + m, p - m) for p, m in pairs]


def propagate(fields, table, adjoint):
    left, right = (TURNED, 0) if adjoint else (0, TURNED)
    pairs = [fold_columns(*f) for f in fields]
    pairs = unfold(both_right(pairs, table, right + P_PLUS, right + P_MINUS))
    pairs = [fold_rows(*pair_columns(*p)) for p in pairs]
    pairs = unfold(both_left(pairs, table, left + P_PLUS, left + P_MINUS))
    return [pair_rows(*p) for p in pairs]


def to_spectrum(fields, table):
    pairs = [fold_columns(*f) for f in fields]
    pairs = both_right(pairs, table, TURNED + F_EVEN, TURNED + F_ODD)
    pairs = [fold_rows(*pair_columns(*p)) for p in pairs]
    pairs = both_left(pairs, table, F_EVEN, F_ODD)
    return [pair_rows(*p) for p in pairs]


def from_spectrum(fields, table):
    pairs = [pair_columns(*f) for f in fields]
    pairs = unfold(both_right(pairs, table, F_EVEN, F_ODD))
    pairs = [pair_rows(*pair_columns(*p)) for p in pairs]
    pairs = unfold(both_left(pairs, table, TURNED + F_EVEN, TURNED + F_ODD))
    return [pair_rows(*p) for p in pairs]


def compute_kernel(
    plan, windows, probes, received, measured, table,
    rows_out, grads,
    amplitude,
):
    depth = lax.axis_index("depth")
    at = jnp.where(depth == 0, OWN_LEFT, PREV_RIGHT)
    jobs = plan[at]
    row = lax.broadcasted_iota(jnp.int32, (N, N), 0)

    def work(numbers):
        each = range(len(numbers))
        words = [[plan[at + 2 + 5 * j + w] for w in range(5)] for j in numbers]

        for k in each:
            _, _, _, _, slot = words[k]

            @pl.when(depth == 0)
            def _(k=k, slot=slot):
                amplitude[k] = measured[slot]

            @pl.when(depth == 1)
            def _(k=k):
                src = pl.multiple_of(PAD + (plan[PREV_RIGHT + 1] + 8 * numbers[k]) * 8, 8)
                for s in range(2):
                    for c in range(2):
                        amplitude[k, pl.ds(128 * s + 64 * c, 64), :] = received[
                            s, c, pl.ds(src, 64), :
                        ]

        def base_of(k):
            return jnp.where(depth == 0, 0, lax.div(words[k][0], 8))

        def window(k, s):
            r, _, _, start, _ = words[k]
            here = (row >= jnp.where(depth == 0, r, 0)) & (row < jnp.where(depth == 0, N, r))
            src = pl.multiple_of(PAD + (start - base_of(k)) * 8, 8)
            return [
                jnp.where(here, windows[s, numbers[k], c], received[s, c, pl.ds(src, N), :])
                for c in range(2)
            ]

        turned = [[probes[j, c] for c in range(2)] for j in numbers]
        waves = [product(p, window(k, 0)) for k, p in enumerate(turned)]
        waves = propagate(waves, table, False)
        slices = [window(k, 1) for k in each]
        spectra = to_spectrum([product(w, o) for w, o in zip(waves, slices)], table)
        backs = []
        for k in each:
            re, im = spectra[k]
            factor = 1.0 - amplitude[k] * lax.rsqrt(re * re + im * im + 1.0)
            backs.append((re * factor, im * factor))
        backs = from_spectrum(backs, table)
        for k in each:
            grads[1, numbers[k], 0], grads[1, numbers[k], 1] = conj_product(waves[k], backs[k])
        backs = [conj_product(o, b) for o, b in zip(slices, backs)]
        backs = propagate(backs, table, True)
        for k in each:
            grads[0, numbers[k], 0], grads[0, numbers[k], 1] = conj_product(turned[k], backs[k])
        for k in each:
            r, start = words[k][0], words[k][3]
            base = base_of(k)
            count = jnp.where(depth == 0, lax.div(r + 7, 8), 32 - lax.div(r, 8))

            def step(g, carry, k=k, base=base, start=start, count=count):
                for q in range(4):
                    granule = jnp.minimum(4 * g + q, count - 1)
                    src = pl.multiple_of((base + granule) * 8, 8)
                    dst = pl.multiple_of((start + granule) * 8, 8)
                    for s in range(2):
                        for c in range(2):
                            rows_out[s, c, pl.ds(dst, 8), :] = grads[
                                s, numbers[k], c, pl.ds(src, 8), :
                            ]
                return carry

            lax.fori_loop(0, lax.div(count + 3, 4), step, 0)

    @pl.when(jobs >= 2)
    def _():
        work([0, 1])

    @pl.when(lax.rem(jobs, 2) == 1)
    def _():
        work([jobs - 1])


def gather_kernel(plan, rows, tile_in, out, tile, out_sems):
    row = lax.broadcasted_iota(jnp.int32, (CHUNK, N), 0)
    lane = lax.broadcasted_iota(jnp.int32, (CHUNK, N), 1)

    def add(at, j, c, lower):
        r = plan[at + 2 + 5 * j]
        start = plan[at + 2 + 5 * j + 3]
        first = 0 if lower else lax.div(r, CHUNK)
        last = lax.div(r + CHUNK - 1, CHUNK) if lower else N // CHUNK
        skip = 0 if lower else lax.div(r, 8)
        keep = lane >= plan[at + 2 + 5 * j + 2]
        low = pl.multiple_of(plan[at + 2 + 5 * j + 1] * N, N)
        high = pl.multiple_of(plan[at + 2 + 5 * j + 1] * N + N, N)

        def step(g, carry):
            dst = pl.multiple_of(g * CHUNK, CHUNK)
            inside = (row + dst < r) if lower else (row + dst >= r)
            src = pl.multiple_of(CHUNK + (start - skip) * 8 + g * CHUNK, 8)
            value = jnp.where(inside, rows[0 if lower else 1, c, pl.ds(src, CHUNK), :], 0.0)
            tile[c, pl.ds(dst, CHUNK), pl.ds(low, N)] += jnp.where(keep, value, 0.0)
            tile[c, pl.ds(dst, CHUNK), pl.ds(high, N)] += jnp.where(keep, 0.0, value)
            return carry

        lax.fori_loop(first, last, step, 0)

    for c in range(2):
        for at, lower in ((OWN_RIGHT, False), (PREV_LEFT, True)):

            def step(j, carry, at=at, lower=lower, c=c):
                add(at, j, c, lower)
                return carry

            lax.fori_loop(0, plan[at], step, 0)
        pltpu.make_async_copy(tile.at[c], out.at[c], out_sems.at[c]).start()
    for c in range(2):
        pltpu.make_async_copy(tile.at[c], out.at[c], out_sems.at[c]).wait()


SMEM = pl.BlockSpec(memory_space=pltpu.SMEM)
VMEM = pl.BlockSpec(memory_space=pltpu.VMEM)
HBM = pl.BlockSpec(memory_space=pltpu.HBM)


def shape(*dims):
    return jax.ShapeDtypeStruct(dims, jnp.float32)


def shards(n_lat, object_slices, probe, measured, positions, counts):
    columns = object_slices.shape[3]
    tile = object_slices.reshape(object_slices.shape[1:])
    dma = pltpu.SemaphoreType.DMA
    positions = positions.T
    own_plan, prev_positions, prev_counts, tile, measured = pl.pallas_call(
        functools.partial(announce_kernel, n_lat),
        name="announce",
        out_shape=(
            jax.ShapeDtypeStruct((2 * SPAN,), jnp.int32),
            jax.ShapeDtypeStruct(positions.shape, jnp.int32),
            jax.ShapeDtypeStruct(counts.shape, jnp.int32),
            shape(*tile.shape),
            shape(*measured.shape),
        ),
        in_specs=[HBM, HBM, HBM, HBM],
        out_specs=(SMEM, VMEM, VMEM, VMEM, VMEM),
        scratch_shapes=[
            pltpu.VMEM((4, N, N), jnp.float32),
            pltpu.VMEM((2, N, HALF), jnp.float32),
            pltpu.SMEM((2, 4), jnp.int32),
            pltpu.SMEM((1,), jnp.int32),
            dma((2,)), dma((2,)), dma((4,)),
        ],
        compiler_params=pltpu.CompilerParams(
            collective_id=2, has_side_effects=True, vmem_limit_bytes=46 << 20
        ),
    )(positions, counts, tile, measured)
    plan, ahead, behind = pl.pallas_call(
        pack_kernel,
        name="pack",
        out_shape=(
            jax.ShapeDtypeStruct((4 * SPAN,), jnp.int32),
            shape(2, ROWS, N),
            shape(2, ROWS, N),
        ),
        in_specs=[SMEM, SMEM, SMEM, VMEM, VMEM],
        out_specs=(SMEM, VMEM, VMEM),
        compiler_params=pltpu.CompilerParams(vmem_limit_bytes=4 << 20),
    )(own_plan, prev_positions, prev_counts, tile, measured)
    received, windows, probes = pl.pallas_call(
        functools.partial(exchange_kernel, n_lat),
        name="exchange",
        out_shape=(
            shape(2, 2, ROWS + 2 * PAD, N),
            shape(2, MAX_JOBS, 2, N, N),
            shape(MAX_JOBS, 2, N, N),
        ),
        in_specs=[SMEM, VMEM, VMEM, VMEM, VMEM],
        out_specs=(VMEM, VMEM, VMEM),
        scratch_shapes=[
            pltpu.VMEM((2, N, columns), jnp.float32),
            dma((2,)), dma((2,)), dma, dma,
        ],
        compiler_params=pltpu.CompilerParams(
            collective_id=0, has_side_effects=True, vmem_limit_bytes=12 << 20
        ),
    )(plan, ahead, behind, tile, probe)

    table = jnp.asarray(tables())
    rows_out, grads = pl.pallas_call(
        compute_kernel,
        name="compute",
        out_shape=(shape(2, 2, ROWS, N), shape(2, MAX_JOBS, 2, N, N)),
        in_specs=[SMEM, VMEM, VMEM, VMEM, VMEM, VMEM],
        out_specs=(VMEM, VMEM),
        scratch_shapes=[pltpu.VMEM((2, N, N), jnp.float32)],
        compiler_params=pltpu.CompilerParams(vmem_limit_bytes=30 << 20),
    )(plan, windows, probes, received, measured, table)

    rows_back, tile = pl.pallas_call(
        functools.partial(return_kernel, n_lat),
        name="giveback",
        out_shape=(shape(2, 2, ROWS + 2 * CHUNK, N), shape(2, N, columns)),
        in_specs=[SMEM, VMEM, VMEM],
        out_specs=(VMEM, VMEM),
        scratch_shapes=[
            pltpu.VMEM((MAX_JOBS, 2, N, N), jnp.float32),
            dma((2,)), dma((2,)), dma, dma,
        ],
        compiler_params=pltpu.CompilerParams(
            collective_id=1, has_side_effects=True, vmem_limit_bytes=12 << 20
        ),
    )(plan, rows_out, grads)

    out, _ = pl.pallas_call(
        gather_kernel,
        name="gather",
        out_shape=(shape(2, N, columns), shape(2, N, columns)),
        in_specs=[SMEM, VMEM, VMEM],
        out_specs=(HBM, VMEM),
        scratch_shapes=[dma((2,))],
        input_output_aliases={2: 1},
        compiler_params=pltpu.CompilerParams(vmem_limit_bytes=12 << 20),
    )(plan, rows_back, tile)
    return out.reshape(object_slices.shape)


def solution(mesh):
    return jax.shard_map(
        functools.partial(shards, mesh.shape["lat"]),
        mesh=mesh,
        in_specs=(
            P("depth", None, "lat", None),
            P(),
            P("lat", None, None),
            P("lat", None),
            P("lat"),
        ),
        out_specs=P("depth", None, "lat", None),
        check_vma=False,
    )
```

```python
import functools

import jax
import jax.numpy as jnp
import ml_dtypes
import numpy as np
from jax import lax
from jax.experimental import pallas as pl
from jax.experimental.pallas import tpu as pltpu
from jax.sharding import PartitionSpec as P

N = 256
HALF = 128
STRENGTH = 8.0
MAX_JOBS = 3
BUDGET = 48
ROWS = 8 * BUDGET
PAD = 256
CHUNK = 32
SPAN = 20


def split_bf16(a):
    hi = a.astype(np.float32).astype(ml_dtypes.bfloat16)
    lo = (a - hi.astype(np.float64)).astype(np.float32).astype(ml_dtypes.bfloat16)
    return hi, lo


def tables():
    index = np.arange(N)
    angle = 2.0 * np.pi * ((index[:, None] * index[None, :]) % N) / N
    dft = np.exp(-1j * angle) / 16.0
    centred = (index - N * (index >= HALF)) / N
    turn = np.exp(1j * np.pi * STRENGTH * centred**2)
    prop = np.conj(dft) @ (turn[:, None] * dft)
    c0, c1 = prop[:HALF, :HALF], prop[:HALF, HALF:]

    def real_form(m):
        return np.block([[m.real, -m.imag], [m.imag, m.real]])

    forms = [real_form(m) for m in ((c0 + c1) / 2, (c0 - c1) / 2, dft[0::2, :HALF], dft[1::2, :HALF])]
    forms = forms + [m.T for m in forms]
    return np.stack([np.stack(split_bf16(m)) for m in forms])


OWN_LEFT, OWN_RIGHT, PREV_LEFT, PREV_RIGHT = 0, SPAN, 2 * SPAN, 3 * SPAN


def choose_sides(rows_of, cols_of, live):
    up = [lax.div(rows_of[i] + 7, 8) for i in range(4)]
    down = [32 - lax.div(rows_of[i], 8) for i in range(4)]
    best = jnp.int32(1 << 20)
    pick = jnp.int32(0)
    for mask in range(16):
        right = [(mask >> i) & 1 for i in range(4)]
        n_right = sum(right)
        if n_right > MAX_JOBS:
            continue
        top = max([i + 1 for i in range(4) if right[i]], default=0)
        lefts = [jnp.where(live > i, up[i], 0) for i in range(4) if not right[i]]
        cost_left = sum(lefts, jnp.int32(0))
        cost_right = sum([down[i] + 8 for i in range(4) if right[i]], jnp.int32(0))
        widest = jnp.maximum(cost_left, cost_right)
        most = jnp.maximum(live - n_right, n_right)
        bad = (live < top) | (widest > BUDGET) | (most > MAX_JOBS)
        key = most * 64 + widest + jnp.where(bad, jnp.int32(1 << 16), 0)
        pick = jnp.where(key < best, mask, pick)
        best = jnp.minimum(key, best)
    blocks = [jnp.minimum(lax.div(cols_of[i], N), 6) for i in range(4)]
    sides = []
    for side in range(2):
        mine = [(live > i) & ((lax.shift_right_logical(pick, i) & 1) == side) for i in range(4)]
        size = up if side == 0 else down
        count, total = jnp.int32(0), jnp.int32(0)
        words = [[jnp.int32(0)] * 5 for _ in range(MAX_JOBS)]
        for i in range(4):
            fields = [rows_of[i], blocks[i], cols_of[i] - blocks[i] * N, total, jnp.int32(i)]
            for j in range(MAX_JOBS):
                here = mine[i] & (count == j)
                words[j] = [jnp.where(here, f, w) for f, w in zip(fields, words[j])]
            count = count + jnp.where(mine[i], 1, 0)
            total = total + jnp.where(mine[i], size[i], 0)
        sides.append([count, total] + [w for job in words for w in job])
    return sides


def lanes():
    return lax.broadcasted_iota(jnp.int32, (8, N), 1)


def announce_kernel(
    n_lat, pos_hbm, cnt, tile_hbm, measured_hbm,
    own_plan, prev_pos, prev_cnt, tile, apart,
    measured, spread, pos, live, send, recv, local,
):
    depth = lax.axis_index("depth")
    lat = lax.axis_index("lat")
    after = lax.rem(lat + 1, n_lat)
    before = lax.rem(lat + n_lat - 1, n_lat)
    barrier = pltpu.get_barrier_semaphore()
    for other in (after, before):
        pl.semaphore_signal(
            barrier, inc=1, device_id=(depth, other), device_id_type=pl.DeviceIdType.MESH
        )
    loads = [
        pltpu.make_async_copy(measured_hbm, measured, local.at[0]),
        pltpu.make_async_copy(tile_hbm, tile, local.at[1]),
        pltpu.make_async_copy(pos_hbm, pos, local.at[2]),
        pltpu.make_async_copy(cnt, live, local.at[3]),
    ]
    for load in loads:
        load.start()
    pl.semaphore_wait(barrier, 2)
    copies = [
        remote(pos_hbm, prev_pos, send.at[0], recv.at[0], depth, after),
        remote(cnt, prev_cnt, send.at[1], recv.at[1], depth, after),
    ]
    for copy in copies:
        copy.start()
    row = lax.broadcasted_iota(jnp.int32, (N, N), 0)
    lane = lax.broadcasted_iota(jnp.int32, (N, N), 1)
    order = jnp.where(lane < HALF, 2 * lane, 2 * lane - (N - 1))
    shuffle = jnp.where(row == order, 1.0, 0.0).astype(jnp.bfloat16)
    loads[0].wait()
    def rearrange(slot, carry):
        hi, lo = halves(measured[slot])
        columns = dot(
            jnp.concatenate([hi, lo], axis=1), jnp.concatenate([shuffle, shuffle], axis=0)
        )
        for h in range(2):
            spread[h] = columns[:, HALF * h : HALF * h + HALF]
        for p in range(2):
            for h in range(2):
                apart[slot, HALF * p : HALF * p + HALF, HALF * h : HALF * h + HALF] = spread[
                    h, pl.ds(p, HALF, stride=2), :
                ]
        return carry

    lax.fori_loop(0, 4, rearrange, 0)
    for load in loads[2:]:
        load.wait()
    own = choose_sides([pos[0, i] for i in range(4)], [pos[1, i] for i in range(4)], live[0])
    for k, side in enumerate(own):
        for w, word in enumerate(side):
            own_plan[k * SPAN + w] = word
    loads[1].wait()
    for copy in copies:
        copy.wait()


def pack_kernel(
    own_plan, prev_pos, prev_cnt, tile, measured, plan, ahead, behind
):
    depth = lax.axis_index("depth")
    prev = choose_sides(
        [prev_pos[0, i] for i in range(4)], [prev_pos[1, i] for i in range(4)], prev_cnt[0]
    )
    for k, side in enumerate(prev):
        for w, word in enumerate(side):
            plan[k * SPAN + w] = own_plan[k * SPAN + w]
            plan[PREV_LEFT + k * SPAN + w] = word

    def copy_rows(out, at, j, first, count):
        start = plan[at + 2 + 5 * j + 3]
        low = pl.multiple_of(plan[at + 2 + 5 * j + 1] * N, N)
        high = pl.multiple_of(plan[at + 2 + 5 * j + 1] * N + N, N)
        keep = lanes() >= plan[at + 2 + 5 * j + 2]

        def step(g, carry):
            for k in range(4):
                granule = jnp.minimum(4 * g + k, count - 1)
                src = pl.multiple_of((first + granule) * 8, 8)
                dst = pl.multiple_of((start + granule) * 8, 8)
                for c in range(2):
                    out[c, pl.ds(dst, 8), :] = jnp.where(
                        keep,
                        tile[c, pl.ds(src, 8), pl.ds(low, N)],
                        tile[c, pl.ds(src, 8), pl.ds(high, N)],
                    )
            return carry

        lax.fori_loop(0, lax.div(count + 3, 4), step, 0)

    def right_job(j, carry):
        first = lax.div(plan[OWN_RIGHT + 2 + 5 * j], 8)
        copy_rows(ahead, OWN_RIGHT, j, first, 32 - first)
        slot = plan[OWN_RIGHT + 2 + 5 * j + 4]
        dst = pl.multiple_of((plan[OWN_RIGHT + 1] + 8 * j) * 8, 8)
        for c in range(2):
            src = pl.multiple_of(depth * HALF + 64 * c, 64)
            ahead[c, pl.ds(dst, 64), :] = measured[slot, pl.ds(src, 64), :]
        return carry

    lax.fori_loop(0, plan[OWN_RIGHT], right_job, 0)

    def left_job(j, carry):
        copy_rows(behind, PREV_LEFT, j, 0, lax.div(plan[PREV_LEFT + 2 + 5 * j] + 7, 8))
        return carry

    lax.fori_loop(0, plan[PREV_LEFT], left_job, 0)


def exchange_kernel(
    n_lat, plan, ahead, behind, tile, probe, received, windows, probes,
    other, row_send, row_recv, tile_send, tile_recv,
):
    depth = lax.axis_index("depth")
    lat = lax.axis_index("lat")
    after = lax.rem(lat + 1, n_lat)
    before = lax.rem(lat + n_lat - 1, n_lat)
    greet(depth, lat, after, before)
    pl.semaphore_wait(pltpu.get_barrier_semaphore(), 4)

    def slot(s):
        return received.at[s, :, pl.ds(PAD, ROWS), :]

    sends = [
        remote(ahead, slot(depth), row_send.at[0], row_recv.at[depth], 1, after),
        remote(behind, slot(depth), row_send.at[1], row_recv.at[depth], 0, before),
    ]
    for copy in sends:
        copy.start()
    swap = remote(tile, other, tile_send, tile_recv, 1 - depth, lat)
    swap.start()
    at = jnp.where(depth == 0, OWN_LEFT, PREV_RIGHT)
    def turn(i, carry):
        j, c = lax.div(i, 2), lax.rem(i, 2)
        shift = plan[at + 2 + 5 * j + 2]
        shift = jnp.where(shift == N, 0, shift)
        probes[j, c] = pltpu.roll(pltpu.roll(probe[c], plan[at + 2 + 5 * j], 0), shift, 1)
        return carry

    lax.fori_loop(0, 2 * MAX_JOBS, turn, 0)
    pick_columns(plan, at, tile, windows, depth)
    swap.wait()
    pick_columns(plan, at, other, windows, 1 - depth)
    for copy in sends:
        copy.wait_send()
    for s in range(2):
        remote(ahead, slot(s), row_send.at[0], row_recv.at[s], 1, after).wait_recv()


def pick_columns(plan, at, source, windows, s):
    lane = lanes()
    columns = [
        plan[at + 2 + 5 * j + 1] * N + plan[at + 2 + 5 * j + 2] for j in range(MAX_JOBS)
    ]

    def step(g, carry):
        rows = pl.ds(pl.multiple_of(g * 8, 8), 8)
        for c in range(2):
            picked = [jnp.zeros((8, N), jnp.float32)] * MAX_JOBS
            for q in range(source.shape[2] // N):
                value = source[c, rows, q * N : q * N + N]
                for j, column in enumerate(columns):
                    offset = lane + (q * N - column)
                    picked[j] = jnp.where((offset >= 0) & (offset < N), value, picked[j])
            for j in range(MAX_JOBS):
                windows[s, j, c, rows, :] = picked[j]
        return carry

    lax.fori_loop(0, N // 8, step, 0)


def remote(src, dst, send, recv, depth, lat):
    return pltpu.make_async_remote_copy(
        src_ref=src,
        dst_ref=dst,
        send_sem=send,
        recv_sem=recv,
        device_id=(depth, lat),
        device_id_type=pl.DeviceIdType.MESH,
    )


def greet(depth, lat, after, before):
    barrier = pltpu.get_barrier_semaphore()
    partners = [
        (depth, after),
        (depth, before),
        (1 - depth, jnp.where(depth == 0, after, before)),
        (1 - depth, lat),
    ]
    for partner in partners:
        pl.semaphore_signal(
            barrier, inc=1, device_id=partner, device_id_type=pl.DeviceIdType.MESH
        )


def return_kernel(
    n_lat, plan, rows, windows, received, tile,
    partner, row_send, row_recv, swap_send, swap_recv,
):
    depth = lax.axis_index("depth")
    lat = lax.axis_index("lat")
    after = lax.rem(lat + 1, n_lat)
    before = lax.rem(lat + n_lat - 1, n_lat)
    greet(depth, lat, after, before)
    pl.semaphore_wait(pltpu.get_barrier_semaphore(), 4)
    target = jnp.where(depth == 0, after, before)

    def part(c):
        return received.at[c, :, pl.ds(CHUNK, ROWS), :]

    sends = [
        remote(rows.at[s], part(depth), row_send.at[s], row_recv.at[depth], s, target)
        for s in range(2)
    ]
    for copy in sends:
        copy.start()
    swap = remote(windows.at[1 - depth], partner, swap_send, swap_recv, 1 - depth, lat)
    swap.start()
    sum_windows(plan, depth, lambda j, c, at: windows[depth, j, c, at, :], tile, True)
    swap.wait()
    sum_windows(plan, 1 - depth, lambda j, c, at: partner[j, c, at, :], tile, False)
    for copy in sends:
        copy.wait_send()
    for c in range(2):
        remote(rows.at[0], part(c), row_send.at[0], row_recv.at[c], 0, target).wait_recv()


def sum_windows(plan, core, read, tile, first):
    at = jnp.where(core == 0, OWN_LEFT, PREV_RIGHT)
    row = lax.broadcasted_iota(jnp.int32, (8, N), 0)
    lane = lanes()
    jobs = []
    for j in range(MAX_JOBS):
        r = plan[at + 2 + 5 * j]
        low = jnp.where(core == 0, r, 0)
        high = jnp.where(plan[at] > j, jnp.where(core == 0, N, r), 0)
        jobs.append((low, high, plan[at + 2 + 5 * j + 1] * N + plan[at + 2 + 5 * j + 2]))

    def step(g, carry):
        dst = pl.ds(pl.multiple_of(g * 8, 8), 8)
        here = row + g * 8
        for c in range(2):
            values = [
                jnp.where((here >= low) & (here < high), read(j, c, dst), 0.0)
                for j, (low, high, _) in enumerate(jobs)
            ]
            for q in range(tile.shape[2] // N):
                total = None if first else tile[c, dst, q * N : q * N + N]
                for value, (_, _, column) in zip(values, jobs):
                    offset = lane + (q * N - column)
                    inside = (offset >= 0) & (offset < N)
                    value = jnp.where(inside, value, 0.0)
                    total = value if total is None else total + value
                tile[c, dst, q * N : q * N + N] = total
        return carry

    lax.fori_loop(0, N // 8, step, 0)


P_PLUS, P_MINUS, F_EVEN, F_ODD = 0, 1, 2, 3
TURNED = 4


def halves(x):
    hi = x.astype(jnp.bfloat16)
    lo = (x - hi.astype(jnp.float32)).astype(jnp.bfloat16)
    return hi, lo


def dot(a, b):
    return jnp.dot(a, b, preferred_element_type=jnp.float32)


def times_right(x, table, at):
    hi, lo = halves(x)
    return dot(
        jnp.concatenate([hi, lo, hi], axis=1),
        jnp.concatenate([table[at, 0], table[at, 0], table[at, 1]], axis=0),
    )


def times_left(table, at, x):
    hi, lo = halves(x)
    return dot(
        jnp.concatenate([table[at, 0], table[at, 0], table[at, 1]], axis=1),
        jnp.concatenate([hi, lo, hi], axis=0),
    )


def fold_columns(re, im):
    plus = jnp.concatenate([re[:, :HALF] + re[:, HALF:], im[:, :HALF] + im[:, HALF:]], axis=1)
    minus = jnp.concatenate([re[:, :HALF] - re[:, HALF:], im[:, :HALF] - im[:, HALF:]], axis=1)
    return plus, minus


def pair_columns(re, im):
    return (
        jnp.concatenate([re[:, :HALF], im[:, :HALF]], axis=1),
        jnp.concatenate([re[:, HALF:], im[:, HALF:]], axis=1),
    )


def fold_rows(re, im):
    plus = jnp.concatenate([re[:HALF] + re[HALF:], im[:HALF] + im[HALF:]], axis=0)
    minus = jnp.concatenate([re[:HALF] - re[HALF:], im[:HALF] - im[HALF:]], axis=0)
    return plus, minus


def pair_rows(re, im):
    return (
        jnp.concatenate([re[:HALF], im[:HALF]], axis=0),
        jnp.concatenate([re[HALF:], im[HALF:]], axis=0),
    )


def product(u, v):
    return u[0] * v[0] - u[1] * v[1], u[0] * v[1] + u[1] * v[0]


def conj_product(u, v):
    return u[0] * v[0] + u[1] * v[1], u[0] * v[1] - u[1] * v[0]


def both_right(pairs, table, first, second):
    return [(times_right(p, table, first), times_right(m, table, second)) for p, m in pairs]


def both_left(pairs, table, first, second):
    return [(times_left(table, first, p), times_left(table, second, m)) for p, m in pairs]


def unfold(pairs):
    return [(p + m, p - m) for p, m in pairs]


def propagate(fields, table, adjoint):
    left, right = (TURNED, 0) if adjoint else (0, TURNED)
    pairs = [fold_columns(*f) for f in fields]
    pairs = unfold(both_right(pairs, table, right + P_PLUS, right + P_MINUS))
    pairs = [fold_rows(*pair_columns(*p)) for p in pairs]
    pairs = unfold(both_left(pairs, table, left + P_PLUS, left + P_MINUS))
    return [pair_rows(*p) for p in pairs]


def to_spectrum(fields, table):
    pairs = [fold_columns(*f) for f in fields]
    pairs = both_right(pairs, table, TURNED + F_EVEN, TURNED + F_ODD)
    pairs = [fold_rows(*pair_columns(*p)) for p in pairs]
    pairs = both_left(pairs, table, F_EVEN, F_ODD)
    return [pair_rows(*p) for p in pairs]


def from_spectrum(fields, table):
    pairs = [pair_columns(*f) for f in fields]
    pairs = unfold(both_right(pairs, table, F_EVEN, F_ODD))
    pairs = [pair_rows(*pair_columns(*p)) for p in pairs]
    pairs = unfold(both_left(pairs, table, TURNED + F_EVEN, TURNED + F_ODD))
    return [pair_rows(*p) for p in pairs]


def compute_kernel(
    plan, windows, probes, received, measured, table,
    rows_out, grads,
    amplitude,
):
    depth = lax.axis_index("depth")
    at = jnp.where(depth == 0, OWN_LEFT, PREV_RIGHT)
    jobs = plan[at]
    row = lax.broadcasted_iota(jnp.int32, (N, N), 0)

    def work(numbers):
        each = range(len(numbers))
        words = [[plan[at + 2 + 5 * j + w] for w in range(5)] for j in numbers]

        for k in each:
            _, _, _, _, slot = words[k]

            @pl.when(depth == 0)
            def _(k=k, slot=slot):
                amplitude[k] = measured[slot]

            @pl.when(depth == 1)
            def _(k=k):
                src = pl.multiple_of(PAD + (plan[PREV_RIGHT + 1] + 8 * numbers[k]) * 8, 8)
                for s in range(2):
                    for c in range(2):
                        amplitude[k, pl.ds(128 * s + 64 * c, 64), :] = received[
                            s, c, pl.ds(src, 64), :
                        ]

        def base_of(k):
            return jnp.where(depth == 0, 0, lax.div(words[k][0], 8))

        def window(k, s):
            r, _, _, start, _ = words[k]
            here = (row >= jnp.where(depth == 0, r, 0)) & (row < jnp.where(depth == 0, N, r))
            src = pl.multiple_of(PAD + (start - base_of(k)) * 8, 8)
            return [
                jnp.where(here, windows[s, numbers[k], c], received[s, c, pl.ds(src, N), :])
                for c in range(2)
            ]

        turned = [[probes[j, c] for c in range(2)] for j in numbers]
        waves = [product(p, window(k, 0)) for k, p in enumerate(turned)]
        waves = propagate(waves, table, False)
        slices = [window(k, 1) for k in each]
        spectra = to_spectrum([product(w, o) for w, o in zip(waves, slices)], table)
        backs = []
        for k in each:
            re, im = spectra[k]
            factor = 1.0 - amplitude[k] * lax.rsqrt(re * re + im * im + 1.0)
            backs.append((re * factor, im * factor))
        backs = from_spectrum(backs, table)
        for k in each:
            grads[1, numbers[k], 0], grads[1, numbers[k], 1] = conj_product(waves[k], backs[k])
        backs = [conj_product(o, b) for o, b in zip(slices, backs)]
        backs = propagate(backs, table, True)
        for k in each:
            grads[0, numbers[k], 0], grads[0, numbers[k], 1] = conj_product(turned[k], backs[k])
        for k in each:
            r, start = words[k][0], words[k][3]
            base = base_of(k)
            count = jnp.where(depth == 0, lax.div(r + 7, 8), 32 - lax.div(r, 8))

            def step(g, carry, k=k, base=base, start=start, count=count):
                for q in range(4):
                    granule = jnp.minimum(4 * g + q, count - 1)
                    src = pl.multiple_of((base + granule) * 8, 8)
                    dst = pl.multiple_of((start + granule) * 8, 8)
                    for s in range(2):
                        for c in range(2):
                            rows_out[s, c, pl.ds(dst, 8), :] = grads[
                                s, numbers[k], c, pl.ds(src, 8), :
                            ]
                return carry

            lax.fori_loop(0, lax.div(count + 3, 4), step, 0)

    @pl.when(jobs >= 2)
    def _():
        work([0, 1])

    @pl.when(lax.rem(jobs, 2) == 1)
    def _():
        work([jobs - 1])


def gather_kernel(plan, rows, tile_in, out, tile, out_sems):
    row = lax.broadcasted_iota(jnp.int32, (CHUNK, N), 0)
    lane = lax.broadcasted_iota(jnp.int32, (CHUNK, N), 1)

    def add(at, j, c, lower):
        r = plan[at + 2 + 5 * j]
        start = plan[at + 2 + 5 * j + 3]
        first = 0 if lower else lax.div(r, CHUNK)
        last = lax.div(r + CHUNK - 1, CHUNK) if lower else N // CHUNK
        skip = 0 if lower else lax.div(r, 8)
        keep = lane >= plan[at + 2 + 5 * j + 2]
        low = pl.multiple_of(plan[at + 2 + 5 * j + 1] * N, N)
        high = pl.multiple_of(plan[at + 2 + 5 * j + 1] * N + N, N)

        def step(g, carry):
            dst = pl.multiple_of(g * CHUNK, CHUNK)
            inside = (row + dst < r) if lower else (row + dst >= r)
            src = pl.multiple_of(CHUNK + (start - skip) * 8 + g * CHUNK, 8)
            value = jnp.where(inside, rows[0 if lower else 1, c, pl.ds(src, CHUNK), :], 0.0)
            tile[c, pl.ds(dst, CHUNK), pl.ds(low, N)] += jnp.where(keep, value, 0.0)
            tile[c, pl.ds(dst, CHUNK), pl.ds(high, N)] += jnp.where(keep, 0.0, value)
            return carry

        lax.fori_loop(first, last, step, 0)

    for c in range(2):
        for at, lower in ((OWN_RIGHT, False), (PREV_LEFT, True)):

            def step(j, carry, at=at, lower=lower, c=c):
                add(at, j, c, lower)
                return carry

            lax.fori_loop(0, plan[at], step, 0)
        pltpu.make_async_copy(tile.at[c], out.at[c], out_sems.at[c]).start()
    for c in range(2):
        pltpu.make_async_copy(tile.at[c], out.at[c], out_sems.at[c]).wait()


SMEM = pl.BlockSpec(memory_space=pltpu.SMEM)
VMEM = pl.BlockSpec(memory_space=pltpu.VMEM)
HBM = pl.BlockSpec(memory_space=pltpu.HBM)


def shape(*dims):
    return jax.ShapeDtypeStruct(dims, jnp.float32)


def shards(n_lat, object_slices, probe, measured, positions, counts):
    columns = object_slices.shape[3]
    tile = object_slices.reshape(object_slices.shape[1:])
    dma = pltpu.SemaphoreType.DMA
    positions = positions.T
    own_plan, prev_positions, prev_counts, tile, measured = pl.pallas_call(
        functools.partial(announce_kernel, n_lat),
        name="announce",
        out_shape=(
            jax.ShapeDtypeStruct((2 * SPAN,), jnp.int32),
            jax.ShapeDtypeStruct(positions.shape, jnp.int32),
            jax.ShapeDtypeStruct(counts.shape, jnp.int32),
            shape(*tile.shape),
            shape(*measured.shape),
        ),
        in_specs=[HBM, HBM, HBM, HBM],
        out_specs=(SMEM, VMEM, VMEM, VMEM, VMEM),
        scratch_shapes=[
            pltpu.VMEM((4, N, N), jnp.float32),
            pltpu.VMEM((2, N, HALF), jnp.float32),
            pltpu.SMEM((2, 4), jnp.int32),
            pltpu.SMEM((1,), jnp.int32),
            dma((2,)), dma((2,)), dma((4,)),
        ],
        compiler_params=pltpu.CompilerParams(
            collective_id=2, has_side_effects=True, vmem_limit_bytes=46 << 20
        ),
    )(positions, counts, tile, measured)
    plan, ahead, behind = pl.pallas_call(
        pack_kernel,
        name="pack",
        out_shape=(
            jax.ShapeDtypeStruct((4 * SPAN,), jnp.int32),
            shape(2, ROWS, N),
            shape(2, ROWS, N),
        ),
        in_specs=[SMEM, SMEM, SMEM, VMEM, VMEM],
        out_specs=(SMEM, VMEM, VMEM),
        compiler_params=pltpu.CompilerParams(vmem_limit_bytes=4 << 20),
    )(own_plan, prev_positions, prev_counts, tile, measured)
    received, windows, probes = pl.pallas_call(
        functools.partial(exchange_kernel, n_lat),
        name="exchange",
        out_shape=(
            shape(2, 2, ROWS + 2 * PAD, N),
            shape(2, MAX_JOBS, 2, N, N),
            shape(MAX_JOBS, 2, N, N),
        ),
        in_specs=[SMEM, VMEM, VMEM, VMEM, VMEM],
        out_specs=(VMEM, VMEM, VMEM),
        scratch_shapes=[
            pltpu.VMEM((2, N, columns), jnp.float32),
            dma((2,)), dma((2,)), dma, dma,
        ],
        compiler_params=pltpu.CompilerParams(
            collective_id=0, has_side_effects=True, vmem_limit_bytes=12 << 20
        ),
    )(plan, ahead, behind, tile, probe)

    table = jnp.asarray(tables())
    rows_out, grads = pl.pallas_call(
        compute_kernel,
        name="compute",
        out_shape=(shape(2, 2, ROWS, N), shape(2, MAX_JOBS, 2, N, N)),
        in_specs=[SMEM, VMEM, VMEM, VMEM, VMEM, VMEM],
        out_specs=(VMEM, VMEM),
        scratch_shapes=[pltpu.VMEM((2, N, N), jnp.float32)],
        compiler_params=pltpu.CompilerParams(vmem_limit_bytes=30 << 20),
    )(plan, windows, probes, received, measured, table)

    rows_back, tile = pl.pallas_call(
        functools.partial(return_kernel, n_lat),
        name="giveback",
        out_shape=(shape(2, 2, ROWS + 2 * CHUNK, N), shape(2, N, columns)),
        in_specs=[SMEM, VMEM, VMEM],
        out_specs=(VMEM, VMEM),
        scratch_shapes=[
            pltpu.VMEM((MAX_JOBS, 2, N, N), jnp.float32),
            dma((2,)), dma((2,)), dma, dma,
        ],
        compiler_params=pltpu.CompilerParams(
            collective_id=1, has_side_effects=True, vmem_limit_bytes=12 << 20
        ),
    )(plan, rows_out, grads)

    out, _ = pl.pallas_call(
        gather_kernel,
        name="gather",
        out_shape=(shape(2, N, columns), shape(2, N, columns)),
        in_specs=[SMEM, VMEM, VMEM],
        out_specs=(HBM, VMEM),
        scratch_shapes=[dma((2,))],
        input_output_aliases={2: 1},
        compiler_params=pltpu.CompilerParams(vmem_limit_bytes=12 << 20),
    )(plan, rows_back, tile)
    return out.reshape(object_slices.shape)


def solution(mesh):
    return jax.shard_map(
        functools.partial(shards, mesh.shape["lat"]),
        mesh=mesh,
        in_specs=(
            P("depth", None, "lat", None),
            P(),
            P("lat", None, None),
            P("lat", None),
            P("lat"),
        ),
        out_specs=P("depth", None, "lat", None),
        check_vma=False,
    )
```

```python
import functools

import jax
import jax.numpy as jnp
import ml_dtypes
import numpy as np
from jax import lax
from jax.experimental import pallas as pl
from jax.experimental.pallas import tpu as pltpu
from jax.sharding import PartitionSpec as P

N = 256
HALF = 128
STRENGTH = 8.0
MAX_JOBS = 3
BUDGET = 48
ROWS = 8 * BUDGET
PAD = 256
CHUNK = 32
SPAN = 20


def split_bf16(a):
    hi = a.astype(np.float32).astype(ml_dtypes.bfloat16)
    lo = (a - hi.astype(np.float64)).astype(np.float32).astype(ml_dtypes.bfloat16)
    return hi, lo


def tables():
    index = np.arange(N)
    angle = 2.0 * np.pi * ((index[:, None] * index[None, :]) % N) / N
    dft = np.exp(-1j * angle) / 16.0
    centred = (index - N * (index >= HALF)) / N
    turn = np.exp(1j * np.pi * STRENGTH * centred**2)
    prop = np.conj(dft) @ (turn[:, None] * dft)
    c0, c1 = prop[:HALF, :HALF], prop[:HALF, HALF:]

    def real_form(m):
        return np.block([[m.real, -m.imag], [m.imag, m.real]])

    forms = [real_form(m) for m in ((c0 + c1) / 2, (c0 - c1) / 2, dft[0::2, :HALF], dft[1::2, :HALF])]
    forms = forms + [m.T for m in forms]
    return np.stack([np.stack(split_bf16(m)) for m in forms])


OWN_LEFT, OWN_RIGHT, PREV_LEFT, PREV_RIGHT = 0, SPAN, 2 * SPAN, 3 * SPAN


def choose_sides(rows_of, cols_of, live):
    up = [lax.div(rows_of[i] + 7, 8) for i in range(4)]
    down = [32 - lax.div(rows_of[i], 8) for i in range(4)]
    best = jnp.int32(1 << 20)
    pick = jnp.int32(0)
    for mask in range(16):
        right = [(mask >> i) & 1 for i in range(4)]
        n_right = sum(right)
        if n_right > MAX_JOBS:
            continue
        top = max([i + 1 for i in range(4) if right[i]], default=0)
        lefts = [jnp.where(live > i, up[i], 0) for i in range(4) if not right[i]]
        cost_left = sum(lefts, jnp.int32(0))
        cost_right = sum([down[i] + 8 for i in range(4) if right[i]], jnp.int32(0))
        widest = jnp.maximum(cost_left, cost_right)
        most = jnp.maximum(live - n_right, n_right)
        bad = (live < top) | (widest > BUDGET) | (most > MAX_JOBS)
        key = most * 64 + widest + jnp.where(bad, jnp.int32(1 << 16), 0)
        pick = jnp.where(key < best, mask, pick)
        best = jnp.minimum(key, best)
    blocks = [jnp.minimum(lax.div(cols_of[i], N), 6) for i in range(4)]
    sides = []
    for side in range(2):
        mine = [(live > i) & ((lax.shift_right_logical(pick, i) & 1) == side) for i in range(4)]
        size = up if side == 0 else down
        count, total = jnp.int32(0), jnp.int32(0)
        words = [[jnp.int32(0)] * 5 for _ in range(MAX_JOBS)]
        for i in range(4):
            fields = [rows_of[i], blocks[i], cols_of[i] - blocks[i] * N, total, jnp.int32(i)]
            for j in range(MAX_JOBS):
                here = mine[i] & (count == j)
                words[j] = [jnp.where(here, f, w) for f, w in zip(fields, words[j])]
            count = count + jnp.where(mine[i], 1, 0)
            total = total + jnp.where(mine[i], size[i], 0)
        sides.append([count, total] + [w for job in words for w in job])
    return sides


def lanes():
    return lax.broadcasted_iota(jnp.int32, (8, N), 1)


def announce_kernel(
    n_lat, pos_hbm, cnt, tile_hbm, measured_hbm,
    own_plan, prev_pos, prev_cnt, tile, apart,
    measured, spread, pos, live, send, recv, local,
):
    depth = lax.axis_index("depth")
    lat = lax.axis_index("lat")
    after = lax.rem(lat + 1, n_lat)
    before = lax.rem(lat + n_lat - 1, n_lat)
    barrier = pltpu.get_barrier_semaphore()
    pl.semaphore_signal(
        barrier, inc=1, device_id=(depth, before), device_id_type=pl.DeviceIdType.MESH
    )
    loads = [
        pltpu.make_async_copy(measured_hbm, measured, local.at[0]),
        pltpu.make_async_copy(tile_hbm, tile, local.at[1]),
        pltpu.make_async_copy(pos_hbm, pos, local.at[2]),
        pltpu.make_async_copy(cnt, live, local.at[3]),
    ]
    for load in loads:
        load.start()
    pl.semaphore_wait(barrier, 1)
    copies = [
        remote(pos_hbm, prev_pos, send.at[0], recv.at[0], depth, after),
        remote(cnt, prev_cnt, send.at[1], recv.at[1], depth, after),
    ]
    for copy in copies:
        copy.start()
    row = lax.broadcasted_iota(jnp.int32, (N, N), 0)
    lane = lax.broadcasted_iota(jnp.int32, (N, N), 1)
    order = jnp.where(lane < HALF, 2 * lane, 2 * lane - (N - 1))
    shuffle = jnp.where(row == order, 1.0, 0.0).astype(jnp.bfloat16)
    loads[0].wait()
    def rearrange(slot, carry):
        hi, lo = halves(measured[slot])
        columns = dot(
            jnp.concatenate([hi, lo], axis=1), jnp.concatenate([shuffle, shuffle], axis=0)
        )
        for h in range(2):
            spread[h] = columns[:, HALF * h : HALF * h + HALF]
        for p in range(2):
            for h in range(2):
                apart[slot, HALF * p : HALF * p + HALF, HALF * h : HALF * h + HALF] = spread[
                    h, pl.ds(p, HALF, stride=2), :
                ]
        return carry

    lax.fori_loop(0, 4, rearrange, 0)
    for load in loads[2:]:
        load.wait()
    own = choose_sides([pos[0, i] for i in range(4)], [pos[1, i] for i in range(4)], live[0])
    for k, side in enumerate(own):
        for w, word in enumerate(side):
            own_plan[k * SPAN + w] = word
    loads[1].wait()
    for copy in copies:
        copy.wait()


def pack_kernel(
    own_plan, prev_pos, prev_cnt, tile, measured, plan, ahead, behind
):
    depth = lax.axis_index("depth")
    prev = choose_sides(
        [prev_pos[0, i] for i in range(4)], [prev_pos[1, i] for i in range(4)], prev_cnt[0]
    )
    for k, side in enumerate(prev):
        for w, word in enumerate(side):
            plan[k * SPAN + w] = own_plan[k * SPAN + w]
            plan[PREV_LEFT + k * SPAN + w] = word

    def copy_rows(out, at, j, first, count):
        start = plan[at + 2 + 5 * j + 3]
        low = pl.multiple_of(plan[at + 2 + 5 * j + 1] * N, N)
        high = pl.multiple_of(plan[at + 2 + 5 * j + 1] * N + N, N)
        keep = lanes() >= plan[at + 2 + 5 * j + 2]

        def step(g, carry):
            for k in range(4):
                granule = jnp.minimum(4 * g + k, count - 1)
                src = pl.multiple_of((first + granule) * 8, 8)
                dst = pl.multiple_of((start + granule) * 8, 8)
                for c in range(2):
                    out[c, pl.ds(dst, 8), :] = jnp.where(
                        keep,
                        tile[c, pl.ds(src, 8), pl.ds(low, N)],
                        tile[c, pl.ds(src, 8), pl.ds(high, N)],
                    )
            return carry

        lax.fori_loop(0, lax.div(count + 3, 4), step, 0)

    def right_job(j, carry):
        first = lax.div(plan[OWN_RIGHT + 2 + 5 * j], 8)
        copy_rows(ahead, OWN_RIGHT, j, first, 32 - first)
        slot = plan[OWN_RIGHT + 2 + 5 * j + 4]
        dst = pl.multiple_of((plan[OWN_RIGHT + 1] + 8 * j) * 8, 8)
        for c in range(2):
            src = pl.multiple_of(depth * HALF + 64 * c, 64)
            ahead[c, pl.ds(dst, 64), :] = measured[slot, pl.ds(src, 64), :]
        return carry

    lax.fori_loop(0, plan[OWN_RIGHT], right_job, 0)

    def left_job(j, carry):
        copy_rows(behind, PREV_LEFT, j, 0, lax.div(plan[PREV_LEFT + 2 + 5 * j] + 7, 8))
        return carry

    lax.fori_loop(0, plan[PREV_LEFT], left_job, 0)


def exchange_kernel(
    n_lat, plan, ahead, behind, tile, probe, received, windows, probes,
    other, row_send, row_recv, tile_send, tile_recv,
):
    depth = lax.axis_index("depth")
    lat = lax.axis_index("lat")
    after = lax.rem(lat + 1, n_lat)
    before = lax.rem(lat + n_lat - 1, n_lat)
    origin = jnp.where(depth == 0, after, before)
    greet([(0, origin), (1, origin), (1 - depth, lat)])

    def slot(s):
        return received.at[s, :, pl.ds(PAD, ROWS), :]

    sends = [
        remote(ahead, slot(depth), row_send.at[0], row_recv.at[depth], 1, after),
        remote(behind, slot(depth), row_send.at[1], row_recv.at[depth], 0, before),
    ]
    for copy in sends:
        copy.start()
    swap = remote(tile, other, tile_send, tile_recv, 1 - depth, lat)
    swap.start()
    at = jnp.where(depth == 0, OWN_LEFT, PREV_RIGHT)
    def turn(i, carry):
        j, c = lax.div(i, 2), lax.rem(i, 2)
        shift = plan[at + 2 + 5 * j + 2]
        shift = jnp.where(shift == N, 0, shift)
        probes[j, c] = pltpu.roll(pltpu.roll(probe[c], plan[at + 2 + 5 * j], 0), shift, 1)
        return carry

    lax.fori_loop(0, 2 * MAX_JOBS, turn, 0)
    pick_columns(plan, at, tile, windows, depth)
    swap.wait()
    pick_columns(plan, at, other, windows, 1 - depth)
    for copy in sends:
        copy.wait_send()
    for s in range(2):
        remote(ahead, slot(s), row_send.at[0], row_recv.at[s], 1, after).wait_recv()


def pick_columns(plan, at, source, windows, s):
    lane = lanes()
    columns = [
        plan[at + 2 + 5 * j + 1] * N + plan[at + 2 + 5 * j + 2] for j in range(MAX_JOBS)
    ]

    def step(g, carry):
        rows = pl.ds(pl.multiple_of(g * 8, 8), 8)
        for c in range(2):
            picked = [jnp.zeros((8, N), jnp.float32)] * MAX_JOBS
            for q in range(source.shape[2] // N):
                value = source[c, rows, q * N : q * N + N]
                for j, column in enumerate(columns):
                    offset = lane + (q * N - column)
                    picked[j] = jnp.where((offset >= 0) & (offset < N), value, picked[j])
            for j in range(MAX_JOBS):
                windows[s, j, c, rows, :] = picked[j]
        return carry

    lax.fori_loop(0, N // 8, step, 0)


def remote(src, dst, send, recv, depth, lat):
    return pltpu.make_async_remote_copy(
        src_ref=src,
        dst_ref=dst,
        send_sem=send,
        recv_sem=recv,
        device_id=(depth, lat),
        device_id_type=pl.DeviceIdType.MESH,
    )


def greet(sources):
    barrier = pltpu.get_barrier_semaphore()
    for source in sources:
        pl.semaphore_signal(
            barrier, inc=1, device_id=source, device_id_type=pl.DeviceIdType.MESH
        )
    pl.semaphore_wait(barrier, 3)


def return_kernel(
    n_lat, plan, rows, windows, received, tile,
    partner, row_send, row_recv, swap_send, swap_recv,
):
    depth = lax.axis_index("depth")
    lat = lax.axis_index("lat")
    after = lax.rem(lat + 1, n_lat)
    before = lax.rem(lat + n_lat - 1, n_lat)
    greet([(0, before), (1, after), (1 - depth, lat)])
    target = jnp.where(depth == 0, after, before)

    def part(c):
        return received.at[c, :, pl.ds(CHUNK, ROWS), :]

    sends = [
        remote(rows.at[s], part(depth), row_send.at[s], row_recv.at[depth], s, target)
        for s in range(2)
    ]
    for copy in sends:
        copy.start()
    swap = remote(windows.at[1 - depth], partner, swap_send, swap_recv, 1 - depth, lat)
    swap.start()
    sum_windows(plan, depth, lambda j, c, at: windows[depth, j, c, at, :], tile, True)
    swap.wait()
    sum_windows(plan, 1 - depth, lambda j, c, at: partner[j, c, at, :], tile, False)
    for copy in sends:
        copy.wait_send()
    for c in range(2):
        remote(rows.at[0], part(c), row_send.at[0], row_recv.at[c], 0, target).wait_recv()


def sum_windows(plan, core, read, tile, first):
    at = jnp.where(core == 0, OWN_LEFT, PREV_RIGHT)
    row = lax.broadcasted_iota(jnp.int32, (8, N), 0)
    lane = lanes()
    jobs = []
    for j in range(MAX_JOBS):
        r = plan[at + 2 + 5 * j]
        low = jnp.where(core == 0, r, 0)
        high = jnp.where(plan[at] > j, jnp.where(core == 0, N, r), 0)
        jobs.append((low, high, plan[at + 2 + 5 * j + 1] * N + plan[at + 2 + 5 * j + 2]))

    def step(g, carry):
        dst = pl.ds(pl.multiple_of(g * 8, 8), 8)
        here = row + g * 8
        for c in range(2):
            values = [
                jnp.where((here >= low) & (here < high), read(j, c, dst), 0.0)
                for j, (low, high, _) in enumerate(jobs)
            ]
            for q in range(tile.shape[2] // N):
                total = None if first else tile[c, dst, q * N : q * N + N]
                for value, (_, _, column) in zip(values, jobs):
                    offset = lane + (q * N - column)
                    inside = (offset >= 0) & (offset < N)
                    value = jnp.where(inside, value, 0.0)
                    total = value if total is None else total + value
                tile[c, dst, q * N : q * N + N] = total
        return carry

    lax.fori_loop(0, N // 8, step, 0)


P_PLUS, P_MINUS, F_EVEN, F_ODD = 0, 1, 2, 3
TURNED = 4


def halves(x):
    hi = x.astype(jnp.bfloat16)
    lo = (x - hi.astype(jnp.float32)).astype(jnp.bfloat16)
    return hi, lo


def dot(a, b):
    return jnp.dot(a, b, preferred_element_type=jnp.float32)


def times_right(x, table, at):
    hi, lo = halves(x)
    return dot(
        jnp.concatenate([hi, lo, hi], axis=1),
        jnp.concatenate([table[at, 0], table[at, 0], table[at, 1]], axis=0),
    )


def times_left(table, at, x):
    hi, lo = halves(x)
    return dot(
        jnp.concatenate([table[at, 0], table[at, 0], table[at, 1]], axis=1),
        jnp.concatenate([hi, lo, hi], axis=0),
    )


def fold_columns(re, im):
    plus = jnp.concatenate([re[:, :HALF] + re[:, HALF:], im[:, :HALF] + im[:, HALF:]], axis=1)
    minus = jnp.concatenate([re[:, :HALF] - re[:, HALF:], im[:, :HALF] - im[:, HALF:]], axis=1)
    return plus, minus


def pair_columns(re, im):
    return (
        jnp.concatenate([re[:, :HALF], im[:, :HALF]], axis=1),
        jnp.concatenate([re[:, HALF:], im[:, HALF:]], axis=1),
    )


def fold_rows(re, im):
    plus = jnp.concatenate([re[:HALF] + re[HALF:], im[:HALF] + im[HALF:]], axis=0)
    minus = jnp.concatenate([re[:HALF] - re[HALF:], im[:HALF] - im[HALF:]], axis=0)
    return plus, minus


def pair_rows(re, im):
    return (
        jnp.concatenate([re[:HALF], im[:HALF]], axis=0),
        jnp.concatenate([re[HALF:], im[HALF:]], axis=0),
    )


def product(u, v):
    return u[0] * v[0] - u[1] * v[1], u[0] * v[1] + u[1] * v[0]


def conj_product(u, v):
    return u[0] * v[0] + u[1] * v[1], u[0] * v[1] - u[1] * v[0]


def both_right(pairs, table, first, second):
    return [(times_right(p, table, first), times_right(m, table, second)) for p, m in pairs]


def both_left(pairs, table, first, second):
    return [(times_left(table, first, p), times_left(table, second, m)) for p, m in pairs]


def unfold(pairs):
    return [(p + m, p - m) for p, m in pairs]


def propagate(fields, table, adjoint):
    left, right = (TURNED, 0) if adjoint else (0, TURNED)
    pairs = [fold_columns(*f) for f in fields]
    pairs = unfold(both_right(pairs, table, right + P_PLUS, right + P_MINUS))
    pairs = [fold_rows(*pair_columns(*p)) for p in pairs]
    pairs = unfold(both_left(pairs, table, left + P_PLUS, left + P_MINUS))
    return [pair_rows(*p) for p in pairs]


def to_spectrum(fields, table):
    pairs = [fold_columns(*f) for f in fields]
    pairs = both_right(pairs, table, TURNED + F_EVEN, TURNED + F_ODD)
    pairs = [fold_rows(*pair_columns(*p)) for p in pairs]
    pairs = both_left(pairs, table, F_EVEN, F_ODD)
    return [pair_rows(*p) for p in pairs]


def from_spectrum(fields, table):
    pairs = [pair_columns(*f) for f in fields]
    pairs = unfold(both_right(pairs, table, F_EVEN, F_ODD))
    pairs = [pair_rows(*pair_columns(*p)) for p in pairs]
    pairs = unfold(both_left(pairs, table, TURNED + F_EVEN, TURNED + F_ODD))
    return [pair_rows(*p) for p in pairs]


def compute_kernel(
    plan, windows, probes, received, measured, table,
    rows_out, grads,
    amplitude,
):
    depth = lax.axis_index("depth")
    at = jnp.where(depth == 0, OWN_LEFT, PREV_RIGHT)
    jobs = plan[at]
    row = lax.broadcasted_iota(jnp.int32, (N, N), 0)

    def work(numbers):
        each = range(len(numbers))
        words = [[plan[at + 2 + 5 * j + w] for w in range(5)] for j in numbers]

        for k in each:
            _, _, _, _, slot = words[k]

            @pl.when(depth == 0)
            def _(k=k, slot=slot):
                amplitude[k] = measured[slot]

            @pl.when(depth == 1)
            def _(k=k):
                src = pl.multiple_of(PAD + (plan[PREV_RIGHT + 1] + 8 * numbers[k]) * 8, 8)
                for s in range(2):
                    for c in range(2):
                        amplitude[k, pl.ds(128 * s + 64 * c, 64), :] = received[
                            s, c, pl.ds(src, 64), :
                        ]

        def base_of(k):
            return jnp.where(depth == 0, 0, lax.div(words[k][0], 8))

        def window(k, s):
            r, _, _, start, _ = words[k]
            here = (row >= jnp.where(depth == 0, r, 0)) & (row < jnp.where(depth == 0, N, r))
            src = pl.multiple_of(PAD + (start - base_of(k)) * 8, 8)
            return [
                jnp.where(here, windows[s, numbers[k], c], received[s, c, pl.ds(src, N), :])
                for c in range(2)
            ]

        turned = [[probes[j, c] for c in range(2)] for j in numbers]
        waves = [product(p, window(k, 0)) for k, p in enumerate(turned)]
        waves = propagate(waves, table, False)
        slices = [window(k, 1) for k in each]
        spectra = to_spectrum([product(w, o) for w, o in zip(waves, slices)], table)
        backs = []
        for k in each:
            re, im = spectra[k]
            factor = 1.0 - amplitude[k] * lax.rsqrt(re * re + im * im + 1.0)
            backs.append((re * factor, im * factor))
        backs = from_spectrum(backs, table)
        for k in each:
            grads[1, numbers[k], 0], grads[1, numbers[k], 1] = conj_product(waves[k], backs[k])
        backs = [conj_product(o, b) for o, b in zip(slices, backs)]
        backs = propagate(backs, table, True)
        for k in each:
            grads[0, numbers[k], 0], grads[0, numbers[k], 1] = conj_product(turned[k], backs[k])
        for k in each:
            r, start = words[k][0], words[k][3]
            base = base_of(k)
            count = jnp.where(depth == 0, lax.div(r + 7, 8), 32 - lax.div(r, 8))

            def step(g, carry, k=k, base=base, start=start, count=count):
                for q in range(4):
                    granule = jnp.minimum(4 * g + q, count - 1)
                    src = pl.multiple_of((base + granule) * 8, 8)
                    dst = pl.multiple_of((start + granule) * 8, 8)
                    for s in range(2):
                        for c in range(2):
                            rows_out[s, c, pl.ds(dst, 8), :] = grads[
                                s, numbers[k], c, pl.ds(src, 8), :
                            ]
                return carry

            lax.fori_loop(0, lax.div(count + 3, 4), step, 0)

    @pl.when(jobs >= 2)
    def _():
        work([0, 1])

    @pl.when(lax.rem(jobs, 2) == 1)
    def _():
        work([jobs - 1])


def gather_kernel(plan, rows, tile_in, out, tile, out_sems):
    row = lax.broadcasted_iota(jnp.int32, (CHUNK, N), 0)
    lane = lax.broadcasted_iota(jnp.int32, (CHUNK, N), 1)

    def add(at, j, c, lower):
        r = plan[at + 2 + 5 * j]
        start = plan[at + 2 + 5 * j + 3]
        first = 0 if lower else lax.div(r, CHUNK)
        last = lax.div(r + CHUNK - 1, CHUNK) if lower else N // CHUNK
        skip = 0 if lower else lax.div(r, 8)
        keep = lane >= plan[at + 2 + 5 * j + 2]
        low = pl.multiple_of(plan[at + 2 + 5 * j + 1] * N, N)
        high = pl.multiple_of(plan[at + 2 + 5 * j + 1] * N + N, N)

        def step(g, carry):
            dst = pl.multiple_of(g * CHUNK, CHUNK)
            inside = (row + dst < r) if lower else (row + dst >= r)
            src = pl.multiple_of(CHUNK + (start - skip) * 8 + g * CHUNK, 8)
            value = jnp.where(inside, rows[0 if lower else 1, c, pl.ds(src, CHUNK), :], 0.0)
            tile[c, pl.ds(dst, CHUNK), pl.ds(low, N)] += jnp.where(keep, value, 0.0)
            tile[c, pl.ds(dst, CHUNK), pl.ds(high, N)] += jnp.where(keep, 0.0, value)
            return carry

        lax.fori_loop(first, last, step, 0)

    for c in range(2):
        for at, lower in ((OWN_RIGHT, False), (PREV_LEFT, True)):

            def step(j, carry, at=at, lower=lower, c=c):
                add(at, j, c, lower)
                return carry

            lax.fori_loop(0, plan[at], step, 0)
        pltpu.make_async_copy(tile.at[c], out.at[c], out_sems.at[c]).start()
    for c in range(2):
        pltpu.make_async_copy(tile.at[c], out.at[c], out_sems.at[c]).wait()


SMEM = pl.BlockSpec(memory_space=pltpu.SMEM)
VMEM = pl.BlockSpec(memory_space=pltpu.VMEM)
HBM = pl.BlockSpec(memory_space=pltpu.HBM)


def shape(*dims):
    return jax.ShapeDtypeStruct(dims, jnp.float32)


def shards(n_lat, object_slices, probe, measured, positions, counts):
    columns = object_slices.shape[3]
    tile = object_slices.reshape(object_slices.shape[1:])
    dma = pltpu.SemaphoreType.DMA
    positions = positions.T
    own_plan, prev_positions, prev_counts, tile, measured = pl.pallas_call(
        functools.partial(announce_kernel, n_lat),
        name="announce",
        out_shape=(
            jax.ShapeDtypeStruct((2 * SPAN,), jnp.int32),
            jax.ShapeDtypeStruct(positions.shape, jnp.int32),
            jax.ShapeDtypeStruct(counts.shape, jnp.int32),
            shape(*tile.shape),
            shape(*measured.shape),
        ),
        in_specs=[HBM, HBM, HBM, HBM],
        out_specs=(SMEM, VMEM, VMEM, VMEM, VMEM),
        scratch_shapes=[
            pltpu.VMEM((4, N, N), jnp.float32),
            pltpu.VMEM((2, N, HALF), jnp.float32),
            pltpu.SMEM((2, 4), jnp.int32),
            pltpu.SMEM((1,), jnp.int32),
            dma((2,)), dma((2,)), dma((4,)),
        ],
        compiler_params=pltpu.CompilerParams(
            collective_id=2, has_side_effects=True, vmem_limit_bytes=46 << 20
        ),
    )(positions, counts, tile, measured)
    plan, ahead, behind = pl.pallas_call(
        pack_kernel,
        name="pack",
        out_shape=(
            jax.ShapeDtypeStruct((4 * SPAN,), jnp.int32),
            shape(2, ROWS, N),
            shape(2, ROWS, N),
        ),
        in_specs=[SMEM, SMEM, SMEM, VMEM, VMEM],
        out_specs=(SMEM, VMEM, VMEM),
        compiler_params=pltpu.CompilerParams(vmem_limit_bytes=4 << 20),
    )(own_plan, prev_positions, prev_counts, tile, measured)
    received, windows, probes = pl.pallas_call(
        functools.partial(exchange_kernel, n_lat),
        name="exchange",
        out_shape=(
            shape(2, 2, ROWS + 2 * PAD, N),
            shape(2, MAX_JOBS, 2, N, N),
            shape(MAX_JOBS, 2, N, N),
        ),
        in_specs=[SMEM, VMEM, VMEM, VMEM, VMEM],
        out_specs=(VMEM, VMEM, VMEM),
        scratch_shapes=[
            pltpu.VMEM((2, N, columns), jnp.float32),
            dma((2,)), dma((2,)), dma, dma,
        ],
        compiler_params=pltpu.CompilerParams(
            collective_id=0, has_side_effects=True, vmem_limit_bytes=12 << 20
        ),
    )(plan, ahead, behind, tile, probe)

    table = jnp.asarray(tables())
    rows_out, grads = pl.pallas_call(
        compute_kernel,
        name="compute",
        out_shape=(shape(2, 2, ROWS, N), shape(2, MAX_JOBS, 2, N, N)),
        in_specs=[SMEM, VMEM, VMEM, VMEM, VMEM, VMEM],
        out_specs=(VMEM, VMEM),
        scratch_shapes=[pltpu.VMEM((2, N, N), jnp.float32)],
        compiler_params=pltpu.CompilerParams(vmem_limit_bytes=30 << 20),
    )(plan, windows, probes, received, measured, table)

    rows_back, tile = pl.pallas_call(
        functools.partial(return_kernel, n_lat),
        name="giveback",
        out_shape=(shape(2, 2, ROWS + 2 * CHUNK, N), shape(2, N, columns)),
        in_specs=[SMEM, VMEM, VMEM],
        out_specs=(VMEM, VMEM),
        scratch_shapes=[
            pltpu.VMEM((MAX_JOBS, 2, N, N), jnp.float32),
            dma((2,)), dma((2,)), dma, dma,
        ],
        compiler_params=pltpu.CompilerParams(
            collective_id=1, has_side_effects=True, vmem_limit_bytes=12 << 20
        ),
    )(plan, rows_out, grads)

    out, _ = pl.pallas_call(
        gather_kernel,
        name="gather",
        out_shape=(shape(2, N, columns), shape(2, N, columns)),
        in_specs=[SMEM, VMEM, VMEM],
        out_specs=(HBM, VMEM),
        scratch_shapes=[dma((2,))],
        input_output_aliases={2: 1},
        compiler_params=pltpu.CompilerParams(vmem_limit_bytes=12 << 20),
    )(plan, rows_back, tile)
    return out.reshape(object_slices.shape)


def solution(mesh):
    return jax.shard_map(
        functools.partial(shards, mesh.shape["lat"]),
        mesh=mesh,
        in_specs=(
            P("depth", None, "lat", None),
            P(),
            P("lat", None, None),
            P("lat", None),
            P("lat"),
        ),
        out_specs=P("depth", None, "lat", None),
        check_vma=False,
    )
```

```python
import functools

import jax
import jax.numpy as jnp
import ml_dtypes
import numpy as np
from jax import lax
from jax.experimental import pallas as pl
from jax.experimental.pallas import tpu as pltpu
from jax.sharding import PartitionSpec as P

N = 256
HALF = 128
STRENGTH = 8.0
MAX_JOBS = 3
BUDGET = 48
ROWS = 8 * BUDGET
PAD = 256
CHUNK = 32
SPAN = 20


def split_bf16(a):
    hi = a.astype(np.float32).astype(ml_dtypes.bfloat16)
    lo = (a - hi.astype(np.float64)).astype(np.float32).astype(ml_dtypes.bfloat16)
    return hi, lo


def tables():
    index = np.arange(N)
    angle = 2.0 * np.pi * ((index[:, None] * index[None, :]) % N) / N
    dft = np.exp(-1j * angle) / 16.0
    centred = (index - N * (index >= HALF)) / N
    turn = np.exp(1j * np.pi * STRENGTH * centred**2)
    prop = np.conj(dft) @ (turn[:, None] * dft)
    c0, c1 = prop[:HALF, :HALF], prop[:HALF, HALF:]

    def real_form(m):
        return np.block([[m.real, -m.imag], [m.imag, m.real]])

    forms = [real_form(m) for m in ((c0 + c1) / 2, (c0 - c1) / 2, dft[0::2, :HALF], dft[1::2, :HALF])]
    forms = forms + [m.T for m in forms]
    return np.stack([np.stack(split_bf16(m)) for m in forms])


OWN_LEFT, OWN_RIGHT, PREV_LEFT, PREV_RIGHT = 0, SPAN, 2 * SPAN, 3 * SPAN


def choose_sides(rows_of, cols_of, live):
    up = [lax.div(rows_of[i] + 7, 8) for i in range(4)]
    down = [32 - lax.div(rows_of[i], 8) for i in range(4)]
    best = jnp.int32(1 << 20)
    pick = jnp.int32(0)
    for mask in range(16):
        right = [(mask >> i) & 1 for i in range(4)]
        n_right = sum(right)
        if n_right > MAX_JOBS:
            continue
        top = max([i + 1 for i in range(4) if right[i]], default=0)
        lefts = [jnp.where(live > i, up[i], 0) for i in range(4) if not right[i]]
        cost_left = sum(lefts, jnp.int32(0))
        cost_right = sum([down[i] + 8 for i in range(4) if right[i]], jnp.int32(0))
        widest = jnp.maximum(cost_left, cost_right)
        most = jnp.maximum(live - n_right, n_right)
        bad = (live < top) | (widest > BUDGET) | (most > MAX_JOBS)
        key = most * 64 + widest + jnp.where(bad, jnp.int32(1 << 16), 0)
        pick = jnp.where(key < best, mask, pick)
        best = jnp.minimum(key, best)
    blocks = [jnp.minimum(lax.div(cols_of[i], N), 6) for i in range(4)]
    sides = []
    for side in range(2):
        mine = [(live > i) & ((lax.shift_right_logical(pick, i) & 1) == side) for i in range(4)]
        size = up if side == 0 else down
        count, total = jnp.int32(0), jnp.int32(0)
        words = [[jnp.int32(0)] * 5 for _ in range(MAX_JOBS)]
        for i in range(4):
            fields = [rows_of[i], blocks[i], cols_of[i] - blocks[i] * N, total, jnp.int32(i)]
            for j in range(MAX_JOBS):
                here = mine[i] & (count == j)
                words[j] = [jnp.where(here, f, w) for f, w in zip(fields, words[j])]
            count = count + jnp.where(mine[i], 1, 0)
            total = total + jnp.where(mine[i], size[i], 0)
        sides.append([count, total] + [w for job in words for w in job])
    return sides


def lanes():
    return lax.broadcasted_iota(jnp.int32, (8, N), 1)


def announce_kernel(
    n_lat, pos_hbm, cnt, tile_hbm,
    own_plan, prev_pos, prev_cnt, tile,
    pos, live, send, recv, local,
):
    depth = lax.axis_index("depth")
    lat = lax.axis_index("lat")
    after = lax.rem(lat + 1, n_lat)
    before = lax.rem(lat + n_lat - 1, n_lat)
    barrier = pltpu.get_barrier_semaphore()
    pl.semaphore_signal(
        barrier, inc=1, device_id=(depth, before), device_id_type=pl.DeviceIdType.MESH
    )
    loads = [
        pltpu.make_async_copy(tile_hbm, tile, local.at[0]),
        pltpu.make_async_copy(pos_hbm, pos, local.at[1]),
        pltpu.make_async_copy(cnt, live, local.at[2]),
    ]
    for load in loads:
        load.start()
    pl.semaphore_wait(barrier, 1)
    copies = [
        remote(pos_hbm, prev_pos, send.at[0], recv.at[0], depth, after),
        remote(cnt, prev_cnt, send.at[1], recv.at[1], depth, after),
    ]
    for copy in copies:
        copy.start()
    for load in loads[1:]:
        load.wait()
    own = choose_sides([pos[0, i] for i in range(4)], [pos[1, i] for i in range(4)], live[0])
    for k, side in enumerate(own):
        for w, word in enumerate(side):
            own_plan[k * SPAN + w] = word
    loads[0].wait()
    for copy in copies:
        copy.wait()


def pack_kernel(
    own_plan, prev_pos, prev_cnt, tile, measured, plan, ahead, behind
):
    depth = lax.axis_index("depth")
    prev = choose_sides(
        [prev_pos[0, i] for i in range(4)], [prev_pos[1, i] for i in range(4)], prev_cnt[0]
    )
    for k, side in enumerate(prev):
        for w, word in enumerate(side):
            plan[k * SPAN + w] = own_plan[k * SPAN + w]
            plan[PREV_LEFT + k * SPAN + w] = word

    def copy_rows(out, at, j, first, count):
        start = plan[at + 2 + 5 * j + 3]
        low = pl.multiple_of(plan[at + 2 + 5 * j + 1] * N, N)
        high = pl.multiple_of(plan[at + 2 + 5 * j + 1] * N + N, N)
        keep = lanes() >= plan[at + 2 + 5 * j + 2]

        def step(g, carry):
            for k in range(4):
                granule = jnp.minimum(4 * g + k, count - 1)
                src = pl.multiple_of((first + granule) * 8, 8)
                dst = pl.multiple_of((start + granule) * 8, 8)
                for c in range(2):
                    out[c, pl.ds(dst, 8), :] = jnp.where(
                        keep,
                        tile[c, pl.ds(src, 8), pl.ds(low, N)],
                        tile[c, pl.ds(src, 8), pl.ds(high, N)],
                    )
            return carry

        lax.fori_loop(0, lax.div(count + 3, 4), step, 0)

    def right_job(j, carry):
        first = lax.div(plan[OWN_RIGHT + 2 + 5 * j], 8)
        copy_rows(ahead, OWN_RIGHT, j, first, 32 - first)
        slot = plan[OWN_RIGHT + 2 + 5 * j + 4]
        dst = pl.multiple_of((plan[OWN_RIGHT + 1] + 8 * j) * 8, 8)
        for c in range(2):
            src = pl.multiple_of(depth * HALF + 64 * c, 64)
            ahead[c, pl.ds(dst, 64), :] = measured[slot, pl.ds(src, 64), :]
        return carry

    lax.fori_loop(0, plan[OWN_RIGHT], right_job, 0)

    def left_job(j, carry):
        copy_rows(behind, PREV_LEFT, j, 0, lax.div(plan[PREV_LEFT + 2 + 5 * j] + 7, 8))
        return carry

    lax.fori_loop(0, plan[PREV_LEFT], left_job, 0)


def exchange_kernel(
    n_lat, plan, ahead, behind, tile, probe, received, windows, probes,
    other, row_send, row_recv, tile_send, tile_recv,
):
    depth = lax.axis_index("depth")
    lat = lax.axis_index("lat")
    after = lax.rem(lat + 1, n_lat)
    before = lax.rem(lat + n_lat - 1, n_lat)
    origin = jnp.where(depth == 0, after, before)
    greet([(0, origin), (1, origin), (1 - depth, lat)])

    def slot(s):
        return received.at[s, :, pl.ds(PAD, ROWS), :]

    sends = [
        remote(ahead, slot(depth), row_send.at[0], row_recv.at[depth], 1, after),
        remote(behind, slot(depth), row_send.at[1], row_recv.at[depth], 0, before),
    ]
    for copy in sends:
        copy.start()
    swap = remote(tile, other, tile_send, tile_recv, 1 - depth, lat)
    swap.start()
    at = jnp.where(depth == 0, OWN_LEFT, PREV_RIGHT)
    def turn(i, carry):
        j, c = lax.div(i, 2), lax.rem(i, 2)
        shift = plan[at + 2 + 5 * j + 2]
        shift = jnp.where(shift == N, 0, shift)
        probes[j, c] = pltpu.roll(pltpu.roll(probe[c], plan[at + 2 + 5 * j], 0), shift, 1)
        return carry

    lax.fori_loop(0, 2 * MAX_JOBS, turn, 0)
    pick_columns(plan, at, tile, windows, depth)
    swap.wait()
    pick_columns(plan, at, other, windows, 1 - depth)
    for copy in sends:
        copy.wait_send()
    for s in range(2):
        remote(ahead, slot(s), row_send.at[0], row_recv.at[s], 1, after).wait_recv()


def pick_columns(plan, at, source, windows, s):
    lane = lanes()
    columns = [
        plan[at + 2 + 5 * j + 1] * N + plan[at + 2 + 5 * j + 2] for j in range(MAX_JOBS)
    ]

    def step(g, carry):
        rows = pl.ds(pl.multiple_of(g * 8, 8), 8)
        for c in range(2):
            picked = [jnp.zeros((8, N), jnp.float32)] * MAX_JOBS
            for q in range(source.shape[2] // N):
                value = source[c, rows, q * N : q * N + N]
                for j, column in enumerate(columns):
                    offset = lane + (q * N - column)
                    picked[j] = jnp.where((offset >= 0) & (offset < N), value, picked[j])
            for j in range(MAX_JOBS):
                windows[s, j, c, rows, :] = picked[j]
        return carry

    lax.fori_loop(0, N // 8, step, 0)


def remote(src, dst, send, recv, depth, lat):
    return pltpu.make_async_remote_copy(
        src_ref=src,
        dst_ref=dst,
        send_sem=send,
        recv_sem=recv,
        device_id=(depth, lat),
        device_id_type=pl.DeviceIdType.MESH,
    )


def greet(sources):
    barrier = pltpu.get_barrier_semaphore()
    for source in sources:
        pl.semaphore_signal(
            barrier, inc=1, device_id=source, device_id_type=pl.DeviceIdType.MESH
        )
    pl.semaphore_wait(barrier, 3)


def return_kernel(
    n_lat, plan, rows, windows, received, tile,
    partner, row_send, row_recv, swap_send, swap_recv,
):
    depth = lax.axis_index("depth")
    lat = lax.axis_index("lat")
    after = lax.rem(lat + 1, n_lat)
    before = lax.rem(lat + n_lat - 1, n_lat)
    greet([(0, before), (1, after), (1 - depth, lat)])
    target = jnp.where(depth == 0, after, before)

    def part(c):
        return received.at[c, :, pl.ds(CHUNK, ROWS), :]

    sends = [
        remote(rows.at[s], part(depth), row_send.at[s], row_recv.at[depth], s, target)
        for s in range(2)
    ]
    for copy in sends:
        copy.start()
    swap = remote(windows.at[1 - depth], partner, swap_send, swap_recv, 1 - depth, lat)
    swap.start()
    sum_windows(plan, depth, lambda j, c, at: windows[depth, j, c, at, :], tile, True)
    swap.wait()
    sum_windows(plan, 1 - depth, lambda j, c, at: partner[j, c, at, :], tile, False)
    for copy in sends:
        copy.wait_send()
    for c in range(2):
        remote(rows.at[0], part(c), row_send.at[0], row_recv.at[c], 0, target).wait_recv()


def sum_windows(plan, core, read, tile, first):
    at = jnp.where(core == 0, OWN_LEFT, PREV_RIGHT)
    row = lax.broadcasted_iota(jnp.int32, (8, N), 0)
    lane = lanes()
    jobs = []
    for j in range(MAX_JOBS):
        r = plan[at + 2 + 5 * j]
        low = jnp.where(core == 0, r, 0)
        high = jnp.where(plan[at] > j, jnp.where(core == 0, N, r), 0)
        jobs.append((low, high, plan[at + 2 + 5 * j + 1] * N + plan[at + 2 + 5 * j + 2]))

    def step(g, carry):
        dst = pl.ds(pl.multiple_of(g * 8, 8), 8)
        here = row + g * 8
        for c in range(2):
            values = [
                jnp.where((here >= low) & (here < high), read(j, c, dst), 0.0)
                for j, (low, high, _) in enumerate(jobs)
            ]
            for q in range(tile.shape[2] // N):
                total = None if first else tile[c, dst, q * N : q * N + N]
                for value, (_, _, column) in zip(values, jobs):
                    offset = lane + (q * N - column)
                    inside = (offset >= 0) & (offset < N)
                    value = jnp.where(inside, value, 0.0)
                    total = value if total is None else total + value
                tile[c, dst, q * N : q * N + N] = total
        return carry

    lax.fori_loop(0, N // 8, step, 0)


P_PLUS, P_MINUS, F_EVEN, F_ODD = 0, 1, 2, 3
TURNED = 4


def halves(x):
    hi = x.astype(jnp.bfloat16)
    lo = (x - hi.astype(jnp.float32)).astype(jnp.bfloat16)
    return hi, lo


def dot(a, b):
    return jnp.dot(a, b, preferred_element_type=jnp.float32)


def times_right(x, table, at):
    hi, lo = halves(x)
    return dot(
        jnp.concatenate([hi, lo, hi], axis=1),
        jnp.concatenate([table[at, 0], table[at, 0], table[at, 1]], axis=0),
    )


def times_left(table, at, x):
    hi, lo = halves(x)
    return dot(
        jnp.concatenate([table[at, 0], table[at, 0], table[at, 1]], axis=1),
        jnp.concatenate([hi, lo, hi], axis=0),
    )


def fold_columns(re, im):
    plus = jnp.concatenate([re[:, :HALF] + re[:, HALF:], im[:, :HALF] + im[:, HALF:]], axis=1)
    minus = jnp.concatenate([re[:, :HALF] - re[:, HALF:], im[:, :HALF] - im[:, HALF:]], axis=1)
    return plus, minus


def pair_columns(re, im):
    return (
        jnp.concatenate([re[:, :HALF], im[:, :HALF]], axis=1),
        jnp.concatenate([re[:, HALF:], im[:, HALF:]], axis=1),
    )


def fold_rows(re, im):
    plus = jnp.concatenate([re[:HALF] + re[HALF:], im[:HALF] + im[HALF:]], axis=0)
    minus = jnp.concatenate([re[:HALF] - re[HALF:], im[:HALF] - im[HALF:]], axis=0)
    return plus, minus


def pair_rows(re, im):
    return (
        jnp.concatenate([re[:HALF], im[:HALF]], axis=0),
        jnp.concatenate([re[HALF:], im[HALF:]], axis=0),
    )


def product(u, v):
    return u[0] * v[0] - u[1] * v[1], u[0] * v[1] + u[1] * v[0]


def conj_product(u, v):
    return u[0] * v[0] + u[1] * v[1], u[0] * v[1] - u[1] * v[0]


def both_right(pairs, table, first, second):
    return [(times_right(p, table, first), times_right(m, table, second)) for p, m in pairs]


def both_left(pairs, table, first, second):
    return [(times_left(table, first, p), times_left(table, second, m)) for p, m in pairs]


def unfold(pairs):
    return [(p + m, p - m) for p, m in pairs]


def propagate(fields, table, adjoint):
    left, right = (TURNED, 0) if adjoint else (0, TURNED)
    pairs = [fold_columns(*f) for f in fields]
    pairs = unfold(both_right(pairs, table, right + P_PLUS, right + P_MINUS))
    pairs = [fold_rows(*pair_columns(*p)) for p in pairs]
    pairs = unfold(both_left(pairs, table, left + P_PLUS, left + P_MINUS))
    return [pair_rows(*p) for p in pairs]


def to_spectrum(fields, table):
    pairs = [fold_columns(*f) for f in fields]
    pairs = both_right(pairs, table, TURNED + F_EVEN, TURNED + F_ODD)
    pairs = [fold_rows(*pair_columns(*p)) for p in pairs]
    pairs = both_left(pairs, table, F_EVEN, F_ODD)
    return [pair_rows(*p) for p in pairs]


def from_spectrum(fields, table):
    pairs = [pair_columns(*f) for f in fields]
    pairs = unfold(both_right(pairs, table, F_EVEN, F_ODD))
    pairs = [pair_rows(*pair_columns(*p)) for p in pairs]
    pairs = unfold(both_left(pairs, table, TURNED + F_EVEN, TURNED + F_ODD))
    return [pair_rows(*p) for p in pairs]


def compute_kernel(
    plan, windows, probes, received, measured, table,
    rows_out, grads,
    amplitude, spread,
):
    depth = lax.axis_index("depth")
    at = jnp.where(depth == 0, OWN_LEFT, PREV_RIGHT)
    jobs = plan[at]
    row = lax.broadcasted_iota(jnp.int32, (N, N), 0)
    lane = lax.broadcasted_iota(jnp.int32, (N, N), 1)
    order = jnp.where(lane < HALF, 2 * lane, 2 * lane - (N - 1))
    shuffle = jnp.where(row == order, 1.0, 0.0).astype(jnp.bfloat16)

    def work(numbers):
        each = range(len(numbers))
        words = [[plan[at + 2 + 5 * j + w] for w in range(5)] for j in numbers]

        for k in each:
            _, _, _, _, slot = words[k]

            @pl.when(depth == 0)
            def _(k=k, slot=slot):
                amplitude[k] = measured[slot]

            @pl.when(depth == 1)
            def _(k=k):
                src = pl.multiple_of(PAD + (plan[PREV_RIGHT + 1] + 8 * numbers[k]) * 8, 8)
                for s in range(2):
                    for c in range(2):
                        amplitude[k, pl.ds(128 * s + 64 * c, 64), :] = received[
                            s, c, pl.ds(src, 64), :
                        ]

        def base_of(k):
            return jnp.where(depth == 0, 0, lax.div(words[k][0], 8))

        def window(k, s):
            r, _, _, start, _ = words[k]
            here = (row >= jnp.where(depth == 0, r, 0)) & (row < jnp.where(depth == 0, N, r))
            src = pl.multiple_of(PAD + (start - base_of(k)) * 8, 8)
            return [
                jnp.where(here, windows[s, numbers[k], c], received[s, c, pl.ds(src, N), :])
                for c in range(2)
            ]

        turned = [[probes[j, c] for c in range(2)] for j in numbers]
        waves = [product(p, window(k, 0)) for k, p in enumerate(turned)]
        waves = propagate(waves, table, False)
        slices = [window(k, 1) for k in each]
        spectra = to_spectrum([product(w, o) for w, o in zip(waves, slices)], table)
        backs = []
        for k in each:
            hi, lo = halves(amplitude[k])
            apart = dot(
                jnp.concatenate([hi, lo], axis=1), jnp.concatenate([shuffle, shuffle], axis=0)
            )
            for h in range(2):
                spread[k, h] = apart[:, HALF * h : HALF * h + HALF]
        for k in each:
            apart = jnp.concatenate(
                [
                    jnp.concatenate(
                        [spread[k, h, pl.ds(p, HALF, stride=2), :] for h in range(2)], axis=1
                    )
                    for p in range(2)
                ],
                axis=0,
            )
            re, im = spectra[k]
            factor = 1.0 - apart * lax.rsqrt(re * re + im * im + 1.0)
            backs.append((re * factor, im * factor))
        backs = from_spectrum(backs, table)
        for k in each:
            grads[1, numbers[k], 0], grads[1, numbers[k], 1] = conj_product(waves[k], backs[k])
        backs = [conj_product(o, b) for o, b in zip(slices, backs)]
        backs = propagate(backs, table, True)
        for k in each:
            grads[0, numbers[k], 0], grads[0, numbers[k], 1] = conj_product(turned[k], backs[k])
        for k in each:
            r, start = words[k][0], words[k][3]
            base = base_of(k)
            count = jnp.where(depth == 0, lax.div(r + 7, 8), 32 - lax.div(r, 8))

            def step(g, carry, k=k, base=base, start=start, count=count):
                for q in range(4):
                    granule = jnp.minimum(4 * g + q, count - 1)
                    src = pl.multiple_of((base + granule) * 8, 8)
                    dst = pl.multiple_of((start + granule) * 8, 8)
                    for s in range(2):
                        for c in range(2):
                            rows_out[s, c, pl.ds(dst, 8), :] = grads[
                                s, numbers[k], c, pl.ds(src, 8), :
                            ]
                return carry

            lax.fori_loop(0, lax.div(count + 3, 4), step, 0)

    @pl.when(jobs >= 2)
    def _():
        work([0, 1])

    @pl.when(lax.rem(jobs, 2) == 1)
    def _():
        work([jobs - 1])


def gather_kernel(plan, rows, tile_in, out, tile, out_sems):
    row = lax.broadcasted_iota(jnp.int32, (CHUNK, N), 0)
    lane = lax.broadcasted_iota(jnp.int32, (CHUNK, N), 1)

    def add(at, j, c, lower):
        r = plan[at + 2 + 5 * j]
        start = plan[at + 2 + 5 * j + 3]
        first = 0 if lower else lax.div(r, CHUNK)
        last = lax.div(r + CHUNK - 1, CHUNK) if lower else N // CHUNK
        skip = 0 if lower else lax.div(r, 8)
        keep = lane >= plan[at + 2 + 5 * j + 2]
        low = pl.multiple_of(plan[at + 2 + 5 * j + 1] * N, N)
        high = pl.multiple_of(plan[at + 2 + 5 * j + 1] * N + N, N)

        def step(g, carry):
            dst = pl.multiple_of(g * CHUNK, CHUNK)
            inside = (row + dst < r) if lower else (row + dst >= r)
            src = pl.multiple_of(CHUNK + (start - skip) * 8 + g * CHUNK, 8)
            value = jnp.where(inside, rows[0 if lower else 1, c, pl.ds(src, CHUNK), :], 0.0)
            tile[c, pl.ds(dst, CHUNK), pl.ds(low, N)] += jnp.where(keep, value, 0.0)
            tile[c, pl.ds(dst, CHUNK), pl.ds(high, N)] += jnp.where(keep, 0.0, value)
            return carry

        lax.fori_loop(first, last, step, 0)

    for c in range(2):
        for at, lower in ((OWN_RIGHT, False), (PREV_LEFT, True)):

            def step(j, carry, at=at, lower=lower, c=c):
                add(at, j, c, lower)
                return carry

            lax.fori_loop(0, plan[at], step, 0)
        pltpu.make_async_copy(tile.at[c], out.at[c], out_sems.at[c]).start()
    for c in range(2):
        pltpu.make_async_copy(tile.at[c], out.at[c], out_sems.at[c]).wait()


SMEM = pl.BlockSpec(memory_space=pltpu.SMEM)
VMEM = pl.BlockSpec(memory_space=pltpu.VMEM)
HBM = pl.BlockSpec(memory_space=pltpu.HBM)


def shape(*dims):
    return jax.ShapeDtypeStruct(dims, jnp.float32)


def shards(n_lat, object_slices, probe, measured, positions, counts):
    columns = object_slices.shape[3]
    tile = object_slices.reshape(object_slices.shape[1:])
    dma = pltpu.SemaphoreType.DMA
    positions = positions.T
    own_plan, prev_positions, prev_counts, tile = pl.pallas_call(
        functools.partial(announce_kernel, n_lat),
        name="announce",
        out_shape=(
            jax.ShapeDtypeStruct((2 * SPAN,), jnp.int32),
            jax.ShapeDtypeStruct(positions.shape, jnp.int32),
            jax.ShapeDtypeStruct(counts.shape, jnp.int32),
            shape(*tile.shape),
        ),
        in_specs=[HBM, HBM, HBM],
        out_specs=(SMEM, VMEM, VMEM, VMEM),
        scratch_shapes=[
            pltpu.SMEM((2, 4), jnp.int32),
            pltpu.SMEM((1,), jnp.int32),
            dma((2,)), dma((2,)), dma((3,)),
        ],
        compiler_params=pltpu.CompilerParams(
            collective_id=2, has_side_effects=True, vmem_limit_bytes=46 << 20
        ),
    )(positions, counts, tile)
    plan, ahead, behind = pl.pallas_call(
        pack_kernel,
        name="pack",
        out_shape=(
            jax.ShapeDtypeStruct((4 * SPAN,), jnp.int32),
            shape(2, ROWS, N),
            shape(2, ROWS, N),
        ),
        in_specs=[SMEM, SMEM, SMEM, VMEM, VMEM],
        out_specs=(SMEM, VMEM, VMEM),
        compiler_params=pltpu.CompilerParams(vmem_limit_bytes=4 << 20),
    )(own_plan, prev_positions, prev_counts, tile, measured)
    received, windows, probes = pl.pallas_call(
        functools.partial(exchange_kernel, n_lat),
        name="exchange",
        out_shape=(
            shape(2, 2, ROWS + 2 * PAD, N),
            shape(2, MAX_JOBS, 2, N, N),
            shape(MAX_JOBS, 2, N, N),
        ),
        in_specs=[SMEM, VMEM, VMEM, VMEM, VMEM],
        out_specs=(VMEM, VMEM, VMEM),
        scratch_shapes=[
            pltpu.VMEM((2, N, columns), jnp.float32),
            dma((2,)), dma((2,)), dma, dma,
        ],
        compiler_params=pltpu.CompilerParams(
            collective_id=0, has_side_effects=True, vmem_limit_bytes=12 << 20
        ),
    )(plan, ahead, behind, tile, probe)

    table = jnp.asarray(tables())
    rows_out, grads = pl.pallas_call(
        compute_kernel,
        name="compute",
        out_shape=(shape(2, 2, ROWS, N), shape(2, MAX_JOBS, 2, N, N)),
        in_specs=[SMEM, VMEM, VMEM, VMEM, VMEM, VMEM],
        out_specs=(VMEM, VMEM),
        scratch_shapes=[
            pltpu.VMEM((2, N, N), jnp.float32),
            pltpu.VMEM((2, 2, N, HALF), jnp.float32),
        ],
        compiler_params=pltpu.CompilerParams(vmem_limit_bytes=30 << 20),
    )(plan, windows, probes, received, measured, table)

    rows_back, tile = pl.pallas_call(
        functools.partial(return_kernel, n_lat),
        name="giveback",
        out_shape=(shape(2, 2, ROWS + 2 * CHUNK, N), shape(2, N, columns)),
        in_specs=[SMEM, VMEM, VMEM],
        out_specs=(VMEM, VMEM),
        scratch_shapes=[
            pltpu.VMEM((MAX_JOBS, 2, N, N), jnp.float32),
            dma((2,)), dma((2,)), dma, dma,
        ],
        compiler_params=pltpu.CompilerParams(
            collective_id=1, has_side_effects=True, vmem_limit_bytes=12 << 20
        ),
    )(plan, rows_out, grads)

    out, _ = pl.pallas_call(
        gather_kernel,
        name="gather",
        out_shape=(shape(2, N, columns), shape(2, N, columns)),
        in_specs=[SMEM, VMEM, VMEM],
        out_specs=(HBM, VMEM),
        scratch_shapes=[dma((2,))],
        input_output_aliases={2: 1},
        compiler_params=pltpu.CompilerParams(vmem_limit_bytes=12 << 20),
    )(plan, rows_back, tile)
    return out.reshape(object_slices.shape)


def solution(mesh):
    return jax.shard_map(
        functools.partial(shards, mesh.shape["lat"]),
        mesh=mesh,
        in_specs=(
            P("depth", None, "lat", None),
            P(),
            P("lat", None, None),
            P("lat", None),
            P("lat"),
        ),
        out_specs=P("depth", None, "lat", None),
        check_vma=False,
    )
```

```python
import functools

import jax
import jax.numpy as jnp
import ml_dtypes
import numpy as np
from jax import lax
from jax.experimental import pallas as pl
from jax.experimental.pallas import tpu as pltpu
from jax.sharding import PartitionSpec as P

N = 256
HALF = 128
STRENGTH = 8.0
MAX_JOBS = 3
BUDGET = 48
ROWS = 8 * BUDGET
PAD = 256
CHUNK = 32
SPAN = 20


def split_bf16(a):
    hi = a.astype(np.float32).astype(ml_dtypes.bfloat16)
    lo = (a - hi.astype(np.float64)).astype(np.float32).astype(ml_dtypes.bfloat16)
    return hi, lo


def tables():
    index = np.arange(N)
    angle = 2.0 * np.pi * ((index[:, None] * index[None, :]) % N) / N
    dft = np.exp(-1j * angle) / 16.0
    centred = (index - N * (index >= HALF)) / N
    turn = np.exp(1j * np.pi * STRENGTH * centred**2)
    prop = np.conj(dft) @ (turn[:, None] * dft)
    c0, c1 = prop[:HALF, :HALF], prop[:HALF, HALF:]

    def real_form(m):
        return np.block([[m.real, -m.imag], [m.imag, m.real]])

    forms = [real_form(m) for m in ((c0 + c1) / 2, (c0 - c1) / 2, dft[0::2, :HALF], dft[1::2, :HALF])]
    forms = forms + [m.T for m in forms]
    return np.stack([np.stack(split_bf16(m)) for m in forms])


OWN_LEFT, OWN_RIGHT, PREV_LEFT, PREV_RIGHT = 0, SPAN, 2 * SPAN, 3 * SPAN


def choose_sides(rows_of, cols_of, live):
    up = [lax.div(rows_of[i] + 7, 8) for i in range(4)]
    down = [32 - lax.div(rows_of[i], 8) for i in range(4)]
    best = jnp.int32(1 << 20)
    pick = jnp.int32(0)
    for mask in range(16):
        right = [(mask >> i) & 1 for i in range(4)]
        n_right = sum(right)
        if n_right > MAX_JOBS:
            continue
        top = max([i + 1 for i in range(4) if right[i]], default=0)
        lefts = [jnp.where(live > i, up[i], 0) for i in range(4) if not right[i]]
        cost_left = sum(lefts, jnp.int32(0))
        cost_right = sum([down[i] + 8 for i in range(4) if right[i]], jnp.int32(0))
        widest = jnp.maximum(cost_left, cost_right)
        most = jnp.maximum(live - n_right, n_right)
        bad = (live < top) | (widest > BUDGET) | (most > MAX_JOBS)
        key = most * 64 + widest + jnp.where(bad, jnp.int32(1 << 16), 0)
        pick = jnp.where(key < best, mask, pick)
        best = jnp.minimum(key, best)
    blocks = [jnp.minimum(lax.div(cols_of[i], N), 6) for i in range(4)]
    sides = []
    for side in range(2):
        mine = [(live > i) & ((lax.shift_right_logical(pick, i) & 1) == side) for i in range(4)]
        size = up if side == 0 else down
        count, total = jnp.int32(0), jnp.int32(0)
        words = [[jnp.int32(0)] * 5 for _ in range(MAX_JOBS)]
        for i in range(4):
            fields = [rows_of[i], blocks[i], cols_of[i] - blocks[i] * N, total, jnp.int32(i)]
            for j in range(MAX_JOBS):
                here = mine[i] & (count == j)
                words[j] = [jnp.where(here, f, w) for f, w in zip(fields, words[j])]
            count = count + jnp.where(mine[i], 1, 0)
            total = total + jnp.where(mine[i], size[i], 0)
        sides.append([count, total] + [w for job in words for w in job])
    return sides


def lanes():
    return lax.broadcasted_iota(jnp.int32, (8, N), 1)


def announce_kernel(
    n_lat, pos_hbm, cnt, tile_hbm,
    own_plan, prev_pos, prev_cnt, tile,
    pos, live, send, recv, local,
):
    depth = lax.axis_index("depth")
    lat = lax.axis_index("lat")
    after = lax.rem(lat + 1, n_lat)
    before = lax.rem(lat + n_lat - 1, n_lat)
    barrier = pltpu.get_barrier_semaphore()
    pl.semaphore_signal(
        barrier, inc=1, device_id=(depth, before), device_id_type=pl.DeviceIdType.MESH
    )
    loads = [
        pltpu.make_async_copy(tile_hbm, tile, local.at[0]),
        pltpu.make_async_copy(pos_hbm, pos, local.at[1]),
        pltpu.make_async_copy(cnt, live, local.at[2]),
    ]
    for load in loads:
        load.start()
    pl.semaphore_wait(barrier, 1)
    copies = [
        remote(pos_hbm, prev_pos, send.at[0], recv.at[0], depth, after),
        remote(cnt, prev_cnt, send.at[1], recv.at[1], depth, after),
    ]
    for copy in copies:
        copy.start()
    for load in loads[1:]:
        load.wait()
    own = choose_sides([pos[0, i] for i in range(4)], [pos[1, i] for i in range(4)], live[0])
    for k, side in enumerate(own):
        for w, word in enumerate(side):
            own_plan[k * SPAN + w] = word
    loads[0].wait()
    for copy in copies:
        copy.wait()


def pack_kernel(
    own_plan, prev_pos, prev_cnt, tile, measured, plan, ahead, behind
):
    depth = lax.axis_index("depth")
    prev = choose_sides(
        [prev_pos[0, i] for i in range(4)], [prev_pos[1, i] for i in range(4)], prev_cnt[0]
    )
    for k, side in enumerate(prev):
        for w, word in enumerate(side):
            plan[k * SPAN + w] = own_plan[k * SPAN + w]
            plan[PREV_LEFT + k * SPAN + w] = word

    def copy_rows(out, at, j, first, count):
        start = plan[at + 2 + 5 * j + 3]
        low = pl.multiple_of(plan[at + 2 + 5 * j + 1] * N, N)
        high = pl.multiple_of(plan[at + 2 + 5 * j + 1] * N + N, N)
        keep = lanes() >= plan[at + 2 + 5 * j + 2]

        def step(g, carry):
            for k in range(4):
                granule = jnp.minimum(4 * g + k, count - 1)
                src = pl.multiple_of((first + granule) * 8, 8)
                dst = pl.multiple_of((start + granule) * 8, 8)
                for c in range(2):
                    out[c, pl.ds(dst, 8), :] = jnp.where(
                        keep,
                        tile[c, pl.ds(src, 8), pl.ds(low, N)],
                        tile[c, pl.ds(src, 8), pl.ds(high, N)],
                    )
            return carry

        lax.fori_loop(0, lax.div(count + 3, 4), step, 0)

    def right_job(j, carry):
        first = lax.div(plan[OWN_RIGHT + 2 + 5 * j], 8)
        copy_rows(ahead, OWN_RIGHT, j, first, 32 - first)
        slot = plan[OWN_RIGHT + 2 + 5 * j + 4]
        dst = pl.multiple_of((plan[OWN_RIGHT + 1] + 8 * j) * 8, 8)
        for c in range(2):
            src = pl.multiple_of(depth * HALF + 64 * c, 64)
            ahead[c, pl.ds(dst, 64), :] = measured[slot, pl.ds(src, 64), :]
        return carry

    lax.fori_loop(0, plan[OWN_RIGHT], right_job, 0)

    def left_job(j, carry):
        copy_rows(behind, PREV_LEFT, j, 0, lax.div(plan[PREV_LEFT + 2 + 5 * j] + 7, 8))
        return carry

    lax.fori_loop(0, plan[PREV_LEFT], left_job, 0)


def exchange_kernel(
    n_lat, plan, ahead, behind, tile, probe, received, windows, probes,
    other, row_send, row_recv, tile_send, tile_recv,
):
    depth = lax.axis_index("depth")
    lat = lax.axis_index("lat")
    after = lax.rem(lat + 1, n_lat)
    before = lax.rem(lat + n_lat - 1, n_lat)
    origin = jnp.where(depth == 0, after, before)
    greet([(0, origin), (1, origin), (1 - depth, lat)])

    def slot(s):
        return received.at[s, :, pl.ds(PAD, ROWS), :]

    sends = [
        remote(ahead, slot(depth), row_send.at[0], row_recv.at[depth], 1, after),
        remote(behind, slot(depth), row_send.at[1], row_recv.at[depth], 0, before),
    ]
    for copy in sends:
        copy.start()
    swap = remote(tile, other, tile_send, tile_recv, 1 - depth, lat)
    swap.start()
    at = jnp.where(depth == 0, OWN_LEFT, PREV_RIGHT)
    def turn(i, carry):
        j, c = lax.div(i, 2), lax.rem(i, 2)
        shift = plan[at + 2 + 5 * j + 2]
        shift = jnp.where(shift == N, 0, shift)
        probes[j, c] = pltpu.roll(pltpu.roll(probe[c], plan[at + 2 + 5 * j], 0), shift, 1)
        return carry

    lax.fori_loop(0, 2 * MAX_JOBS, turn, 0)
    pick_columns(plan, at, tile, windows, depth)
    swap.wait()
    pick_columns(plan, at, other, windows, 1 - depth)
    for copy in sends:
        copy.wait_send()
    for s in range(2):
        remote(ahead, slot(s), row_send.at[0], row_recv.at[s], 1, after).wait_recv()


def pick_columns(plan, at, source, windows, s):
    lane = lanes()
    columns = [
        plan[at + 2 + 5 * j + 1] * N + plan[at + 2 + 5 * j + 2] for j in range(MAX_JOBS)
    ]

    def step(g, carry):
        rows = pl.ds(pl.multiple_of(g * 8, 8), 8)
        for c in range(2):
            picked = [jnp.zeros((8, N), jnp.float32)] * MAX_JOBS
            for q in range(source.shape[2] // N):
                value = source[c, rows, q * N : q * N + N]
                for j, column in enumerate(columns):
                    offset = lane + (q * N - column)
                    picked[j] = jnp.where((offset >= 0) & (offset < N), value, picked[j])
            for j in range(MAX_JOBS):
                windows[s, j, c, rows, :] = picked[j]
        return carry

    lax.fori_loop(0, N // 8, step, 0)


def remote(src, dst, send, recv, depth, lat):
    return pltpu.make_async_remote_copy(
        src_ref=src,
        dst_ref=dst,
        send_sem=send,
        recv_sem=recv,
        device_id=(depth, lat),
        device_id_type=pl.DeviceIdType.MESH,
    )


def greet(sources):
    barrier = pltpu.get_barrier_semaphore()
    for source in sources:
        pl.semaphore_signal(
            barrier, inc=1, device_id=source, device_id_type=pl.DeviceIdType.MESH
        )
    pl.semaphore_wait(barrier, 3)


def return_kernel(
    n_lat, plan, rows, windows, received, tile,
    partner, row_send, row_recv, swap_send, swap_recv,
):
    depth = lax.axis_index("depth")
    lat = lax.axis_index("lat")
    after = lax.rem(lat + 1, n_lat)
    before = lax.rem(lat + n_lat - 1, n_lat)
    greet([(0, before), (1, after), (1 - depth, lat)])
    target = jnp.where(depth == 0, after, before)

    def part(c):
        return received.at[c, :, pl.ds(CHUNK, ROWS), :]

    sends = [
        remote(rows.at[s], part(depth), row_send.at[s], row_recv.at[depth], s, target)
        for s in range(2)
    ]
    for copy in sends:
        copy.start()
    swap = remote(windows.at[1 - depth], partner, swap_send, swap_recv, 1 - depth, lat)
    swap.start()
    sum_windows(plan, depth, lambda j, c, at: windows[depth, j, c, at, :], tile, True)
    swap.wait()
    sum_windows(plan, 1 - depth, lambda j, c, at: partner[j, c, at, :], tile, False)
    for copy in sends:
        copy.wait_send()
    for c in range(2):
        remote(rows.at[0], part(c), row_send.at[0], row_recv.at[c], 0, target).wait_recv()


def sum_windows(plan, core, read, tile, first):
    at = jnp.where(core == 0, OWN_LEFT, PREV_RIGHT)
    row = lax.broadcasted_iota(jnp.int32, (8, N), 0)
    lane = lanes()
    jobs = []
    for j in range(MAX_JOBS):
        r = plan[at + 2 + 5 * j]
        low = jnp.where(core == 0, r, 0)
        high = jnp.where(plan[at] > j, jnp.where(core == 0, N, r), 0)
        jobs.append((low, high, plan[at + 2 + 5 * j + 1] * N + plan[at + 2 + 5 * j + 2]))

    def step(g, carry):
        dst = pl.ds(pl.multiple_of(g * 8, 8), 8)
        here = row + g * 8
        for c in range(2):
            values = [
                jnp.where((here >= low) & (here < high), read(j, c, dst), 0.0)
                for j, (low, high, _) in enumerate(jobs)
            ]
            for q in range(tile.shape[2] // N):
                total = None if first else tile[c, dst, q * N : q * N + N]
                for value, (_, _, column) in zip(values, jobs):
                    offset = lane + (q * N - column)
                    inside = (offset >= 0) & (offset < N)
                    value = jnp.where(inside, value, 0.0)
                    total = value if total is None else total + value
                tile[c, dst, q * N : q * N + N] = total
        return carry

    lax.fori_loop(0, N // 8, step, 0)


P_PLUS, P_MINUS, F_EVEN, F_ODD = 0, 1, 2, 3
TURNED = 4


def halves(x):
    hi = x.astype(jnp.bfloat16)
    lo = (x - hi.astype(jnp.float32)).astype(jnp.bfloat16)
    return hi, lo


def dot(a, b):
    return jnp.dot(a, b, preferred_element_type=jnp.float32)


def times_right(x, table, at):
    hi, lo = halves(x)
    return dot(
        jnp.concatenate([hi, lo, hi], axis=1),
        jnp.concatenate([table[at, 0], table[at, 0], table[at, 1]], axis=0),
    )


def times_left(table, at, x):
    hi, lo = halves(x)
    return dot(
        jnp.concatenate([table[at, 0], table[at, 0], table[at, 1]], axis=1),
        jnp.concatenate([hi, lo, hi], axis=0),
    )


def fold_columns(re, im):
    plus = jnp.concatenate([re[:, :HALF] + re[:, HALF:], im[:, :HALF] + im[:, HALF:]], axis=1)
    minus = jnp.concatenate([re[:, :HALF] - re[:, HALF:], im[:, :HALF] - im[:, HALF:]], axis=1)
    return plus, minus


def pair_columns(re, im):
    return (
        jnp.concatenate([re[:, :HALF], im[:, :HALF]], axis=1),
        jnp.concatenate([re[:, HALF:], im[:, HALF:]], axis=1),
    )


def fold_rows(re, im):
    plus = jnp.concatenate([re[:HALF] + re[HALF:], im[:HALF] + im[HALF:]], axis=0)
    minus = jnp.concatenate([re[:HALF] - re[HALF:], im[:HALF] - im[HALF:]], axis=0)
    return plus, minus


def pair_rows(re, im):
    return (
        jnp.concatenate([re[:HALF], im[:HALF]], axis=0),
        jnp.concatenate([re[HALF:], im[HALF:]], axis=0),
    )


def product(u, v):
    return u[0] * v[0] - u[1] * v[1], u[0] * v[1] + u[1] * v[0]


def conj_product(u, v):
    return u[0] * v[0] + u[1] * v[1], u[0] * v[1] - u[1] * v[0]


def both_right(pairs, table, first, second):
    return [(times_right(p, table, first), times_right(m, table, second)) for p, m in pairs]


def both_left(pairs, table, first, second):
    return [(times_left(table, first, p), times_left(table, second, m)) for p, m in pairs]


def unfold(pairs):
    return [(p + m, p - m) for p, m in pairs]


def propagate(fields, table, adjoint):
    left, right = (TURNED, 0) if adjoint else (0, TURNED)
    pairs = [fold_columns(*f) for f in fields]
    pairs = unfold(both_right(pairs, table, right + P_PLUS, right + P_MINUS))
    pairs = [fold_rows(*pair_columns(*p)) for p in pairs]
    pairs = unfold(both_left(pairs, table, left + P_PLUS, left + P_MINUS))
    return [pair_rows(*p) for p in pairs]


def to_spectrum(fields, table):
    pairs = [fold_columns(*f) for f in fields]
    pairs = both_right(pairs, table, TURNED + F_EVEN, TURNED + F_ODD)
    pairs = [fold_rows(*pair_columns(*p)) for p in pairs]
    pairs = both_left(pairs, table, F_EVEN, F_ODD)
    return [pair_rows(*p) for p in pairs]


def from_spectrum(fields, table):
    pairs = [pair_columns(*f) for f in fields]
    pairs = unfold(both_right(pairs, table, F_EVEN, F_ODD))
    pairs = [pair_rows(*pair_columns(*p)) for p in pairs]
    pairs = unfold(both_left(pairs, table, TURNED + F_EVEN, TURNED + F_ODD))
    return [pair_rows(*p) for p in pairs]


def compute_kernel(
    plan, windows, probes, received, measured, table,
    rows_out, grads,
    amplitude, spread,
):
    depth = lax.axis_index("depth")
    at = jnp.where(depth == 0, OWN_LEFT, PREV_RIGHT)
    jobs = plan[at]
    row = lax.broadcasted_iota(jnp.int32, (N, N), 0)
    lane = lax.broadcasted_iota(jnp.int32, (N, N), 1)
    order = jnp.where(lane < HALF, 2 * lane, 2 * lane - (N - 1))
    shuffle = jnp.where(row == order, 1.0, 0.0).astype(jnp.bfloat16)

    def work(numbers):
        each = range(len(numbers))
        words = [[plan[at + 2 + 5 * j + w] for w in range(5)] for j in numbers]

        for k in each:
            _, _, _, _, slot = words[k]

            @pl.when(depth == 0)
            def _(k=k, slot=slot):
                amplitude[k] = measured[slot]

            @pl.when(depth == 1)
            def _(k=k):
                src = pl.multiple_of(PAD + (plan[PREV_RIGHT + 1] + 8 * numbers[k]) * 8, 8)
                for s in range(2):
                    for c in range(2):
                        amplitude[k, pl.ds(128 * s + 64 * c, 64), :] = received[
                            s, c, pl.ds(src, 64), :
                        ]

        def base_of(k):
            return jnp.where(depth == 0, 0, lax.div(words[k][0], 8))

        def window(k, s):
            r, _, _, start, _ = words[k]
            here = (row >= jnp.where(depth == 0, r, 0)) & (row < jnp.where(depth == 0, N, r))
            src = pl.multiple_of(PAD + (start - base_of(k)) * 8, 8)
            return [
                jnp.where(here, windows[s, numbers[k], c], received[s, c, pl.ds(src, N), :])
                for c in range(2)
            ]

        turned = [[probes[j, c] for c in range(2)] for j in numbers]
        waves = [product(p, window(k, 0)) for k, p in enumerate(turned)]
        waves = propagate(waves, table, False)
        slices = [window(k, 1) for k in each]
        spectra = to_spectrum([product(w, o) for w, o in zip(waves, slices)], table)
        backs = []
        for k in each:
            hi, lo = halves(amplitude[k])
            apart = dot(
                jnp.concatenate([hi, lo], axis=1), jnp.concatenate([shuffle, shuffle], axis=0)
            )
            for h in range(2):
                spread[k, h] = apart[:, HALF * h : HALF * h + HALF]
        for k in each:
            apart = jnp.concatenate(
                [
                    jnp.concatenate(
                        [spread[k, h, pl.ds(p, HALF, stride=2), :] for h in range(2)], axis=1
                    )
                    for p in range(2)
                ],
                axis=0,
            )
            re, im = spectra[k]
            factor = 1.0 - apart * lax.rsqrt(re * re + im * im + 1.0)
            backs.append((re * factor, im * factor))
        backs = from_spectrum(backs, table)
        for k in each:
            grads[1, numbers[k], 0], grads[1, numbers[k], 1] = conj_product(waves[k], backs[k])
        backs = [conj_product(o, b) for o, b in zip(slices, backs)]
        backs = propagate(backs, table, True)
        for k in each:
            grads[0, numbers[k], 0], grads[0, numbers[k], 1] = conj_product(turned[k], backs[k])
        for k in each:
            r, start = words[k][0], words[k][3]
            base = base_of(k)
            count = jnp.where(depth == 0, lax.div(r + 7, 8), 32 - lax.div(r, 8))

            def step(g, carry, k=k, base=base, start=start, count=count):
                for q in range(4):
                    granule = jnp.minimum(4 * g + q, count - 1)
                    src = pl.multiple_of((base + granule) * 8, 8)
                    dst = pl.multiple_of((start + granule) * 8, 8)
                    for s in range(2):
                        for c in range(2):
                            rows_out[s, c, pl.ds(dst, 8), :] = grads[
                                s, numbers[k], c, pl.ds(src, 8), :
                            ]
                return carry

            lax.fori_loop(0, lax.div(count + 3, 4), step, 0)

    @pl.when(jobs >= 2)
    def _():
        work([0, 1])

    @pl.when(lax.rem(jobs, 2) == 1)
    def _():
        work([jobs - 1])


def gather_kernel(plan, rows, tile_in, out, tile, out_sems):
    row = lax.broadcasted_iota(jnp.int32, (CHUNK, N), 0)
    lane = lax.broadcasted_iota(jnp.int32, (CHUNK, N), 1)

    def stores(c):
        return [
            pltpu.make_async_copy(
                tile.at[c, pl.ds(64 * q, 64)], out.at[c, pl.ds(64 * q, 64)], out_sems.at[c, q]
            )
            for q in range(N // 64)
        ]

    def add(at, j, c, lower):
        r = plan[at + 2 + 5 * j]
        start = plan[at + 2 + 5 * j + 3]
        first = 0 if lower else lax.div(r, CHUNK)
        last = lax.div(r + CHUNK - 1, CHUNK) if lower else N // CHUNK
        skip = 0 if lower else lax.div(r, 8)
        keep = lane >= plan[at + 2 + 5 * j + 2]
        low = pl.multiple_of(plan[at + 2 + 5 * j + 1] * N, N)
        high = pl.multiple_of(plan[at + 2 + 5 * j + 1] * N + N, N)

        def step(g, carry):
            dst = pl.multiple_of(g * CHUNK, CHUNK)
            inside = (row + dst < r) if lower else (row + dst >= r)
            src = pl.multiple_of(CHUNK + (start - skip) * 8 + g * CHUNK, 8)
            value = jnp.where(inside, rows[0 if lower else 1, c, pl.ds(src, CHUNK), :], 0.0)
            tile[c, pl.ds(dst, CHUNK), pl.ds(low, N)] += jnp.where(keep, value, 0.0)
            tile[c, pl.ds(dst, CHUNK), pl.ds(high, N)] += jnp.where(keep, 0.0, value)
            return carry

        lax.fori_loop(first, last, step, 0)

    for c in range(2):
        for at, lower in ((OWN_RIGHT, False), (PREV_LEFT, True)):

            def step(j, carry, at=at, lower=lower, c=c):
                add(at, j, c, lower)
                return carry

            lax.fori_loop(0, plan[at], step, 0)
        for copy in stores(c):
            copy.start()
    for c in range(2):
        for copy in stores(c):
            copy.wait()


SMEM = pl.BlockSpec(memory_space=pltpu.SMEM)
VMEM = pl.BlockSpec(memory_space=pltpu.VMEM)
HBM = pl.BlockSpec(memory_space=pltpu.HBM)


def shape(*dims):
    return jax.ShapeDtypeStruct(dims, jnp.float32)


def shards(n_lat, object_slices, probe, measured, positions, counts):
    columns = object_slices.shape[3]
    tile = object_slices.reshape(object_slices.shape[1:])
    dma = pltpu.SemaphoreType.DMA
    positions = positions.T
    own_plan, prev_positions, prev_counts, tile = pl.pallas_call(
        functools.partial(announce_kernel, n_lat),
        name="announce",
        out_shape=(
            jax.ShapeDtypeStruct((2 * SPAN,), jnp.int32),
            jax.ShapeDtypeStruct(positions.shape, jnp.int32),
            jax.ShapeDtypeStruct(counts.shape, jnp.int32),
            shape(*tile.shape),
        ),
        in_specs=[HBM, HBM, HBM],
        out_specs=(SMEM, VMEM, VMEM, VMEM),
        scratch_shapes=[
            pltpu.SMEM((2, 4), jnp.int32),
            pltpu.SMEM((1,), jnp.int32),
            dma((2,)), dma((2,)), dma((3,)),
        ],
        compiler_params=pltpu.CompilerParams(
            collective_id=2, has_side_effects=True, vmem_limit_bytes=46 << 20
        ),
    )(positions, counts, tile)
    plan, ahead, behind = pl.pallas_call(
        pack_kernel,
        name="pack",
        out_shape=(
            jax.ShapeDtypeStruct((4 * SPAN,), jnp.int32),
            shape(2, ROWS, N),
            shape(2, ROWS, N),
        ),
        in_specs=[SMEM, SMEM, SMEM, VMEM, VMEM],
        out_specs=(SMEM, VMEM, VMEM),
        compiler_params=pltpu.CompilerParams(vmem_limit_bytes=4 << 20),
    )(own_plan, prev_positions, prev_counts, tile, measured)
    received, windows, probes = pl.pallas_call(
        functools.partial(exchange_kernel, n_lat),
        name="exchange",
        out_shape=(
            shape(2, 2, ROWS + 2 * PAD, N),
            shape(2, MAX_JOBS, 2, N, N),
            shape(MAX_JOBS, 2, N, N),
        ),
        in_specs=[SMEM, VMEM, VMEM, VMEM, VMEM],
        out_specs=(VMEM, VMEM, VMEM),
        scratch_shapes=[
            pltpu.VMEM((2, N, columns), jnp.float32),
            dma((2,)), dma((2,)), dma, dma,
        ],
        compiler_params=pltpu.CompilerParams(
            collective_id=0, has_side_effects=True, vmem_limit_bytes=12 << 20
        ),
    )(plan, ahead, behind, tile, probe)

    table = jnp.asarray(tables())
    rows_out, grads = pl.pallas_call(
        compute_kernel,
        name="compute",
        out_shape=(shape(2, 2, ROWS, N), shape(2, MAX_JOBS, 2, N, N)),
        in_specs=[SMEM, VMEM, VMEM, VMEM, VMEM, VMEM],
        out_specs=(VMEM, VMEM),
        scratch_shapes=[
            pltpu.VMEM((2, N, N), jnp.float32),
            pltpu.VMEM((2, 2, N, HALF), jnp.float32),
        ],
        compiler_params=pltpu.CompilerParams(vmem_limit_bytes=30 << 20),
    )(plan, windows, probes, received, measured, table)

    rows_back, tile = pl.pallas_call(
        functools.partial(return_kernel, n_lat),
        name="giveback",
        out_shape=(shape(2, 2, ROWS + 2 * CHUNK, N), shape(2, N, columns)),
        in_specs=[SMEM, VMEM, VMEM],
        out_specs=(VMEM, VMEM),
        scratch_shapes=[
            pltpu.VMEM((MAX_JOBS, 2, N, N), jnp.float32),
            dma((2,)), dma((2,)), dma, dma,
        ],
        compiler_params=pltpu.CompilerParams(
            collective_id=1, has_side_effects=True, vmem_limit_bytes=12 << 20
        ),
    )(plan, rows_out, grads)

    out, _ = pl.pallas_call(
        gather_kernel,
        name="gather",
        out_shape=(shape(2, N, columns), shape(2, N, columns)),
        in_specs=[SMEM, VMEM, VMEM],
        out_specs=(HBM, VMEM),
        scratch_shapes=[dma((2, N // 64))],
        input_output_aliases={2: 1},
        compiler_params=pltpu.CompilerParams(vmem_limit_bytes=12 << 20),
    )(plan, rows_back, tile)
    return out.reshape(object_slices.shape)


def solution(mesh):
    return jax.shard_map(
        functools.partial(shards, mesh.shape["lat"]),
        mesh=mesh,
        in_specs=(
            P("depth", None, "lat", None),
            P(),
            P("lat", None, None),
            P("lat", None),
            P("lat"),
        ),
        out_specs=P("depth", None, "lat", None),
        check_vma=False,
    )
```

```python
import functools

import jax
import jax.numpy as jnp
import ml_dtypes
import numpy as np
from jax import lax
from jax.experimental import pallas as pl
from jax.experimental.pallas import tpu as pltpu
from jax.sharding import PartitionSpec as P

N = 256
HALF = 128
STRENGTH = 8.0
MAX_JOBS = 3
BUDGET = 48
ROWS = 8 * BUDGET
PAD = 256
CHUNK = 32
SPAN = 20


def split_bf16(a):
    hi = a.astype(np.float32).astype(ml_dtypes.bfloat16)
    lo = (a - hi.astype(np.float64)).astype(np.float32).astype(ml_dtypes.bfloat16)
    return hi, lo


def tables():
    index = np.arange(N)
    angle = 2.0 * np.pi * ((index[:, None] * index[None, :]) % N) / N
    dft = np.exp(-1j * angle) / 16.0
    centred = (index - N * (index >= HALF)) / N
    turn = np.exp(1j * np.pi * STRENGTH * centred**2)
    prop = np.conj(dft) @ (turn[:, None] * dft)
    c0, c1 = prop[:HALF, :HALF], prop[:HALF, HALF:]

    def real_form(m):
        return np.block([[m.real, -m.imag], [m.imag, m.real]])

    forms = [real_form(m) for m in ((c0 + c1) / 2, (c0 - c1) / 2, dft[0::2, :HALF], dft[1::2, :HALF])]
    forms = forms + [m.T for m in forms]
    return np.stack([np.stack(split_bf16(m)) for m in forms])


OWN_LEFT, OWN_RIGHT, PREV_LEFT, PREV_RIGHT = 0, SPAN, 2 * SPAN, 3 * SPAN


def choose_sides(rows_of, cols_of, live):
    up = [lax.div(rows_of[i] + 7, 8) for i in range(4)]
    down = [32 - lax.div(rows_of[i], 8) for i in range(4)]
    best = jnp.int32(1 << 20)
    pick = jnp.int32(0)
    for mask in range(16):
        right = [(mask >> i) & 1 for i in range(4)]
        n_right = sum(right)
        if n_right > MAX_JOBS:
            continue
        top = max([i + 1 for i in range(4) if right[i]], default=0)
        lefts = [jnp.where(live > i, up[i], 0) for i in range(4) if not right[i]]
        cost_left = sum(lefts, jnp.int32(0))
        cost_right = sum([down[i] + 8 for i in range(4) if right[i]], jnp.int32(0))
        widest = jnp.maximum(cost_left, cost_right)
        most = jnp.maximum(live - n_right, n_right)
        bad = (live < top) | (widest > BUDGET) | (most > MAX_JOBS)
        key = most * 64 + widest + jnp.where(bad, jnp.int32(1 << 16), 0)
        pick = jnp.where(key < best, mask, pick)
        best = jnp.minimum(key, best)
    blocks = [jnp.minimum(lax.div(cols_of[i], N), 6) for i in range(4)]
    sides = []
    for side in range(2):
        mine = [(live > i) & ((lax.shift_right_logical(pick, i) & 1) == side) for i in range(4)]
        size = up if side == 0 else down
        count, total = jnp.int32(0), jnp.int32(0)
        words = [[jnp.int32(0)] * 5 for _ in range(MAX_JOBS)]
        for i in range(4):
            fields = [rows_of[i], blocks[i], cols_of[i] - blocks[i] * N, total, jnp.int32(i)]
            for j in range(MAX_JOBS):
                here = mine[i] & (count == j)
                words[j] = [jnp.where(here, f, w) for f, w in zip(fields, words[j])]
            count = count + jnp.where(mine[i], 1, 0)
            total = total + jnp.where(mine[i], size[i], 0)
        sides.append([count, total] + [w for job in words for w in job])
    return sides


def lanes():
    return lax.broadcasted_iota(jnp.int32, (8, N), 1)


def announce_kernel(
    n_lat, pos_hbm, cnt, tile_hbm,
    own_plan, prev_pos, prev_cnt, tile,
    pos, live, send, recv, local,
):
    depth = lax.axis_index("depth")
    lat = lax.axis_index("lat")
    after = lax.rem(lat + 1, n_lat)
    before = lax.rem(lat + n_lat - 1, n_lat)
    barrier = pltpu.get_barrier_semaphore()
    pl.semaphore_signal(
        barrier, inc=1, device_id=(depth, before), device_id_type=pl.DeviceIdType.MESH
    )
    loads = [
        pltpu.make_async_copy(pos_hbm, pos, local.at[0]),
        pltpu.make_async_copy(cnt, live, local.at[1]),
    ] + [
        pltpu.make_async_copy(
            tile_hbm.at[c, pl.ds(HALF * h, HALF)],
            tile.at[c, pl.ds(HALF * h, HALF)],
            local.at[2 + 2 * c + h],
        )
        for c in range(2)
        for h in range(2)
    ]
    for load in loads:
        load.start()
    pl.semaphore_wait(barrier, 1)
    copies = [
        remote(pos_hbm, prev_pos, send.at[0], recv.at[0], depth, after),
        remote(cnt, prev_cnt, send.at[1], recv.at[1], depth, after),
    ]
    for copy in copies:
        copy.start()
    for load in loads[:2]:
        load.wait()
    own = choose_sides([pos[0, i] for i in range(4)], [pos[1, i] for i in range(4)], live[0])
    for k, side in enumerate(own):
        for w, word in enumerate(side):
            own_plan[k * SPAN + w] = word
    for load in loads[2:]:
        load.wait()
    for copy in copies:
        copy.wait()


def pack_kernel(
    own_plan, prev_pos, prev_cnt, tile, measured, plan, ahead, behind
):
    depth = lax.axis_index("depth")
    prev = choose_sides(
        [prev_pos[0, i] for i in range(4)], [prev_pos[1, i] for i in range(4)], prev_cnt[0]
    )
    for k, side in enumerate(prev):
        for w, word in enumerate(side):
            plan[k * SPAN + w] = own_plan[k * SPAN + w]
            plan[PREV_LEFT + k * SPAN + w] = word

    def copy_rows(out, at, j, first, count):
        start = plan[at + 2 + 5 * j + 3]
        low = pl.multiple_of(plan[at + 2 + 5 * j + 1] * N, N)
        high = pl.multiple_of(plan[at + 2 + 5 * j + 1] * N + N, N)
        keep = lanes() >= plan[at + 2 + 5 * j + 2]

        def step(g, carry):
            for k in range(4):
                granule = jnp.minimum(4 * g + k, count - 1)
                src = pl.multiple_of((first + granule) * 8, 8)
                dst = pl.multiple_of((start + granule) * 8, 8)
                for c in range(2):
                    out[c, pl.ds(dst, 8), :] = jnp.where(
                        keep,
                        tile[c, pl.ds(src, 8), pl.ds(low, N)],
                        tile[c, pl.ds(src, 8), pl.ds(high, N)],
                    )
            return carry

        lax.fori_loop(0, lax.div(count + 3, 4), step, 0)

    def right_job(j, carry):
        first = lax.div(plan[OWN_RIGHT + 2 + 5 * j], 8)
        copy_rows(ahead, OWN_RIGHT, j, first, 32 - first)
        slot = plan[OWN_RIGHT + 2 + 5 * j + 4]
        dst = pl.multiple_of((plan[OWN_RIGHT + 1] + 8 * j) * 8, 8)
        for c in range(2):
            src = pl.multiple_of(depth * HALF + 64 * c, 64)
            ahead[c, pl.ds(dst, 64), :] = measured[slot, pl.ds(src, 64), :]
        return carry

    lax.fori_loop(0, plan[OWN_RIGHT], right_job, 0)

    def left_job(j, carry):
        copy_rows(behind, PREV_LEFT, j, 0, lax.div(plan[PREV_LEFT + 2 + 5 * j] + 7, 8))
        return carry

    lax.fori_loop(0, plan[PREV_LEFT], left_job, 0)


def exchange_kernel(
    n_lat, plan, ahead, behind, tile, probe, received, windows, probes,
    other, row_send, row_recv, tile_send, tile_recv,
):
    depth = lax.axis_index("depth")
    lat = lax.axis_index("lat")
    after = lax.rem(lat + 1, n_lat)
    before = lax.rem(lat + n_lat - 1, n_lat)
    origin = jnp.where(depth == 0, after, before)
    greet([(0, origin), (1, origin), (1 - depth, lat)])

    def slot(s):
        return received.at[s, :, pl.ds(PAD, ROWS), :]

    sends = [
        remote(ahead, slot(depth), row_send.at[0], row_recv.at[depth], 1, after),
        remote(behind, slot(depth), row_send.at[1], row_recv.at[depth], 0, before),
    ]
    for copy in sends:
        copy.start()
    swap = remote(tile, other, tile_send, tile_recv, 1 - depth, lat)
    swap.start()
    at = jnp.where(depth == 0, OWN_LEFT, PREV_RIGHT)
    def turn(i, carry):
        j, c = lax.div(i, 2), lax.rem(i, 2)
        shift = plan[at + 2 + 5 * j + 2]
        shift = jnp.where(shift == N, 0, shift)
        probes[j, c] = pltpu.roll(pltpu.roll(probe[c], plan[at + 2 + 5 * j], 0), shift, 1)
        return carry

    lax.fori_loop(0, 2 * MAX_JOBS, turn, 0)
    pick_columns(plan, at, tile, windows, depth)
    swap.wait()
    pick_columns(plan, at, other, windows, 1 - depth)
    for copy in sends:
        copy.wait_send()
    for s in range(2):
        remote(ahead, slot(s), row_send.at[0], row_recv.at[s], 1, after).wait_recv()


def pick_columns(plan, at, source, windows, s):
    lane = lanes()
    columns = [
        plan[at + 2 + 5 * j + 1] * N + plan[at + 2 + 5 * j + 2] for j in range(MAX_JOBS)
    ]

    def step(g, carry):
        rows = pl.ds(pl.multiple_of(g * 8, 8), 8)
        for c in range(2):
            picked = [jnp.zeros((8, N), jnp.float32)] * MAX_JOBS
            for q in range(source.shape[2] // N):
                value = source[c, rows, q * N : q * N + N]
                for j, column in enumerate(columns):
                    offset = lane + (q * N - column)
                    picked[j] = jnp.where((offset >= 0) & (offset < N), value, picked[j])
            for j in range(MAX_JOBS):
                windows[s, j, c, rows, :] = picked[j]
        return carry

    lax.fori_loop(0, N // 8, step, 0)


def remote(src, dst, send, recv, depth, lat):
    return pltpu.make_async_remote_copy(
        src_ref=src,
        dst_ref=dst,
        send_sem=send,
        recv_sem=recv,
        device_id=(depth, lat),
        device_id_type=pl.DeviceIdType.MESH,
    )


def greet(sources):
    barrier = pltpu.get_barrier_semaphore()
    for source in sources:
        pl.semaphore_signal(
            barrier, inc=1, device_id=source, device_id_type=pl.DeviceIdType.MESH
        )
    pl.semaphore_wait(barrier, 3)


def return_kernel(
    n_lat, plan, rows, windows, received, tile,
    partner, row_send, row_recv, swap_send, swap_recv,
):
    depth = lax.axis_index("depth")
    lat = lax.axis_index("lat")
    after = lax.rem(lat + 1, n_lat)
    before = lax.rem(lat + n_lat - 1, n_lat)
    greet([(0, before), (1, after), (1 - depth, lat)])
    target = jnp.where(depth == 0, after, before)

    def part(c):
        return received.at[c, :, pl.ds(CHUNK, ROWS), :]

    sends = [
        remote(rows.at[s], part(depth), row_send.at[s], row_recv.at[depth], s, target)
        for s in range(2)
    ]
    for copy in sends:
        copy.start()
    swap = remote(windows.at[1 - depth], partner, swap_send, swap_recv, 1 - depth, lat)
    swap.start()
    sum_windows(plan, depth, lambda j, c, at: windows[depth, j, c, at, :], tile, True)
    swap.wait()
    sum_windows(plan, 1 - depth, lambda j, c, at: partner[j, c, at, :], tile, False)
    for copy in sends:
        copy.wait_send()
    for c in range(2):
        remote(rows.at[0], part(c), row_send.at[0], row_recv.at[c], 0, target).wait_recv()


def sum_windows(plan, core, read, tile, first):
    at = jnp.where(core == 0, OWN_LEFT, PREV_RIGHT)
    row = lax.broadcasted_iota(jnp.int32, (8, N), 0)
    lane = lanes()
    jobs = []
    for j in range(MAX_JOBS):
        r = plan[at + 2 + 5 * j]
        low = jnp.where(core == 0, r, 0)
        high = jnp.where(plan[at] > j, jnp.where(core == 0, N, r), 0)
        jobs.append((low, high, plan[at + 2 + 5 * j + 1] * N + plan[at + 2 + 5 * j + 2]))

    def step(g, carry):
        dst = pl.ds(pl.multiple_of(g * 8, 8), 8)
        here = row + g * 8
        for c in range(2):
            values = [
                jnp.where((here >= low) & (here < high), read(j, c, dst), 0.0)
                for j, (low, high, _) in enumerate(jobs)
            ]
            for q in range(tile.shape[2] // N):
                total = None if first else tile[c, dst, q * N : q * N + N]
                for value, (_, _, column) in zip(values, jobs):
                    offset = lane + (q * N - column)
                    inside = (offset >= 0) & (offset < N)
                    value = jnp.where(inside, value, 0.0)
                    total = value if total is None else total + value
                tile[c, dst, q * N : q * N + N] = total
        return carry

    lax.fori_loop(0, N // 8, step, 0)


P_PLUS, P_MINUS, F_EVEN, F_ODD = 0, 1, 2, 3
TURNED = 4


def halves(x):
    hi = x.astype(jnp.bfloat16)
    lo = (x - hi.astype(jnp.float32)).astype(jnp.bfloat16)
    return hi, lo


def dot(a, b):
    return jnp.dot(a, b, preferred_element_type=jnp.float32)


def times_right(x, table, at):
    hi, lo = halves(x)
    return dot(
        jnp.concatenate([hi, lo, hi], axis=1),
        jnp.concatenate([table[at, 0], table[at, 0], table[at, 1]], axis=0),
    )


def times_left(table, at, x):
    hi, lo = halves(x)
    return dot(
        jnp.concatenate([table[at, 0], table[at, 0], table[at, 1]], axis=1),
        jnp.concatenate([hi, lo, hi], axis=0),
    )


def fold_columns(re, im):
    plus = jnp.concatenate([re[:, :HALF] + re[:, HALF:], im[:, :HALF] + im[:, HALF:]], axis=1)
    minus = jnp.concatenate([re[:, :HALF] - re[:, HALF:], im[:, :HALF] - im[:, HALF:]], axis=1)
    return plus, minus


def pair_columns(re, im):
    return (
        jnp.concatenate([re[:, :HALF], im[:, :HALF]], axis=1),
        jnp.concatenate([re[:, HALF:], im[:, HALF:]], axis=1),
    )


def fold_rows(re, im):
    plus = jnp.concatenate([re[:HALF] + re[HALF:], im[:HALF] + im[HALF:]], axis=0)
    minus = jnp.concatenate([re[:HALF] - re[HALF:], im[:HALF] - im[HALF:]], axis=0)
    return plus, minus


def pair_rows(re, im):
    return (
        jnp.concatenate([re[:HALF], im[:HALF]], axis=0),
        jnp.concatenate([re[HALF:], im[HALF:]], axis=0),
    )


def product(u, v):
    return u[0] * v[0] - u[1] * v[1], u[0] * v[1] + u[1] * v[0]


def conj_product(u, v):
    return u[0] * v[0] + u[1] * v[1], u[0] * v[1] - u[1] * v[0]


def both_right(pairs, table, first, second):
    return [(times_right(p, table, first), times_right(m, table, second)) for p, m in pairs]


def both_left(pairs, table, first, second):
    return [(times_left(table, first, p), times_left(table, second, m)) for p, m in pairs]


def unfold(pairs):
    return [(p + m, p - m) for p, m in pairs]


def propagate(fields, table, adjoint):
    left, right = (TURNED, 0) if adjoint else (0, TURNED)
    pairs = [fold_columns(*f) for f in fields]
    pairs = unfold(both_right(pairs, table, right + P_PLUS, right + P_MINUS))
    pairs = [fold_rows(*pair_columns(*p)) for p in pairs]
    pairs = unfold(both_left(pairs, table, left + P_PLUS, left + P_MINUS))
    return [pair_rows(*p) for p in pairs]


def to_spectrum(fields, table):
    pairs = [fold_columns(*f) for f in fields]
    pairs = both_right(pairs, table, TURNED + F_EVEN, TURNED + F_ODD)
    pairs = [fold_rows(*pair_columns(*p)) for p in pairs]
    pairs = both_left(pairs, table, F_EVEN, F_ODD)
    return [pair_rows(*p) for p in pairs]


def from_spectrum(fields, table):
    pairs = [pair_columns(*f) for f in fields]
    pairs = unfold(both_right(pairs, table, F_EVEN, F_ODD))
    pairs = [pair_rows(*pair_columns(*p)) for p in pairs]
    pairs = unfold(both_left(pairs, table, TURNED + F_EVEN, TURNED + F_ODD))
    return [pair_rows(*p) for p in pairs]


def compute_kernel(
    plan, windows, probes, received, measured, table,
    rows_out, grads,
    amplitude, spread,
):
    depth = lax.axis_index("depth")
    at = jnp.where(depth == 0, OWN_LEFT, PREV_RIGHT)
    jobs = plan[at]
    row = lax.broadcasted_iota(jnp.int32, (N, N), 0)
    lane = lax.broadcasted_iota(jnp.int32, (N, N), 1)
    order = jnp.where(lane < HALF, 2 * lane, 2 * lane - (N - 1))
    shuffle = jnp.where(row == order, 1.0, 0.0).astype(jnp.bfloat16)

    def work(numbers):
        each = range(len(numbers))
        words = [[plan[at + 2 + 5 * j + w] for w in range(5)] for j in numbers]

        for k in each:
            _, _, _, _, slot = words[k]

            @pl.when(depth == 0)
            def _(k=k, slot=slot):
                amplitude[k] = measured[slot]

            @pl.when(depth == 1)
            def _(k=k):
                src = pl.multiple_of(PAD + (plan[PREV_RIGHT + 1] + 8 * numbers[k]) * 8, 8)
                for s in range(2):
                    for c in range(2):
                        amplitude[k, pl.ds(128 * s + 64 * c, 64), :] = received[
                            s, c, pl.ds(src, 64), :
                        ]

        def base_of(k):
            return jnp.where(depth == 0, 0, lax.div(words[k][0], 8))

        def window(k, s):
            r, _, _, start, _ = words[k]
            here = (row >= jnp.where(depth == 0, r, 0)) & (row < jnp.where(depth == 0, N, r))
            src = pl.multiple_of(PAD + (start - base_of(k)) * 8, 8)
            return [
                jnp.where(here, windows[s, numbers[k], c], received[s, c, pl.ds(src, N), :])
                for c in range(2)
            ]

        turned = [[probes[j, c] for c in range(2)] for j in numbers]
        waves = [product(p, window(k, 0)) for k, p in enumerate(turned)]
        waves = propagate(waves, table, False)
        slices = [window(k, 1) for k in each]
        spectra = to_spectrum([product(w, o) for w, o in zip(waves, slices)], table)
        backs = []
        for k in each:
            hi, lo = halves(amplitude[k])
            apart = dot(
                jnp.concatenate([hi, lo], axis=1), jnp.concatenate([shuffle, shuffle], axis=0)
            )
            for h in range(2):
                spread[k, h] = apart[:, HALF * h : HALF * h + HALF]
        for k in each:
            apart = jnp.concatenate(
                [
                    jnp.concatenate(
                        [spread[k, h, pl.ds(p, HALF, stride=2), :] for h in range(2)], axis=1
                    )
                    for p in range(2)
                ],
                axis=0,
            )
            re, im = spectra[k]
            factor = 1.0 - apart * lax.rsqrt(re * re + im * im + 1.0)
            backs.append((re * factor, im * factor))
        backs = from_spectrum(backs, table)
        for k in each:
            grads[1, numbers[k], 0], grads[1, numbers[k], 1] = conj_product(waves[k], backs[k])
        backs = [conj_product(o, b) for o, b in zip(slices, backs)]
        backs = propagate(backs, table, True)
        for k in each:
            grads[0, numbers[k], 0], grads[0, numbers[k], 1] = conj_product(turned[k], backs[k])
        for k in each:
            r, start = words[k][0], words[k][3]
            base = base_of(k)
            count = jnp.where(depth == 0, lax.div(r + 7, 8), 32 - lax.div(r, 8))

            def step(g, carry, k=k, base=base, start=start, count=count):
                for q in range(4):
                    granule = jnp.minimum(4 * g + q, count - 1)
                    src = pl.multiple_of((base + granule) * 8, 8)
                    dst = pl.multiple_of((start + granule) * 8, 8)
                    for s in range(2):
                        for c in range(2):
                            rows_out[s, c, pl.ds(dst, 8), :] = grads[
                                s, numbers[k], c, pl.ds(src, 8), :
                            ]
                return carry

            lax.fori_loop(0, lax.div(count + 3, 4), step, 0)

    @pl.when(jobs >= 2)
    def _():
        work([0, 1])

    @pl.when(lax.rem(jobs, 2) == 1)
    def _():
        work([jobs - 1])


def gather_kernel(plan, rows, tile_in, out, tile, out_sems):
    row = lax.broadcasted_iota(jnp.int32, (CHUNK, N), 0)
    lane = lax.broadcasted_iota(jnp.int32, (CHUNK, N), 1)

    def add(at, j, c, lower):
        r = plan[at + 2 + 5 * j]
        start = plan[at + 2 + 5 * j + 3]
        first = 0 if lower else lax.div(r, CHUNK)
        last = lax.div(r + CHUNK - 1, CHUNK) if lower else N // CHUNK
        skip = 0 if lower else lax.div(r, 8)
        keep = lane >= plan[at + 2 + 5 * j + 2]
        low = pl.multiple_of(plan[at + 2 + 5 * j + 1] * N, N)
        high = pl.multiple_of(plan[at + 2 + 5 * j + 1] * N + N, N)

        def step(g, carry):
            dst = pl.multiple_of(g * CHUNK, CHUNK)
            inside = (row + dst < r) if lower else (row + dst >= r)
            src = pl.multiple_of(CHUNK + (start - skip) * 8 + g * CHUNK, 8)
            value = jnp.where(inside, rows[0 if lower else 1, c, pl.ds(src, CHUNK), :], 0.0)
            tile[c, pl.ds(dst, CHUNK), pl.ds(low, N)] += jnp.where(keep, value, 0.0)
            tile[c, pl.ds(dst, CHUNK), pl.ds(high, N)] += jnp.where(keep, 0.0, value)
            return carry

        lax.fori_loop(first, last, step, 0)

    for c in range(2):
        for at, lower in ((OWN_RIGHT, False), (PREV_LEFT, True)):

            def step(j, carry, at=at, lower=lower, c=c):
                add(at, j, c, lower)
                return carry

            lax.fori_loop(0, plan[at], step, 0)
        pltpu.make_async_copy(tile.at[c], out.at[c], out_sems.at[c]).start()
    for c in range(2):
        pltpu.make_async_copy(tile.at[c], out.at[c], out_sems.at[c]).wait()


SMEM = pl.BlockSpec(memory_space=pltpu.SMEM)
VMEM = pl.BlockSpec(memory_space=pltpu.VMEM)
HBM = pl.BlockSpec(memory_space=pltpu.HBM)


def shape(*dims):
    return jax.ShapeDtypeStruct(dims, jnp.float32)


def shards(n_lat, object_slices, probe, measured, positions, counts):
    columns = object_slices.shape[3]
    tile = object_slices.reshape(object_slices.shape[1:])
    dma = pltpu.SemaphoreType.DMA
    positions = positions.T
    own_plan, prev_positions, prev_counts, tile = pl.pallas_call(
        functools.partial(announce_kernel, n_lat),
        name="announce",
        out_shape=(
            jax.ShapeDtypeStruct((2 * SPAN,), jnp.int32),
            jax.ShapeDtypeStruct(positions.shape, jnp.int32),
            jax.ShapeDtypeStruct(counts.shape, jnp.int32),
            shape(*tile.shape),
        ),
        in_specs=[HBM, HBM, HBM],
        out_specs=(SMEM, VMEM, VMEM, VMEM),
        scratch_shapes=[
            pltpu.SMEM((2, 4), jnp.int32),
            pltpu.SMEM((1,), jnp.int32),
            dma((2,)), dma((2,)), dma((6,)),
        ],
        compiler_params=pltpu.CompilerParams(
            collective_id=2, has_side_effects=True, vmem_limit_bytes=46 << 20
        ),
    )(positions, counts, tile)
    plan, ahead, behind = pl.pallas_call(
        pack_kernel,
        name="pack",
        out_shape=(
            jax.ShapeDtypeStruct((4 * SPAN,), jnp.int32),
            shape(2, ROWS, N),
            shape(2, ROWS, N),
        ),
        in_specs=[SMEM, SMEM, SMEM, VMEM, VMEM],
        out_specs=(SMEM, VMEM, VMEM),
        compiler_params=pltpu.CompilerParams(vmem_limit_bytes=4 << 20),
    )(own_plan, prev_positions, prev_counts, tile, measured)
    received, windows, probes = pl.pallas_call(
        functools.partial(exchange_kernel, n_lat),
        name="exchange",
        out_shape=(
            shape(2, 2, ROWS + 2 * PAD, N),
            shape(2, MAX_JOBS, 2, N, N),
            shape(MAX_JOBS, 2, N, N),
        ),
        in_specs=[SMEM, VMEM, VMEM, VMEM, VMEM],
        out_specs=(VMEM, VMEM, VMEM),
        scratch_shapes=[
            pltpu.VMEM((2, N, columns), jnp.float32),
            dma((2,)), dma((2,)), dma, dma,
        ],
        compiler_params=pltpu.CompilerParams(
            collective_id=0, has_side_effects=True, vmem_limit_bytes=12 << 20
        ),
    )(plan, ahead, behind, tile, probe)

    table = jnp.asarray(tables())
    rows_out, grads = pl.pallas_call(
        compute_kernel,
        name="compute",
        out_shape=(shape(2, 2, ROWS, N), shape(2, MAX_JOBS, 2, N, N)),
        in_specs=[SMEM, VMEM, VMEM, VMEM, VMEM, VMEM],
        out_specs=(VMEM, VMEM),
        scratch_shapes=[
            pltpu.VMEM((2, N, N), jnp.float32),
            pltpu.VMEM((2, 2, N, HALF), jnp.float32),
        ],
        compiler_params=pltpu.CompilerParams(vmem_limit_bytes=30 << 20),
    )(plan, windows, probes, received, measured, table)

    rows_back, tile = pl.pallas_call(
        functools.partial(return_kernel, n_lat),
        name="giveback",
        out_shape=(shape(2, 2, ROWS + 2 * CHUNK, N), shape(2, N, columns)),
        in_specs=[SMEM, VMEM, VMEM],
        out_specs=(VMEM, VMEM),
        scratch_shapes=[
            pltpu.VMEM((MAX_JOBS, 2, N, N), jnp.float32),
            dma((2,)), dma((2,)), dma, dma,
        ],
        compiler_params=pltpu.CompilerParams(
            collective_id=1, has_side_effects=True, vmem_limit_bytes=12 << 20
        ),
    )(plan, rows_out, grads)

    out, _ = pl.pallas_call(
        gather_kernel,
        name="gather",
        out_shape=(shape(2, N, columns), shape(2, N, columns)),
        in_specs=[SMEM, VMEM, VMEM],
        out_specs=(HBM, VMEM),
        scratch_shapes=[dma((2,))],
        input_output_aliases={2: 1},
        compiler_params=pltpu.CompilerParams(vmem_limit_bytes=12 << 20),
    )(plan, rows_back, tile)
    return out.reshape(object_slices.shape)


def solution(mesh):
    return jax.shard_map(
        functools.partial(shards, mesh.shape["lat"]),
        mesh=mesh,
        in_specs=(
            P("depth", None, "lat", None),
            P(),
            P("lat", None, None),
            P("lat", None),
            P("lat"),
        ),
        out_specs=P("depth", None, "lat", None),
        check_vma=False,
    )
```
